32 devices in a mesh: fsdp: 2 (over x), ctx: 4 (over y, core), tp: 4 (over z).
Axes of the slice: x: 2, y: 2, z: 4, core: 2. Of those that a mesh axis runs over, the one named last changes fastest.
Arguments:
- inputs: bfloat16 [8, 1024, 1024], P('fsdp', 'ctx'), may hold values from -6 to 6
- lengths: int32 [8], P('fsdp'), may hold values from 256 to 1024, as said below
- w_query: bfloat16 [1024, 1024], P(('fsdp', 'ctx'), 'tp'), may hold values from -0.1875 to 0.1875
- w_key: bfloat16 [1024, 1024], P(('fsdp', 'ctx'), 'tp'), may hold values from -0.1875 to 0.1875
- w_value: bfloat16 [1024, 1024], P(('fsdp', 'ctx'), 'tp'), may hold values from -0.1875 to 0.1875
- b_query: float32 [1024], P('tp'), may hold values from -3 to 3
- b_value: float32 [1024], P('tp'), may hold values from -3 to 3
- w_out: bfloat16 [1024, 1024], P(('fsdp', 'ctx'), 'tp'), may hold values from -2 to 2
- b_out: float32 [1024], replicated, may hold values from -3 to 3
- gain_attn: float32 [1024], replicated, may hold values from 0.5 to 1.5
- shift_attn: float32 [1024], replicated, may hold values from -3 to 3
- w_up: bfloat16 [1024, 4096], P(('fsdp', 'ctx'), 'tp'), may hold values from -0.1875 to 0.1875
- b_up: float32 [4096], P('tp'), may hold values from -3 to 3
- w_down: bfloat16 [1024, 4096], P(('fsdp', 'ctx'), 'tp'), may hold values from -0.125 to 0.125
- b_down: float32 [1024], replicated, may hold values from -3 to 3
- gain_ffn: float32 [1024], replicated, may hold values from 0.5 to 1.5
- shift_ffn: float32 [1024], replicated, may hold values from -3 to 3
- cotangent: bfloat16 [8, 1024, 1024], P('fsdp', 'ctx'), may hold values from -6 to 6
Outputs:
- result: bfloat16 [8, 1024, 1024], P('fsdp', 'ctx')
- grad_inputs: float32 [8, 1024, 1024], P('fsdp', 'ctx')
- grad_w_query: float32 [1024, 1024], P(('fsdp', 'ctx'), 'tp')
- grad_w_key: float32 [1024, 1024], P(('fsdp', 'ctx'), 'tp')
- grad_w_value: float32 [1024, 1024], P(('fsdp', 'ctx'), 'tp')
- grad_b_query: float32 [1024], P('tp')
- grad_b_value: float32 [1024], P('tp')
- grad_w_out: float32 [1024, 1024], P(('fsdp', 'ctx'), 'tp')
- grad_b_out: float32 [1024], replicated
- grad_gain_attn: float32 [1024], replicated
- grad_shift_attn: float32 [1024], replicated
- grad_w_up: float32 [1024, 4096], P(('fsdp', 'ctx'), 'tp')
- grad_b_up: float32 [4096], P('tp')
- grad_w_down: float32 [1024, 4096], P(('fsdp', 'ctx'), 'tp')
- grad_b_down: float32 [1024], replicated
- grad_gain_ffn: float32 [1024], replicated
- grad_shift_ffn: float32 [1024], replicated
The draws below stay inside these ranges and needn't reach their ends.
Inputs may be any that keep to these rules, and one draw needn't show every extreme that they name: `lengths`: in each aligned group of 4 sequences one, drawn from the seed, has length 1024.
All inputs are finite; a program needn't handle non-finite values.
Results may differ from the reference program's by a relative error of at most 0.017.
Values may be sent and summed in bfloat16 or wider, within the bound.
A program may use at most 128 MiB of HBM per device.

```python
import math
import jax
import jax.numpy as jnp
from jax import lax

D = 1024
HEADS = 16
FF = 4096
DH = 64
SEQ = 1024
SEQ_DEV = 4
NSEQ = 8


def draw_lengths(key, part):
    base_key = jax.random.fold_in(key, 11)
    pick_key = jax.random.fold_in(key, 23)
    groups = NSEQ // SEQ_DEV
    drawn = jax.random.randint(base_key, (NSEQ,), SEQ // 4, SEQ + 1)
    chosen = jax.random.randint(pick_key, (groups,), 0, SEQ_DEV)
    within = jnp.arange(NSEQ, dtype=jnp.int32) % SEQ_DEV
    longest = within == jnp.repeat(chosen, SEQ_DEV)
    return jnp.where(longest, SEQ, drawn).astype(jnp.int32)


def block_levels(rng, dims, pieces, smallest, high):
    def one(axis_at, shards_of):
        heights = jax.random.uniform(jax.random.fold_in(jax.random.fold_in(rng, 6), axis_at), (shards_of,), jnp.float32, smallest / len(pieces), high / len(pieces))
        return jnp.repeat(jnp.exp(heights), dims[axis_at] // shards_of).reshape((-1,) + (1,) * (len(dims) - axis_at - 1))

    factor_of = one(*pieces[0])
    for cut in pieces[1:]:
        factor_of = factor_of * one(*cut)
    return factor_of


def scatter_about(stream_key, shape, spread, most, split=(), kind=jnp.bfloat16):
    values = spread * jax.random.normal(stream_key, shape, jnp.float32)
    if split:
        values = values * block_levels(stream_key, shape, split, -0.22, 0.18)
    return jnp.clip(values, -most, most).astype(kind)


def setup_inputs(seed: int = 0) -> dict:
    keys = jax.random.split(jax.random.key(seed), 19)
    return {
        "inputs": scatter_about(keys[0], (NSEQ, SEQ, D), 1.0, 6.0, ((0, 2), (1, 4))),
        "lengths": draw_lengths(jax.random.fold_in(keys[18], 71), 0),
        "w_query": scatter_about(keys[2], (D, D), D ** -0.5, 0.1875, ((0, 8), (1, 4))),
        "w_key": scatter_about(keys[3], (D, D), D ** -0.5, 0.1875, ((0, 8), (1, 4))),
        "w_value": scatter_about(keys[4], (D, D), D ** -0.5, 0.1875, ((0, 8), (1, 4))),
        "b_query": scatter_about(keys[5], (D,), 0.5, 3.0, ((0, 4),), jnp.float32),
        "b_value": scatter_about(keys[6], (D,), 0.5, 3.0, ((0, 4),), jnp.float32),
        "w_out": scatter_about(keys[7], (D, D), (max(D // 128, 8)) ** -0.5, 2.0, ((0, 8), (1, 4))),
        "b_out": scatter_about(keys[8], (D,), 0.5, 3.0, (), jnp.float32),
        "gain_attn": jnp.clip(1.0 + 0.1 * jax.random.normal(keys[9], (D,), jnp.float32), 0.5, 1.5),
        "shift_attn": scatter_about(keys[10], (D,), 0.5, 3.0, (), jnp.float32),
        "w_up": scatter_about(keys[11], (D, FF), D ** -0.5, 0.1875, ((0, 8), (1, 4))),
        "b_up": scatter_about(keys[12], (FF,), 0.5, 3.0, ((0, 4),), jnp.float32),
        "w_down": scatter_about(keys[13], (D, FF), (FF // 2) ** -0.5, 0.125, ((0, 8), (1, 4))),
        "b_down": scatter_about(keys[14], (D,), 0.5, 3.0, (), jnp.float32),
        "gain_ffn": jnp.clip(1.0 + 0.1 * jax.random.normal(keys[15], (D,), jnp.float32), 0.5, 1.5),
        "shift_ffn": scatter_about(keys[16], (D,), 0.5, 3.0, (), jnp.float32),
        "cotangent": scatter_about(keys[17], (NSEQ, SEQ, D), 1.0, 6.0, ((0, 2), (1, 4))),
    }


@jax.custom_vjp
def low(v):
    return lax.optimization_barrier(v.astype(jnp.bfloat16)).astype(jnp.float32)

@jax.custom_vjp
def low_back(v):
    return v

def low_keep(v):
    return (low(v), None)

def low_pass(kept, grad):
    return (grad,)

def back_keep(v):
    return (v, None)

def back_low(kept, grad):
    return (low(grad),)
low.defvjp(low_keep, low_pass)
low_back.defvjp(back_keep, back_low)

def layer_norm(hidden, gain, shift):
    row_mean = lax.optimization_barrier(jnp.mean(hidden, -1, keepdims=True))
    centered = hidden - row_mean
    row_var = lax.optimization_barrier(jnp.mean(centered * centered, -1, keepdims=True))
    return centered * lax.rsqrt(row_var + 1e-05) * gain + shift

def matmul_hi(left, right):
    return jnp.dot(left, right, precision=lax.Precision.HIGHEST)

def reference(inputs, lengths, w_query, w_key, w_value, b_query, b_value, w_out, b_out, gain_attn, shift_attn, w_up, b_up, w_down, b_down, gain_ffn, shift_ffn, cotangent):
    valid = jnp.arange(SEQ, dtype=jnp.int32)[None, :] < lengths[:, None]
    scale = 1.0 / math.sqrt(DH)

    def attend(packed):
        qry_rows, key_rows, val_rows, key_ok = packed
        scores = jnp.einsum('qhd,khd->hqk', qry_rows, key_rows, precision=lax.Precision.HIGHEST) * scale
        scores = low_back(scores)
        scores = jnp.where(key_ok[None, None, :], scores, -1e+30)
        attn_prob = jax.nn.softmax(scores, axis=-1)
        return jnp.einsum('hqk,khd->qhd', low(attn_prob), val_rows, precision=lax.Precision.HIGHEST)

    def forward(x_in, wq_f, wk_f, wv_f, bq_f, bv_f, wo_f, bo_f, ga_f, sa_f, wu_f, bu_f, wd_f, bd_f, gf_f, sf_f):
        queries = low(low_back(matmul_hi(x_in, wq_f) + bq_f)).reshape(NSEQ, SEQ, HEADS, DH)
        key_all = low(low_back(matmul_hi(x_in, wk_f))).reshape(NSEQ, SEQ, HEADS, DH)
        values = low(low_back(matmul_hi(x_in, wv_f) + bv_f)).reshape(NSEQ, SEQ, HEADS, DH)
        attended = lax.map(jax.checkpoint(attend), (queries, key_all, values, valid))
        attended = low(low_back(attended.reshape(NSEQ, SEQ, D)))
        resid1 = x_in + low_back(matmul_hi(attended, wo_f.T)) + bo_f
        normed = layer_norm(resid1, ga_f, sa_f)
        pre_act = low_back(matmul_hi(low(normed), wu_f) + bu_f)
        act_low = low(jax.nn.gelu(pre_act, approximate=False))
        resid2 = normed + low_back(matmul_hi(act_low, wd_f.T)) + bd_f
        return layer_norm(resid2, gf_f, sf_f)
    params = [inputs, w_query, w_key, w_value, b_query, b_value, w_out, b_out, gain_attn, shift_attn, w_up, b_up, w_down, b_down, gain_ffn, shift_ffn]
    params = [p.astype(jnp.float32) for p in params]
    output, pull_back = jax.vjp(forward, *params)
    grad_top = cotangent.astype(jnp.float32) * valid[:, :, None].astype(jnp.float32)
    grads = pull_back(grad_top)
    return (output.astype(jnp.bfloat16), grads[0], grads[1], grads[2], grads[3], grads[4], grads[5], grads[6], grads[7], grads[8], grads[9], grads[10], grads[11], grads[12], grads[13], grads[14], grads[15])
```

```python
import math

import jax
import jax.numpy as jnp
from jax import lax
from jax.sharding import PartitionSpec as P

DH = 64


def layer_norm(hidden, gain, shift):
    row_mean = jnp.mean(hidden, -1, keepdims=True)
    centered = hidden - row_mean
    row_var = jnp.mean(centered * centered, -1, keepdims=True)
    return centered * lax.rsqrt(row_var + 1e-05) * gain + shift


def gelu_exact(pre_act):
    return jax.nn.gelu(pre_act, approximate=False)


def dot(left, right):
    return jnp.dot(left, right, preferred_element_type=jnp.float32)


def dot_last(left, right):
    return lax.dot_general(
        left, right, (((1,), (1,)), ((), ())), preferred_element_type=jnp.float32
    )


def dot_first(left, right):
    return lax.dot_general(
        left, right, (((0,), (0,)), ((), ())), preferred_element_type=jnp.float32
    )


def low(v):
    return v.astype(jnp.bfloat16)


def shards(
    inputs,
    lengths,
    w_query,
    w_key,
    w_value,
    b_query,
    b_value,
    w_out,
    b_out,
    gain_attn,
    shift_attn,
    w_up,
    b_up,
    w_down,
    b_down,
    gain_ffn,
    shift_ffn,
    cotangent,
):
    n_fsdp = lax.axis_size("fsdp")
    n_ctx = lax.axis_size("ctx")
    n_tp = lax.axis_size("tp")
    assert n_ctx == n_tp and inputs.shape[0] % n_tp == 0
    seq_dev, seq_loc, width = inputs.shape
    per_tp = seq_dev // n_tp
    seq_full = seq_loc * n_ctx
    scale = 1.0 / math.sqrt(DH)
    c_idx = lax.axis_index("ctx")
    t_idx = lax.axis_index("tp")
    swap = [(c * n_tp + t, t * n_tp + c) for c in range(n_ctx) for t in range(n_tp)]

    def gather_cols(block):
        moved = lax.ppermute(block, ("ctx", "tp"), swap)
        return lax.all_gather(moved, ("fsdp", "tp"), axis=0, tiled=True)

    def scatter_cols(grad):
        mine = lax.psum_scatter(low(grad), ("fsdp", "tp"), scatter_dimension=0, tiled=True)
        return lax.ppermute(mine, ("ctx", "tp"), swap).astype(jnp.float32)

    hid = w_query.shape[1]
    hid_ff = w_up.shape[1]
    attn_w = gather_cols(jnp.concatenate([w_query, w_key, w_value, w_out], axis=1))
    wqkv = attn_w[:, : 3 * hid]
    wo = attn_w[:, 3 * hid :]
    ffn_w = gather_cols(jnp.concatenate([w_up, w_down], axis=1))
    wu = ffn_w[:, :hid_ff]
    wd = ffn_w[:, hid_ff:]
    biases = lax.ppermute(jnp.concatenate([b_query, b_value, b_up]), ("ctx", "tp"), swap)
    bq = biases[:hid]
    bv = biases[hid : 2 * hid]
    bu = biases[2 * hid :]

    def to_tok(rows):
        return lax.all_gather(
            rows.reshape(per_tp, seq_loc, -1), "ctx", axis=1, tiled=True
        ).reshape(per_tp * seq_full, -1)

    def to_share(rows):
        return (
            lax.psum_scatter(
                low(rows).reshape(per_tp, seq_full, -1), "ctx", scatter_dimension=1, tiled=True
            )
            .reshape(per_tp * seq_loc, -1)
            .astype(jnp.float32)
        )

    first_seq = t_idx * per_tp
    in_share = lax.dynamic_slice_in_dim(inputs, first_seq, per_tp, 0).reshape(-1, width)
    ct_share = lax.dynamic_slice_in_dim(cotangent, first_seq, per_tp, 0).reshape(-1, width)
    len_share = lax.dynamic_slice_in_dim(lengths, first_seq, per_tp, 0)
    x_tok = to_tok(in_share)
    positions = c_idx * seq_loc + jnp.arange(seq_loc, dtype=jnp.int32)
    row_valid = (positions[None, :] < len_share[:, None]).reshape(-1, 1)
    key_valid = jnp.arange(seq_full, dtype=jnp.int32)[None, :] < len_share[:, None]

    qkv = dot(x_tok, wqkv)
    queries = low(qkv[:, :hid] + bq)
    keys = low(qkv[:, hid : 2 * hid])
    vals = low(qkv[:, 2 * hid :] + bv)
    heads = hid // DH

    def split(m):
        return m.reshape(per_tp, seq_full, heads, DH).transpose(0, 2, 1, 3)

    def join(m):
        return m.transpose(0, 2, 1, 3).reshape(per_tp * seq_full, heads * DH)

    qh, kh, vh = split(queries), split(keys), split(vals)
    scores = jnp.einsum("bhqd,bhkd->bhqk", qh, kh, preferred_element_type=jnp.float32) * scale
    scores = jnp.where(key_valid[:, None, None, :], scores, -1e30)
    row_top = jnp.max(scores, -1, keepdims=True)
    expo = jnp.exp(scores - row_top)
    row_total = jnp.sum(expo, -1, keepdims=True)
    prob = expo / row_total
    prob_low = low(prob)
    attended = join(low(jnp.einsum("bhqk,bhkd->bhqd", prob_low, vh, preferred_element_type=jnp.float32)))

    resid1 = in_share.astype(jnp.float32) + to_share(dot_last(attended, wo)) + b_out
    normed = layer_norm(resid1, gain_attn, shift_attn)
    normed_low = to_tok(low(normed))
    pre_act = dot(normed_low, wu) + bu
    act_low = low(gelu_exact(pre_act))
    resid2 = normed + to_share(dot_last(act_low, wd)) + b_down
    out_share, final_pull = jax.vjp(layer_norm, resid2, gain_ffn, shift_ffn)
    result = lax.all_gather(
        low(out_share).reshape(per_tp, seq_loc, width), "tp", axis=0, tiled=True
    )
    top_share = ct_share.astype(jnp.float32) * row_valid.astype(jnp.float32)
    d_resid2, d_gain_ffn, d_shift_ffn = final_pull(top_share)
    d_resid2_low = to_tok(low(d_resid2))
    grad_wd = dot_first(d_resid2_low, act_low)
    d_act = dot(d_resid2_low, wd)
    _, gelu_pull = jax.vjp(gelu_exact, pre_act)
    d_pre_low = low(gelu_pull(d_act)[0])
    grad_wu = dot_first(normed_low, d_pre_low)
    g_ffn = scatter_cols(jnp.concatenate([grad_wu, grad_wd], axis=1))
    d_normed = d_resid2 + to_share(dot_last(d_pre_low, wu))
    _, first_pull = jax.vjp(layer_norm, resid1, gain_attn, shift_attn)
    d_resid1, d_gain_attn, d_shift_attn = first_pull(d_normed)
    d_resid1_low = to_tok(low(d_resid1))
    grad_wo = dot_first(d_resid1_low, attended)
    d_att = split(low(dot(d_resid1_low, wo)))
    d_vals = jnp.einsum("bhqk,bhqd->bhkd", prob_low, d_att, preferred_element_type=jnp.float32)
    d_prob = jnp.einsum("bhqd,bhkd->bhqk", d_att, vh, preferred_element_type=jnp.float32)
    row_delta = jnp.sum(prob * d_prob, -1, keepdims=True)
    d_score = low(prob * (d_prob - row_delta))
    d_q = jnp.einsum("bhqk,bhkd->bhqd", d_score, kh, preferred_element_type=jnp.float32) * scale
    d_k = jnp.einsum("bhqk,bhqd->bhkd", d_score, qh, preferred_element_type=jnp.float32) * scale
    d_qkv = jnp.concatenate([join(low(d_q)), join(low(d_k)), join(low(d_vals))], axis=1)
    grad_qkv = dot_first(x_tok, d_qkv)
    g_attn = scatter_cols(jnp.concatenate([grad_qkv, grad_wo], axis=1))
    gi_share = d_resid1 + to_share(dot_last(d_qkv, wqkv))
    grad_inputs = lax.all_gather(
        low(gi_share).reshape(per_tp, seq_loc, width), "tp", axis=0, tiled=True
    ).astype(jnp.float32)

    col_sums = jnp.concatenate(
        [
            jnp.sum(d_qkv[:, :hid].astype(jnp.float32), 0),
            jnp.sum(d_qkv[:, 2 * hid :].astype(jnp.float32), 0),
            jnp.sum(d_pre_low.astype(jnp.float32), 0),
        ]
    )
    blocks = lax.dynamic_update_slice(
        jnp.zeros((n_ctx, col_sums.shape[0]), jnp.float32), col_sums[None], (c_idx, 0)
    )
    whole = jnp.stack(
        [
            jnp.sum(d_resid1, 0),
            d_gain_attn,
            d_shift_attn,
            jnp.sum(d_resid2, 0),
            d_gain_ffn,
            d_shift_ffn,
        ]
    )
    flat = lax.psum(jnp.concatenate([blocks.reshape(-1), whole.reshape(-1)]), ("fsdp", "ctx", "tp"))
    n_block = col_sums.shape[0]
    mine = lax.dynamic_slice_in_dim(flat, t_idx * n_block, n_block, 0)
    whole = flat[n_ctx * n_block :].reshape(6, width)
    return (
        result,
        grad_inputs,
        g_attn[:, :hid],
        g_attn[:, hid : 2 * hid],
        g_attn[:, 2 * hid : 3 * hid],
        mine[:hid],
        mine[hid : 2 * hid],
        g_attn[:, 3 * hid :],
        whole[0],
        whole[1],
        whole[2],
        g_ffn[:, :hid_ff],
        mine[2 * hid :],
        g_ffn[:, hid_ff:],
        whole[3],
        whole[4],
        whole[5],
    )


def solution(mesh):
    weight = P(("fsdp", "ctx"), "tp")
    acts = P("fsdp", "ctx", None)
    return jax.shard_map(
        shards,
        mesh=mesh,
        in_specs=(
            acts,
            P("fsdp"),
            weight,
            weight,
            weight,
            P("tp"),
            P("tp"),
            weight,
            P(),
            P(),
            P(),
            weight,
            P("tp"),
            weight,
            P(),
            P(),
            P(),
            acts,
        ),
        out_specs=(
            acts,
            acts,
            weight,
            weight,
            weight,
            P("tp"),
            P("tp"),
            weight,
            P(),
            P(),
            P(),
            weight,
            P("tp"),
            weight,
            P(),
            P(),
            P(),
        ),
        check_vma=False,
    )
```

```python
import functools
import math

import jax
import jax.numpy as jnp
from jax import lax
from jax.experimental import pallas as pl
from jax.experimental.pallas import tpu as pltpu
from jax.sharding import PartitionSpec as P

DH = 64
MESH = pl.DeviceIdType.MESH
F32 = jnp.float32
BF16 = jnp.bfloat16
TILE = 256
ROWS = 16
CHUNKS = 2


def dot(left, right):
    return jnp.dot(left, right, preferred_element_type=F32)


def dot_last(left, right):
    return lax.dot_general(left, right, (((1,), (1,)), ((), ())), preferred_element_type=F32)


def dot_first(left, right):
    return lax.dot_general(left, right, (((0,), (0,)), ((), ())), preferred_element_type=F32)


def aligned(index, size):
    return pl.ds(pl.multiple_of(index * size, size), size)


def layer(
    dims,
    lens,
    x_h,
    ct_h,
    wq_h,
    wk_h,
    wv_h,
    wo_h,
    wu_h,
    wd_h,
    bias_h,
    vec,
    res_h,
    gi_h,
    gffn_o,
    gatt_o,
    small_o,
    wqkv,
    wo,
    wu,
    wd,
    z0,
    z1,
    z2,
    z3,
    x_tok,
    nl,
    dl2,
    dl1,
    qs,
    kk,
    vv,
    kt,
    vt,
    att,
    datt,
    ot,
    lse,
    act,
    dg,
    dpl,
    dqkv,
    dk_acc,
    dv_acc,
    ps,
    pr,
    ysend,
    yrecv,
    acc_y,
    acc_o,
    xh1,
    rstd1,
    dres,
    res_s,
    gi_s,
    ct_s,
    bias,
    gwd,
    gwu,
    gqkv,
    gwo,
    xg_d,
    xg_u,
    xg_q,
    xg_o,
    zg_d,
    zg_u,
    zg_q,
    zg_o,
    sums,
    sm,
    smz,
    smx,
    smc,
    loc_sem,
    bias_s,
    bias_r,
    wz_s,
    wz_r,
    wy_s,
    wy_r,
    wx_s,
    wx_r,
    ag_s,
    ag_r,
    rs_s,
    rs_r,
    ry_s,
    ry_r,
    out_s,
    out_r,
    gx_s,
    gx_r,
    gz_s,
    gz_r,
    sm_s,
    sm_r,
):
    nf, nc, nt = dims
    f = lax.axis_index("fsdp")
    c = lax.axis_index("ctx")
    t = lax.axis_index("tp")
    yi, ki = c // 2, lax.rem(c, 2)
    c_sib = yi * 2 + (1 - ki)
    c_y = (1 - yi) * 2 + ki
    c_ysib = (1 - yi) * 2 + (1 - ki)
    seq, width = ct_s.shape
    tok = x_tok.shape[0]
    rows_w = z0.shape[1]
    hid = wo.shape[1]
    ff = wu.shape[1]
    heads = hid // DH
    scale = 1.0 / math.sqrt(DH)
    chunk = seq // CHUNKS
    sib = (f, c_sib, t)
    ypeer = (f, c_y, t)
    length = lens[t]

    def remote(src, dst, ssem, rsem, dev):
        return pltpu.make_async_remote_copy(
            src_ref=src, dst_ref=dst, send_sem=ssem, recv_sem=rsem, device_id=dev, device_id_type=MESH
        )

    bar = pltpu.get_barrier_semaphore()
    for dc in range(nc):
        for dt in range(nt):
            if dc or dt:
                pl.semaphore_signal(
                    bar,
                    inc=1,
                    device_id=(f, lax.rem(c + dc, nc), lax.rem(t + dt, nt)),
                    device_id_type=MESH,
                )
    for df in range(1, nf):
        pl.semaphore_signal(bar, inc=1, device_id=(lax.rem(f + df, nf), c, t), device_id_type=MESH)
    pl.semaphore_wait(bar, nc * nt - 1 + nf - 1)

    groups = (
        ((wq_h, wk_h, wv_h), z0, wqkv),
        ((wo_h,), z1, wo),
        ((wu_h,), z2, wu),
        ((wd_h,), z3, wd),
    )

    def own_rows(cc):
        return aligned(f * nc + cc, rows_w)

    def w_start(g):
        srcs, stage, _ = groups[g]
        for k, src in enumerate(srcs):
            cols = pl.ds(k * src.shape[1], src.shape[1])
            pltpu.make_async_copy(src, stage.at[t, :, cols], wz_r.at[g, 0]).start()
            for j in range(1, nt):
                remote(
                    src,
                    stage.at[t, :, cols],
                    wz_s.at[g, j],
                    wz_r.at[g, j],
                    (f, c, lax.rem(t + j, nt)),
                ).start()

    def w_cross(g, j):
        _, stage, final = groups[g]
        ts = lax.rem(t + nt - j, nt)
        if j == 0:
            pltpu.make_async_copy(stage.at[ts], stage.at[ts], wz_r.at[g, 0]).wait()
        else:
            remote(stage.at[ts], stage.at[ts], wz_s.at[g, j], wz_r.at[g, j], (f, c, ts)).wait_recv()

        @pl.when(ts == c)
        def _():
            pltpu.make_async_copy(stage.at[ts], final.at[own_rows(c)], wy_r.at[g, c]).start()

        @pl.when(ts != c)
        def _():
            remote(
                stage.at[ts], final.at[own_rows(c)], wy_s.at[g, j], wy_r.at[g, c], (f, ts, t)
            ).start()

    def w_spread(g, i):
        _, _, final = groups[g]
        cc = lax.rem(c + i, nc)
        if i == 0:
            pltpu.make_async_copy(
                final.at[own_rows(cc)], final.at[own_rows(cc)], wy_r.at[g, cc]
            ).wait()
        else:
            remote(
                final.at[own_rows(cc)], final.at[own_rows(cc)], wy_s.at[g, 0], wy_r.at[g, cc], (f, cc, t)
            ).wait_recv()
        for df in range(1, nf):
            remote(
                final.at[own_rows(cc)],
                final.at[own_rows(cc)],
                wx_s.at[g, df],
                wx_r.at[g, df],
                (lax.rem(f + df, nf), c, t),
            ).start()

    def w_wait(g):
        _, _, final = groups[g]
        for df in range(1, nf):
            fs = lax.rem(f + nf - df, nf)
            part = final.at[aligned(fs, nc * rows_w)]
            remote(part, part, wx_s.at[g, df], wx_r.at[g, df], (fs, c, t)).wait_recv()

    def w_finish(g):
        _, stage, final = groups[g]
        for j in range(1, nt):
            remote(
                stage.at[0], stage.at[0], wz_s.at[g, j], wz_r.at[g, j], (f, c, lax.rem(t + j, nt))
            ).wait_send()
        for j in range(nt):
            ts = lax.rem(t + nt - j, nt)

            @pl.when(ts != c)
            def _():
                remote(
                    stage.at[ts], final.at[own_rows(c)], wy_s.at[g, j], wy_r.at[g, c], (f, ts, t)
                ).wait_send()

        for df in range(1, nf):
            part = final.at[aligned(f, nc * rows_w)]
            remote(
                part, part, wx_s.at[g, df], wx_r.at[g, df], (lax.rem(f + df, nf), c, t)
            ).wait_send()

    def part_of(buf, cc, k):
        return buf.at[pl.ds(pl.multiple_of(cc * seq + k * chunk, chunk), chunk)]

    def ag_copy(buf, a, k, cc, way, dev):
        part = part_of(buf, cc, k)
        return remote(part, part, ag_s.at[a, way, k], ag_r.at[a, way, k], dev)

    def ag_send(buf, a, k):
        ag_copy(buf, a, k, c, 1, ypeer).start()
        ag_copy(buf, a, k, c, 0, sib).start()

    def ag_pass(buf, a, k):
        ag_copy(buf, a, k, c_y, 1, ypeer).wait_recv()
        ag_copy(buf, a, k, c_y, 2, sib).start()

    def ag_wait(buf, a, k, way):
        ag_copy(buf, a, k, c_sib if way == 0 else c_ysib, way, sib).wait_recv()

    def ag_finish(buf, a):
        for k in range(CHUNKS):
            ag_copy(buf, a, k, c, 0, sib).wait_send()
            ag_copy(buf, a, k, c, 1, ypeer).wait_send()
            ag_copy(buf, a, k, c_y, 2, sib).wait_send()

    tiles = width // TILE

    def rs_copy(o, slot):
        return remote(ps.at[slot], pr.at[slot], rs_s.at[o, slot], rs_r.at[o, slot], sib)

    def ry_copy(o, k):
        rows = pl.ds(k * chunk, chunk)
        return remote(ysend.at[rows], yrecv.at[rows], ry_s.at[o, k], ry_r.at[o, k], ypeer)

    def rs_sib(o, slot, produce):
        if o:
            rs_copy(o - 1, slot).wait_send()

        def tile(n, _):
            ps[slot, :, aligned(n, TILE)] = produce(n).astype(BF16)
            return 0

        lax.fori_loop(0, tiles, tile, 0)
        rs_copy(o, slot).start()

    def rs_y(o, produce):
        def tile(n, _):
            acc_y[:, aligned(n, TILE)] = produce(n)
            return 0

        lax.fori_loop(0, tiles, tile, 0)
        rs_copy(o, 0).wait_recv()
        for k in range(CHUNKS):
            if o:
                ry_copy(o - 1, k).wait_send()

            def add(i, _, k=k):
                rows = pl.ds(pl.multiple_of(k * chunk + i * ROWS, ROWS), ROWS)
                ysend[rows] = (acc_y[rows] + pr[0, rows].astype(F32)).astype(BF16)
                return 0

            lax.fori_loop(0, chunk // ROWS, add, 0)
            ry_copy(o, k).start()

    def rs_own(o, produce):
        def tile(n, _):
            acc_o[:, aligned(n, TILE)] = produce(n)
            return 0

        lax.fori_loop(0, tiles, tile, 0)

    def rs_row(rows):
        return acc_o[rows] + pr[1, rows].astype(F32) + yrecv[rows].astype(F32)

    def rs_rows(o, k, body):
        ry_copy(o, k).wait_recv()

        def step(i, _):
            body(pl.ds(pl.multiple_of(k * chunk + i * ROWS, ROWS), ROWS), i)
            return 0

        lax.fori_loop(0, chunk // ROWS, step, 0)

    def add_sum(k, value):
        half = value[0:8]
        for r in range(8, ROWS, 8):
            half = half + value[r : r + 8]
        sums[k] = sums[k] + half

    def mean(value):
        return jnp.sum(value, -1, keepdims=True) * (1.0 / width)

    w_start(0)
    pltpu.make_async_copy(x_h.at[t], x_tok.at[aligned(c, seq)], loc_sem.at[0]).start()
    pltpu.make_async_copy(ct_h.at[t], ct_s, loc_sem.at[1]).start()

    @pl.when(t == c)
    def _():
        pltpu.make_async_copy(bias_h, bias, loc_sem.at[2]).start()
        for j in range(1, nt):
            remote(bias_h, bias, bias_s.at[j], bias_r.at[0], (f, c, lax.rem(t + j, nt))).start()

    pltpu.make_async_copy(x_h.at[t], x_tok.at[aligned(c, seq)], loc_sem.at[0]).wait()
    for k in range(CHUNKS):
        ag_send(x_tok, 0, k)
    w_cross(0, 0)
    sums[...] = jnp.zeros_like(sums)
    for k in range(CHUNKS):
        ag_pass(x_tok, 0, k)
    for j in range(1, nt):
        w_cross(0, j)
    for g in range(1, 4):
        w_start(g)

    @pl.when(t == c)
    def _():
        pltpu.make_async_copy(bias_h, bias, loc_sem.at[2]).wait()

    @pl.when(t != c)
    def _():
        remote(bias_h, bias, bias_s.at[0], bias_r.at[0], (f, c, c)).wait_recv()

    for i in range(nc):
        w_spread(0, i)
    for k in range(CHUNKS):
        ag_wait(x_tok, 0, k, 0)
        ag_wait(x_tok, 0, k, 2)
    for g in range(1, 4):
        w_cross(g, 0)
    w_wait(0)

    def project(b, _):
        rows = aligned(b, seq)
        xb = x_tok[rows]
        qv = dot(xb, wqkv[:, 0:hid]) + bias[0:1, 0:hid]
        qs[rows] = (qv * scale).astype(BF16)
        kb = dot(xb, wqkv[:, hid : 2 * hid])
        kk[rows] = kb.astype(BF16)
        kt[:, rows] = kb.T.astype(BF16)
        vb = dot(xb, wqkv[:, 2 * hid : 3 * hid]) + bias[0:1, hid : 2 * hid]
        vv[rows] = vb.astype(BF16)
        vt[:, rows] = vb.T.astype(BF16)
        return 0

    lax.fori_loop(0, nc, project, 0)

    lane = lax.broadcasted_iota(jnp.int32, (seq, hid), 1)

    def head_part(value, h):
        inside = (lane >= h * DH) & (lane < (h + 1) * DH)
        return jnp.where(inside, value, jnp.zeros_like(value))

    def masked_scores(qm):
        s = dot_last(kk[...], qm)
        key = lax.broadcasted_iota(jnp.int32, s.shape, 0)
        return jnp.where(key < length, s, -1e30)

    def attend(b):
        rows = aligned(b, seq)
        qb = qs[rows]

        def head(h, _):
            s = masked_scores(head_part(qb, h))
            top = jnp.max(s, 0, keepdims=True)
            e = jnp.exp(s - top)
            total = jnp.sum(e, 0, keepdims=True)
            hrows = aligned(h, DH)
            ot[hrows] = dot(vt[hrows], e.astype(BF16)) / total
            lse[h, :, rows] = top + jnp.log(total)
            return 0

        lax.fori_loop(0, heads, head, 0)
        att[rows] = ot[...].T.astype(BF16)

    def out_proj(b):
        ab = att[aligned(b, seq)]
        return lambda n: dot_last(ab, wo[aligned(n, TILE)])

    attend(c_ysib)
    for j in range(1, nt):
        w_cross(1, j)
    attend(c_y)
    for i in range(nc):
        w_spread(1, i)
    w_wait(1)
    rs_sib(0, 0, out_proj(c_ysib))
    rs_y(0, out_proj(c_y))
    for j in range(1, nt):
        w_cross(2, j)
    attend(c_sib)
    rs_sib(0, 1, out_proj(c_sib))
    for i in range(nc):
        w_spread(2, i)
    attend(c)
    rs_own(0, out_proj(c))
    rs_copy(0, 1).wait_recv()

    b_out, gain1, shift1 = vec[0:1], vec[1:2], vec[2:3]
    b_down, gain2, shift2 = vec[3:4], vec[4:5], vec[5:6]
    own = c * seq

    def own_slice(rows):
        return pl.ds(pl.multiple_of(own + rows.start, ROWS), ROWS)

    def norm1(rows, i):
        h = x_tok[own_slice(rows)].astype(F32) + rs_row(rows) + b_out
        cen = h - mean(h)
        inv = lax.rsqrt(mean(cen * cen) + 1e-5)
        xh = cen * inv
        xh1[rows] = xh
        rstd1[rows] = jnp.broadcast_to(inv, (ROWS, 128))
        nl[own_slice(rows)] = (xh * gain1 + shift1).astype(BF16)

    for k in range(CHUNKS):
        rs_rows(0, k, norm1)
        ag_send(nl, 1, k)
    for j in range(1, nt):
        w_cross(3, j)
    w_wait(2)

    def up(b):
        rows = aligned(b, seq)
        nb = nl[rows]

        def tile(n, _):
            cols = aligned(n, TILE)
            v = dot(nb, wu[:, cols]) + bias[0:1, pl.ds(pl.multiple_of(2 * hid + n * TILE, 128), TILE)]
            cdf = 0.5 * (1.0 + lax.erf(v * math.sqrt(0.5)))
            act[rows, cols] = (v * cdf).astype(BF16)
            pdf = jnp.exp(-0.5 * v * v) * (1.0 / math.sqrt(2.0 * math.pi))
            dg[rows, cols] = (cdf + v * pdf).astype(BF16)
            return 0

        lax.fori_loop(0, ff // TILE, tile, 0)

    def down(b):
        ab = act[aligned(b, seq)]
        return lambda n: dot_last(ab, wd[aligned(n, TILE)])

    up(c)
    for i in range(nc):
        w_spread(3, i)
    for k in range(CHUNKS):
        ag_wait(nl, 1, k, 0)
    up(c_sib)
    for k in range(CHUNKS):
        ag_pass(nl, 1, k)
    w_wait(3)
    rs_sib(1, 1, down(c_sib))
    rs_own(1, down(c))
    up(c_y)
    for k in range(CHUNKS):
        ag_wait(nl, 1, k, 2)
    up(c_ysib)
    rs_sib(1, 0, down(c_ysib))
    rs_y(1, down(c_y))
    rs_copy(1, 1).wait_recv()
    pltpu.make_async_copy(ct_h.at[t], ct_s, loc_sem.at[1]).wait()

    def norm2(rows, i):
        h = xh1[rows] * gain1 + shift1 + rs_row(rows) + b_down
        cen = h - mean(h)
        inv = lax.rsqrt(mean(cen * cen) + 1e-5)
        xh = cen * inv
        res_s[rows] = (xh * gain2 + shift2).astype(BF16)
        pos = own + rows.start + lax.broadcasted_iota(jnp.int32, (ROWS, width), 0)
        top = jnp.where(pos < length, ct_s[rows].astype(F32), 0.0)
        add_sum(4, top * xh)
        add_sum(5, top)
        gy = top * gain2
        dr = (gy - mean(gy) - xh * mean(gy * xh)) * inv
        add_sum(3, dr)
        dres[rows] = dr
        dl2[own_slice(rows)] = dr.astype(BF16)

    for k in range(CHUNKS):
        rs_rows(1, k, norm2)
        ag_send(dl2, 2, k)

    def spread(share, out, o):
        pltpu.make_async_copy(share, out.at[t], out_r.at[o, 0]).start()
        for j in range(1, nt):
            remote(
                share, out.at[t], out_s.at[o, j], out_r.at[o, j], (f, c, lax.rem(t + j, nt))
            ).start()

    def spread_wait(share, out, o):
        pltpu.make_async_copy(share, out.at[t], out_r.at[o, 0]).wait()
        for j in range(1, nt):
            ts = lax.rem(t + nt - j, nt)
            remote(share, out.at[ts], out_s.at[o, j], out_r.at[o, j], (f, c, ts)).wait_recv()
            remote(
                share, out.at[t], out_s.at[o, j], out_r.at[o, j], (f, c, lax.rem(t + j, nt))
            ).wait_send()

    spread(res_s, res_h, 0)

    def back(b):
        rows = aligned(b, seq)
        db = dl2[rows]

        def tile(n, _):
            cols = aligned(n, TILE)
            dp = (dot(db, wd[:, cols]) * dg[rows, cols].astype(F32)).astype(BF16)
            dpl[rows, cols] = dp
            dpf = dp.astype(F32)
            sums[6, :, cols] = sums[6, :, cols] + jnp.sum(dpf.reshape(seq // 8, 8, TILE), 0)
            return 0

        lax.fori_loop(0, ff // TILE, tile, 0)

    def up_back(b):
        pb = dpl[aligned(b, seq)]
        return lambda n: dot_last(pb, wu[aligned(n, TILE)])

    def weight_grad(dst, left, right):
        def step(m, _):
            rows = aligned(m, TILE)
            dst[rows] = dot_first(left[:, rows], right[...]).astype(BF16)
            return 0

        lax.fori_loop(0, width // TILE, step, 0)

    grads = ((gwd, xg_d, zg_d), (gwu, xg_u, zg_u), (gwo, xg_o, zg_o), (gqkv, xg_q, zg_q))
    part_rows = nc * rows_w

    def gx_copy(g, df, dev_f):
        buf, got, _ = grads[g]
        return remote(
            buf.at[aligned(dev_f, part_rows)],
            got.at[df - 1],
            gx_s.at[g, df],
            gx_r.at[g, df],
            (dev_f, c, t),
        )

    def g_start(g):
        for df in range(1, nf):
            gx_copy(g, df, lax.rem(f + df, nf)).start()

    def gz_copy(g, dc):
        buf, _, got = grads[g]
        cc = lax.rem(c + dc, nc)
        return remote(buf.at[own_rows(cc)], got.at[t], gz_s.at[g, dc], gz_r.at[g, t], (f, cc, c))

    def g_cross(g):
        buf, got, _ = grads[g]
        for df in range(1, nf):
            gx_copy(g, df, lax.rem(f + nf - df, nf)).wait_recv()

        def add(i, _):
            rows = pl.ds(pl.multiple_of(f * part_rows + i * ROWS, ROWS), ROWS)
            total = buf[rows].astype(F32)
            for df in range(1, nf):
                total = total + got[df - 1, pl.ds(pl.multiple_of(i * ROWS, ROWS), ROWS)].astype(F32)
            buf[rows] = total.astype(BF16)
            return 0

        lax.fori_loop(0, part_rows // ROWS, add, 0)
        for dc in range(1, nc):
            gz_copy(g, dc).start()

        @pl.when(t != c)
        def _():
            gz_copy(g, 0).start()

        @pl.when(t == c)
        def _():
            pltpu.make_async_copy(
                buf.at[own_rows(c)], grads[g][2].at[t], gz_r.at[g, t]
            ).start()

    def g_out(g, store):
        _, _, got = grads[g]
        for s in range(nt):
            remote(got.at[s], got.at[s], gz_s.at[g, 0], gz_r.at[g, s], (f, t, s)).wait_recv()

        def add(i, _):
            rows = pl.ds(pl.multiple_of(i * ROWS, ROWS), ROWS)
            total = got[0, rows].astype(F32)
            for s in range(1, nt):
                total = total + got[s, rows].astype(F32)
            store(rows, total)
            return 0

        lax.fori_loop(0, rows_w // ROWS, add, 0)

    def g_finish(g):
        for df in range(1, nf):
            gx_copy(g, df, lax.rem(f + df, nf)).wait_send()
        for dc in range(1, nc):
            gz_copy(g, dc).wait_send()

        @pl.when(t != c)
        def _():
            gz_copy(g, 0).wait_send()

    back(c)
    for k in range(CHUNKS):
        ag_wait(dl2, 2, k, 0)
    back(c_sib)
    rs_sib(2, 1, up_back(c_sib))
    rs_own(2, up_back(c))
    for k in range(CHUNKS):
        ag_pass(dl2, 2, k)
    back(c_y)
    for k in range(CHUNKS):
        ag_wait(dl2, 2, k, 2)
    back(c_ysib)
    rs_sib(2, 0, up_back(c_ysib))
    rs_y(2, up_back(c_y))
    weight_grad(gwd, dl2, act)
    g_start(0)
    rs_copy(2, 1).wait_recv()

    def norm1_back(rows, i):
        dn = dres[rows] + rs_row(rows)
        xh = xh1[rows]
        add_sum(1, dn * xh)
        add_sum(2, dn)
        gy = dn * gain1
        dr = (gy - mean(gy) - xh * mean(gy * xh)) * rstd1[rows, 0:1]
        add_sum(0, dr)
        dres[rows] = dr
        dl1[own_slice(rows)] = dr.astype(BF16)

    for k in range(CHUNKS):
        rs_rows(2, k, norm1_back)
        ag_send(dl1, 3, k)
    weight_grad(gwu, nl, dpl)
    g_start(1)

    dk_acc[...] = jnp.zeros_like(dk_acc)
    dv_acc[...] = jnp.zeros_like(dv_acc)

    def attend_back(b):
        rows = aligned(b, seq)
        datt[rows] = dot(dl1[rows], wo[...]).astype(BF16)
        qb = qs[rows]
        db = datt[rows]

        def head(h, _):
            qm = head_part(qb, h)
            dm = head_part(db, h)
            p = jnp.exp(masked_scores(qm) - lse[h, :, rows])
            dv_acc[...] += dot(p.astype(BF16), dm)
            pd = p * dot_last(vv[...], dm)
            delta = jnp.sum(pd, 0, keepdims=True)
            ds = (pd - p * delta).astype(BF16)
            dk_acc[...] += dot(ds, qm)
            hrows = aligned(h, DH)
            ot[hrows] = dot(kt[hrows], ds)
            return 0

        lax.fori_loop(0, heads, head, 0)
        dq = (ot[...].T * scale).astype(BF16)
        dqkv[rows, 0:hid] = dq
        dqf = dq.astype(F32)
        sums[7, :, 0:hid] = sums[7, :, 0:hid] + jnp.sum(dqf.reshape(seq // 8, 8, hid), 0)

    attend_back(c)
    for k in range(CHUNKS):
        ag_wait(dl1, 3, k, 0)
    for k in range(CHUNKS):
        ag_pass(dl1, 3, k)
    attend_back(c_sib)
    g_cross(0)
    attend_back(c_y)
    for k in range(CHUNKS):
        ag_wait(dl1, 3, k, 2)
    weight_grad(gwo, dl1, att)
    g_start(2)
    attend_back(c_ysib)
    g_cross(1)

    def finish_kv(b, _):
        rows = aligned(b, seq)
        dqkv[rows, hid : 2 * hid] = dk_acc[rows].astype(BF16)
        dvb = dv_acc[rows].astype(BF16)
        dqkv[rows, 2 * hid : 3 * hid] = dvb
        sums[7, :, hid : 2 * hid] = sums[7, :, hid : 2 * hid] + jnp.sum(
            dvb.astype(F32).reshape(seq // 8, 8, hid), 0
        )
        return 0

    lax.fori_loop(0, nc, finish_kv, 0)

    def in_back(b):
        qb = dqkv[aligned(b, seq)]
        return lambda n: dot_last(qb, wqkv[aligned(n, TILE)])

    rs_sib(3, 0, in_back(c_ysib))
    rs_y(3, in_back(c_y))
    rs_sib(3, 1, in_back(c_sib))
    rs_own(3, in_back(c))
    weight_grad(gqkv, x_tok, dqkv)
    g_start(3)
    sm[...] = jnp.sum(sums[...], 1)

    def sm_copy(stage, j, src, dst, dev):
        return remote(src, dst, sm_s.at[stage, j], sm_r.at[stage, j], dev)

    for j in range(1, nt):
        sm_copy(0, j, sm, smz.at[j], (f, c, lax.rem(t + j, nt))).start()
    rs_copy(3, 1).wait_recv()

    def grad_in(rows, i):
        gi_s[rows] = (dres[rows] + rs_row(rows)).astype(BF16)

    for k in range(CHUNKS):
        rs_rows(3, k, grad_in)
    spread(gi_s, gi_h, 1)
    g_cross(2)
    total = sm[...]
    for j in range(1, nt):
        sm_copy(0, j, sm, smz.at[j], (f, c, lax.rem(t + nt - j, nt))).wait_recv()
        total = total + smz[j]
    smz[0] = total
    for df in range(1, nf):
        sm_copy(1, df, smz.at[0], smx.at[df], (lax.rem(f + df, nf), c, t)).start()
    g_cross(3)

    def store_at(out, base):
        def store(rows, value):
            out[rows, base : base + value.shape[1]] = value

        return store

    for df in range(1, nf):
        sm_copy(1, df, smz.at[0], smx.at[df], (lax.rem(f + nf - df, nf), c, t)).wait_recv()
        total = total + smx[df]
    smx[0] = total
    for dc in range(1, nc):
        sm_copy(2, dc, smx.at[0], smc.at[c], (f, lax.rem(c + dc, nc), t)).start()
    smc[c] = total
    g_out(0, store_at(gffn_o, ff))
    g_out(1, store_at(gffn_o, 0))
    g_out(2, store_at(gatt_o, 3 * hid))
    for dc in range(1, nc):
        cs = lax.rem(c + nc - dc, nc)
        sm_copy(2, dc, smx.at[0], smc.at[cs], (f, cs, t)).wait_recv()
    whole = smc[0]
    for s in range(1, nc):
        whole = whole + smc[s]
    small_o[0:6] = whole[0:6]
    small_o[6:8] = smc[t, 6:8]
    g_out(3, store_at(gatt_o, 0))
    spread_wait(res_s, res_h, 0)
    spread_wait(gi_s, gi_h, 1)

    for g in range(4):
        w_finish(g)
        g_finish(g)
    for a, buf in enumerate((x_tok, nl, dl2, dl1)):
        ag_finish(buf, a)
    rs_copy(3, 0).wait_send()
    rs_copy(3, 1).wait_send()
    for k in range(CHUNKS):
        ry_copy(3, k).wait_send()
    for j in range(1, nt):
        sm_copy(0, j, sm, smz.at[j], (f, c, lax.rem(t + j, nt))).wait_send()
    for df in range(1, nf):
        sm_copy(1, df, smz.at[0], smx.at[df], (lax.rem(f + df, nf), c, t)).wait_send()
    for dc in range(1, nc):
        sm_copy(2, dc, smx.at[0], smc.at[c], (f, lax.rem(c + dc, nc), t)).wait_send()

    @pl.when(t == c)
    def _():
        for j in range(1, nt):
            remote(
                bias_h, bias, bias_s.at[j], bias_r.at[0], (f, c, lax.rem(t + j, nt))
            ).wait_send()


def shards(
    dims,
    inputs,
    lengths,
    w_query,
    w_key,
    w_value,
    b_query,
    b_value,
    w_out,
    b_out,
    gain_attn,
    shift_attn,
    w_up,
    b_up,
    w_down,
    b_down,
    gain_ffn,
    shift_ffn,
    cotangent,
):
    nf, nc, nt = dims
    seq_dev, seq, width = inputs.shape
    rows_w, hid = w_query.shape
    ff = w_up.shape[1]
    assert nc == 4 and nt == nc and seq_dev == nt and ff == width
    tok = seq * nc
    heads = hid // DH
    part = nc * rows_w
    bias = jnp.broadcast_to(jnp.concatenate([b_query, b_value, b_up])[None], (8, 2 * hid + ff))
    zero = jnp.zeros_like(b_out)
    vec = jnp.stack([b_out, gain_attn, shift_attn, b_down, gain_ffn, shift_ffn, zero, zero])
    hbm = pl.BlockSpec(memory_space=pl.ANY)
    vmem = pl.BlockSpec(memory_space=pltpu.VMEM)
    smem = pl.BlockSpec(memory_space=pltpu.SMEM)

    def vb(*shape):
        return pltpu.VMEM(shape, BF16)

    def vf(*shape):
        return pltpu.VMEM(shape, F32)

    def sem(*shape):
        return pltpu.SemaphoreType.DMA(shape)

    result, grad_in, g_ffn, g_att, small = pl.pallas_call(
        functools.partial(layer, dims),
        out_shape=(
            jax.ShapeDtypeStruct((nt, seq, width), BF16),
            jax.ShapeDtypeStruct((nt, seq, width), BF16),
            jax.ShapeDtypeStruct((rows_w, 2 * ff), F32),
            jax.ShapeDtypeStruct((rows_w, 4 * hid), F32),
            jax.ShapeDtypeStruct((8, width), F32),
        ),
        in_specs=[smem] + [hbm] * 9 + [vmem],
        out_specs=(hbm, hbm, vmem, vmem, vmem),
        scratch_shapes=[
            vb(width, 3 * hid),
            vb(width, hid),
            vb(width, ff),
            vb(width, ff),
            vb(nt, rows_w, 3 * hid),
            vb(nt, rows_w, hid),
            vb(nt, rows_w, ff),
            vb(nt, rows_w, ff),
            vb(tok, width),
            vb(tok, width),
            vb(tok, width),
            vb(tok, width),
            vb(tok, hid),
            vb(tok, hid),
            vb(tok, hid),
            vb(hid, tok),
            vb(hid, tok),
            vb(tok, hid),
            vb(tok, hid),
            vf(hid, seq),
            vf(heads, 1, tok),
            vb(tok, ff),
            vb(tok, ff),
            vb(tok, ff),
            vb(tok, 3 * hid),
            vf(tok, hid),
            vf(tok, hid),
            vb(2, seq, width),
            vb(2, seq, width),
            vb(seq, width),
            vb(seq, width),
            vf(seq, width),
            vf(seq, width),
            vf(seq, width),
            vf(seq, 128),
            vf(seq, width),
            vb(seq, width),
            vb(seq, width),
            vb(seq, width),
            vf(8, 2 * hid + ff),
            vb(width, ff),
            vb(width, ff),
            vb(width, 3 * hid),
            vb(width, hid),
            vb(nf - 1, part, ff),
            vb(nf - 1, part, ff),
            vb(nf - 1, part, 3 * hid),
            vb(nf - 1, part, hid),
            vb(nt, rows_w, ff),
            vb(nt, rows_w, ff),
            vb(nt, rows_w, 3 * hid),
            vb(nt, rows_w, hid),
            vf(8, 8, width),
            vf(8, width),
            vf(nt, 8, width),
            vf(nf, 8, width),
            vf(nc, 8, width),
            sem(3),
            sem(nt),
            sem(1),
            sem(4, nt),
            sem(4, nt),
            sem(4, nt),
            sem(4, nc),
            sem(4, nf),
            sem(4, nf),
            sem(4, 3, CHUNKS),
            sem(4, 3, CHUNKS),
            sem(4, 2),
            sem(4, 2),
            sem(4, CHUNKS),
            sem(4, CHUNKS),
            sem(2, nt),
            sem(2, nt),
            sem(4, nf),
            sem(4, nf),
            sem(4, nc),
            sem(4, nt),
            sem(3, max(nf, nc)),
            sem(3, max(nf, nc)),
        ],
        compiler_params=pltpu.CompilerParams(
            collective_id=0, has_side_effects=True, vmem_limit_bytes=63 << 20
        ),
    )(lengths, inputs, cotangent, w_query, w_key, w_value, w_out, w_up, w_down, bias, vec)
    return (
        result,
        grad_in.astype(F32),
        g_att[:, :hid],
        g_att[:, hid : 2 * hid],
        g_att[:, 2 * hid : 3 * hid],
        small[7, :hid],
        small[7, hid : 2 * hid],
        g_att[:, 3 * hid :],
        small[0],
        small[1],
        small[2],
        g_ffn[:, :ff],
        small[6, :ff],
        g_ffn[:, ff:],
        small[3],
        small[4],
        small[5],
    )


def solution(mesh):
    weight = P(("fsdp", "ctx"), "tp")
    acts = P("fsdp", "ctx", None)
    dims = tuple(mesh.shape[a] for a in ("fsdp", "ctx", "tp"))
    return jax.shard_map(
        functools.partial(shards, dims),
        mesh=mesh,
        in_specs=(
            acts,
            P("fsdp"),
            weight,
            weight,
            weight,
            P("tp"),
            P("tp"),
            weight,
            P(),
            P(),
            P(),
            weight,
            P("tp"),
            weight,
            P(),
            P(),
            P(),
            acts,
        ),
        out_specs=(
            acts,
            acts,
            weight,
            weight,
            weight,
            P("tp"),
            P("tp"),
            weight,
            P(),
            P(),
            P(),
            weight,
            P("tp"),
            weight,
            P(),
            P(),
            P(),
        ),
        check_vma=False,
    )
```

```python
import functools
import math

import jax
import jax.numpy as jnp
from jax import lax
from jax.experimental import pallas as pl
from jax.experimental.pallas import tpu as pltpu
from jax.sharding import PartitionSpec as P

DH = 64
MESH = pl.DeviceIdType.MESH
F32 = jnp.float32
BF16 = jnp.bfloat16
TILE = 256
ROWS = 16
CHUNKS = 2


def dot(left, right):
    return jnp.dot(left, right, preferred_element_type=F32)


def dot_last(left, right):
    return lax.dot_general(left, right, (((1,), (1,)), ((), ())), preferred_element_type=F32)


def dot_first(left, right):
    return lax.dot_general(left, right, (((0,), (0,)), ((), ())), preferred_element_type=F32)


def aligned(index, size):
    return pl.ds(pl.multiple_of(index * size, size), size)


def layer(
    dims,
    lens,
    x_h,
    ct_h,
    wq_h,
    wk_h,
    wv_h,
    wo_h,
    wu_h,
    wd_h,
    bias_h,
    vec,
    res_h,
    gi_h,
    gffn_o,
    gatt_o,
    small_o,
    wqkv,
    wo,
    wu,
    wd,
    z0,
    z1,
    z2,
    z3,
    x_tok,
    nl,
    dl2,
    dl1,
    qs,
    kk,
    vv,
    kt,
    vt,
    att,
    datt,
    ot,
    lse,
    act,
    dg,
    dpl,
    dqkv,
    dk_acc,
    dv_acc,
    ps,
    pr,
    ysend,
    yrecv,
    acc_y,
    acc_o,
    xh1,
    rstd1,
    dres,
    res_s,
    gi_s,
    ct_s,
    bias,
    gwd,
    gwu,
    gqkv,
    gwo,
    xg_d,
    xg_u,
    xg_q,
    xg_o,
    zf_d,
    zf_u,
    zf_q,
    zf_o,
    zp_d,
    zp_u,
    zp_q,
    zp_o,
    sums,
    sm,
    smz,
    smx,
    smc,
    loc_sem,
    bias_s,
    bias_r,
    wz_s,
    wz_r,
    wy_s,
    wy_r,
    wx_s,
    wx_r,
    ag_s,
    ag_r,
    rs_s,
    rs_r,
    ry_s,
    ry_r,
    out_s,
    out_r,
    gx_s,
    gx_r,
    gy_s,
    gy_r,
    gz_s,
    gz_r,
    line_s,
    line_r,
    sm_s,
    sm_r,
):
    nf, nc, nt = dims
    f = lax.axis_index("fsdp")
    c = lax.axis_index("ctx")
    t = lax.axis_index("tp")
    yi, ki = c // 2, lax.rem(c, 2)
    c_sib = yi * 2 + (1 - ki)
    c_y = (1 - yi) * 2 + ki
    c_ysib = (1 - yi) * 2 + (1 - ki)
    seq, width = ct_s.shape
    tok = x_tok.shape[0]
    rows_w = z0.shape[1]
    hid = wo.shape[1]
    ff = wu.shape[1]
    heads = hid // DH
    scale = 1.0 / math.sqrt(DH)
    chunk = seq // CHUNKS
    sib = (f, c_sib, t)
    ypeer = (f, c_y, t)
    length = lens[t]

    def remote(src, dst, ssem, rsem, dev):
        return pltpu.make_async_remote_copy(
            src_ref=src, dst_ref=dst, send_sem=ssem, recv_sem=rsem, device_id=dev, device_id_type=MESH
        )

    bar = pltpu.get_barrier_semaphore()
    for dc in range(nc):
        for dt in range(nt):
            if dc or dt:
                pl.semaphore_signal(
                    bar,
                    inc=1,
                    device_id=(f, lax.rem(c + dc, nc), lax.rem(t + dt, nt)),
                    device_id_type=MESH,
                )
    for df in range(1, nf):
        pl.semaphore_signal(bar, inc=1, device_id=(lax.rem(f + df, nf), c, t), device_id_type=MESH)
    pl.semaphore_wait(bar, nc * nt - 1 + nf - 1)

    groups = (
        ((wq_h, wk_h, wv_h), z0, wqkv),
        ((wo_h,), z1, wo),
        ((wu_h,), z2, wu),
        ((wd_h,), z3, wd),
    )

    def own_rows(cc):
        return aligned(f * nc + cc, rows_w)

    def own_copies(g):
        srcs, stage, _ = groups[g]
        for k, src in enumerate(srcs):
            cols = pl.ds(k * src.shape[1], src.shape[1])
            dst = stage.at[t, :, cols]
            pltpu.make_async_copy(src, dst, wz_r.at[g, 0]).start()
            yield src, dst

    def w_start(g):
        for src, dst in own_copies(g):
            for j in range(1, nt):
                remote(src, dst, wz_s.at[g, j], wz_r.at[g, j], (f, c, lax.rem(t + j, nt))).start()

    def w_cross_block(g, ts):
        _, stage, final = groups[g]

        @pl.when(ts == c)
        def _():
            pltpu.make_async_copy(stage.at[ts], final.at[own_rows(c)], wy_r.at[g, c]).start()

        @pl.when(ts != c)
        def _():
            remote(
                stage.at[ts], final.at[own_rows(c)], wy_s.at[g, ts], wy_r.at[g, c], (f, ts, t)
            ).start()

    def w_cross(g, j):
        stage = groups[g][1]
        ts = lax.rem(t + nt - j, nt)
        if j == 0:
            pltpu.make_async_copy(stage.at[ts], stage.at[ts], wz_r.at[g, 0]).wait()
        else:
            remote(stage.at[ts], stage.at[ts], wz_s.at[g, j], wz_r.at[g, j], (f, c, ts)).wait_recv()
        w_cross_block(g, ts)

    def hops(send, h):
        @pl.when((t >= h) & (t < nt - 1))
        def _():
            send(t - h, h + 1, t + 1)

        @pl.when((t + h < nt) & (t > 0))
        def _():
            send(t + h, nt + h, t - 1)

    def arrivals(take, h):
        @pl.when(t >= h)
        def _():
            take(t - h, h, t - 1)

        @pl.when(t + h < nt)
        def _():
            take(t + h, nt - 1 + h, t + 1)

    def w_line_copy(g, src, ts, n, to):
        return remote(
            src, groups[g][1].at[ts], wz_s.at[g, n], wz_r.at[g, n], (f, c, to)
        )

    def w_line_start(g):
        for src, _ in own_copies(g):
            hops(lambda ts, n, to: w_line_copy(g, src, ts, n, to).start(), 0)

    def w_line(g, h):
        stage = groups[g][1]

        def take(ts, n, source):
            w_line_copy(g, stage.at[ts], ts, n, source).wait_recv()

        arrivals(take, h)
        if h < nt - 1:
            hops(lambda ts, n, to: w_line_copy(g, stage.at[ts], ts, n, to).start(), h)
        arrivals(lambda ts, n, source: w_cross_block(g, ts), h)

    def w_spread(g, i):
        _, _, final = groups[g]
        cc = lax.rem(c + i, nc)
        part = final.at[own_rows(cc)]
        if i == 0:
            pltpu.make_async_copy(part, part, wy_r.at[g, cc]).wait()
        else:
            remote(part, part, wy_s.at[g, 0], wy_r.at[g, cc], (f, cc, t)).wait_recv()
        for df in range(1, nf):
            remote(
                part, part, wx_s.at[g, df], wx_r.at[g, df], (lax.rem(f + df, nf), c, t)
            ).start()

    def w_wait(g):
        _, _, final = groups[g]
        for df in range(1, nf):
            fs = lax.rem(f + nf - df, nf)
            part = final.at[aligned(fs, nc * rows_w)]
            remote(part, part, wx_s.at[g, df], wx_r.at[g, df], (fs, c, t)).wait_recv()

    def w_finish(g):
        _, stage, final = groups[g]
        if g < 2:
            for j in range(1, nt):
                remote(
                    stage.at[0], stage.at[0], wz_s.at[g, j], wz_r.at[g, j], (f, c, lax.rem(t + j, nt))
                ).wait_send()
        else:
            for h in range(nt - 1):
                hops(
                    lambda ts, n, to: w_line_copy(g, stage.at[ts], ts, n, to).wait_send(), h
                )
        for j in range(nt):
            ts = lax.rem(t + nt - j, nt)

            @pl.when(ts != c)
            def _():
                remote(
                    stage.at[ts], final.at[own_rows(c)], wy_s.at[g, ts], wy_r.at[g, c], (f, ts, t)
                ).wait_send()

        for df in range(1, nf):
            part = final.at[aligned(f, nc * rows_w)]
            remote(
                part, part, wx_s.at[g, df], wx_r.at[g, df], (lax.rem(f + df, nf), c, t)
            ).wait_send()

    def part_of(buf, cc, k):
        return buf.at[pl.ds(pl.multiple_of(cc * seq + k * chunk, chunk), chunk)]

    def ag_copy(buf, a, k, cc, way, dev):
        part = part_of(buf, cc, k)
        return remote(part, part, ag_s.at[a, way, k], ag_r.at[a, way, k], dev)

    def ag_send(buf, a, k):
        ag_copy(buf, a, k, c, 1, ypeer).start()
        ag_copy(buf, a, k, c, 0, sib).start()

    def ag_pass(buf, a, k):
        ag_copy(buf, a, k, c_y, 1, ypeer).wait_recv()
        ag_copy(buf, a, k, c_y, 2, sib).start()

    def ag_wait(buf, a, k, way):
        ag_copy(buf, a, k, c_sib if way == 0 else c_ysib, way, sib).wait_recv()

    def ag_finish(buf, a):
        for k in range(CHUNKS):
            ag_copy(buf, a, k, c, 0, sib).wait_send()
            ag_copy(buf, a, k, c, 1, ypeer).wait_send()
            ag_copy(buf, a, k, c_y, 2, sib).wait_send()

    tiles = width // TILE

    def rs_copy(o, slot):
        return remote(ps.at[slot], pr.at[slot], rs_s.at[o, slot], rs_r.at[o, slot], sib)

    def ry_copy(o, k):
        rows = pl.ds(k * chunk, chunk)
        return remote(ysend.at[rows], yrecv.at[rows], ry_s.at[o, k], ry_r.at[o, k], ypeer)

    def rs_sib(o, slot, produce):
        if o:
            rs_copy(o - 1, slot).wait_send()

        def tile(n, _):
            ps[slot, :, aligned(n, TILE)] = produce(n).astype(BF16)
            return 0

        lax.fori_loop(0, tiles, tile, 0)
        rs_copy(o, slot).start()

    def rs_y(o, produce):
        def tile(n, _):
            acc_y[:, aligned(n, TILE)] = produce(n)
            return 0

        lax.fori_loop(0, tiles, tile, 0)
        rs_copy(o, 0).wait_recv()
        for k in range(CHUNKS):
            if o:
                ry_copy(o - 1, k).wait_send()

            def add(i, _, k=k):
                rows = pl.ds(pl.multiple_of(k * chunk + i * ROWS, ROWS), ROWS)
                ysend[rows] = (acc_y[rows] + pr[0, rows].astype(F32)).astype(BF16)
                return 0

            lax.fori_loop(0, chunk // ROWS, add, 0)
            ry_copy(o, k).start()

    def rs_own(o, produce):
        def tile(n, _):
            acc_o[:, aligned(n, TILE)] = produce(n)
            return 0

        lax.fori_loop(0, tiles, tile, 0)

    def rs_row(rows):
        return acc_o[rows] + pr[1, rows].astype(F32) + yrecv[rows].astype(F32)

    def rs_rows(o, k, body):
        ry_copy(o, k).wait_recv()

        def step(i, _):
            body(pl.ds(pl.multiple_of(k * chunk + i * ROWS, ROWS), ROWS), i)
            return 0

        lax.fori_loop(0, chunk // ROWS, step, 0)

    def add_sum(k, value):
        half = value[0:8]
        for r in range(8, ROWS, 8):
            half = half + value[r : r + 8]
        sums[k] = sums[k] + half

    def mean(value):
        return jnp.sum(value, -1, keepdims=True) * (1.0 / width)

    w_start(0)
    pltpu.make_async_copy(x_h.at[t], x_tok.at[aligned(c, seq)], loc_sem.at[0]).start()
    pltpu.make_async_copy(ct_h.at[t], ct_s, loc_sem.at[1]).start()

    @pl.when(t == c)
    def _():
        pltpu.make_async_copy(bias_h, bias, loc_sem.at[2]).start()
        for j in range(1, nt):
            remote(bias_h, bias, bias_s.at[j], bias_r.at[0], (f, c, lax.rem(t + j, nt))).start()

    pltpu.make_async_copy(x_h.at[t], x_tok.at[aligned(c, seq)], loc_sem.at[0]).wait()
    for k in range(CHUNKS):
        ag_send(x_tok, 0, k)
    w_start(1)
    w_line_start(2)
    for _ in own_copies(3):
        pass
    for g in range(4):
        w_cross(g, 0)
    sums[...] = jnp.zeros_like(sums)
    for k in range(CHUNKS):
        ag_pass(x_tok, 0, k)
    for j in range(1, nt):
        w_cross(0, j)

    @pl.when(t == c)
    def _():
        pltpu.make_async_copy(bias_h, bias, loc_sem.at[2]).wait()

    @pl.when(t != c)
    def _():
        remote(bias_h, bias, bias_s.at[0], bias_r.at[0], (f, c, c)).wait_recv()

    for i in range(nc):
        w_spread(0, i)
    for j in range(1, nt):
        w_cross(1, j)
    for k in range(CHUNKS):
        ag_wait(x_tok, 0, k, 0)
        ag_wait(x_tok, 0, k, 2)
    for i in range(nc):
        w_spread(1, i)
    w_wait(0)

    def project(b, _):
        rows = aligned(b, seq)
        xb = x_tok[rows]
        qv = dot(xb, wqkv[:, 0:hid]) + bias[0:1, 0:hid]
        qs[rows] = (qv * scale).astype(BF16)
        kb = dot(xb, wqkv[:, hid : 2 * hid])
        kk[rows] = kb.astype(BF16)
        kt[:, rows] = kb.T.astype(BF16)
        vb = dot(xb, wqkv[:, 2 * hid : 3 * hid]) + bias[0:1, hid : 2 * hid]
        vv[rows] = vb.astype(BF16)
        vt[:, rows] = vb.T.astype(BF16)
        return 0

    lax.fori_loop(0, nc, project, 0)

    lane = lax.broadcasted_iota(jnp.int32, (seq, hid), 1)

    def head_part(value, h):
        inside = (lane >= h * DH) & (lane < (h + 1) * DH)
        return jnp.where(inside, value, jnp.zeros_like(value))

    def masked_scores(qm):
        s = dot_last(kk[...], qm)
        key = lax.broadcasted_iota(jnp.int32, s.shape, 0)
        return jnp.where(key < length, s, -1e30)

    def attend(b):
        rows = aligned(b, seq)
        qb = qs[rows]

        def head(h, _):
            s = masked_scores(head_part(qb, h))
            top = jnp.max(s, 0, keepdims=True)
            e = jnp.exp(s - top)
            total = jnp.sum(e, 0, keepdims=True)
            hrows = aligned(h, DH)
            ot[hrows] = dot(vt[hrows], e.astype(BF16)) / total
            lse[h, :, rows] = top + jnp.log(total)
            return 0

        lax.fori_loop(0, heads, head, 0)
        att[rows] = ot[...].T.astype(BF16)

    def out_proj(b):
        ab = att[aligned(b, seq)]
        return lambda n: dot_last(ab, wo[aligned(n, TILE)])

    w_line(2, 1)
    for g in (3,):
        for k, src in enumerate(groups[g][0]):
            hops(lambda ts, n, to: w_line_copy(g, src, ts, n, to).start(), 0)
    attend(c_ysib)
    attend(c_y)
    w_line(2, 2)
    w_wait(1)
    rs_sib(0, 0, out_proj(c_ysib))
    rs_y(0, out_proj(c_y))
    attend(c_sib)
    rs_sib(0, 1, out_proj(c_sib))
    w_line(2, 3)
    w_line(3, 1)
    for i in range(nc):
        w_spread(2, i)
    attend(c)
    rs_own(0, out_proj(c))
    w_line(3, 2)
    rs_copy(0, 1).wait_recv()

    b_out, gain1, shift1 = vec[0:1], vec[1:2], vec[2:3]
    b_down, gain2, shift2 = vec[3:4], vec[4:5], vec[5:6]
    own = c * seq

    def own_slice(rows):
        return pl.ds(pl.multiple_of(own + rows.start, ROWS), ROWS)

    def norm1(rows, i):
        h = x_tok[own_slice(rows)].astype(F32) + rs_row(rows) + b_out
        cen = h - mean(h)
        inv = lax.rsqrt(mean(cen * cen) + 1e-5)
        xh = cen * inv
        xh1[rows] = xh
        rstd1[rows] = jnp.broadcast_to(inv, (ROWS, 128))
        nl[own_slice(rows)] = (xh * gain1 + shift1).astype(BF16)

    for k in range(CHUNKS):
        rs_rows(0, k, norm1)
        ag_send(nl, 1, k)
    w_line(3, 3)
    for i in range(nc):
        w_spread(3, i)
    w_wait(2)

    def up(b):
        rows = aligned(b, seq)
        nb = nl[rows]

        def tile(n, _):
            cols = aligned(n, TILE)
            v = dot(nb, wu[:, cols]) + bias[0:1, pl.ds(pl.multiple_of(2 * hid + n * TILE, 128), TILE)]
            cdf = 0.5 * (1.0 + lax.erf(v * math.sqrt(0.5)))
            act[rows, cols] = (v * cdf).astype(BF16)
            pdf = jnp.exp(-0.5 * v * v) * (1.0 / math.sqrt(2.0 * math.pi))
            dg[rows, cols] = (cdf + v * pdf).astype(BF16)
            return 0

        lax.fori_loop(0, ff // TILE, tile, 0)

    def down(b):
        ab = act[aligned(b, seq)]
        return lambda n: dot_last(ab, wd[aligned(n, TILE)])

    up(c)
    for k in range(CHUNKS):
        ag_wait(nl, 1, k, 0)
    up(c_sib)
    for k in range(CHUNKS):
        ag_pass(nl, 1, k)
    w_wait(3)
    rs_sib(1, 1, down(c_sib))
    rs_own(1, down(c))
    up(c_y)
    for k in range(CHUNKS):
        ag_wait(nl, 1, k, 2)
    up(c_ysib)
    rs_sib(1, 0, down(c_ysib))
    rs_y(1, down(c_y))
    rs_copy(1, 1).wait_recv()
    for g in range(4):
        w_finish(g)
    pltpu.make_async_copy(ct_h.at[t], ct_s, loc_sem.at[1]).wait()

    def norm2(rows, i):
        h = xh1[rows] * gain1 + shift1 + rs_row(rows) + b_down
        cen = h - mean(h)
        inv = lax.rsqrt(mean(cen * cen) + 1e-5)
        xh = cen * inv
        res_s[rows] = (xh * gain2 + shift2).astype(BF16)
        pos = own + rows.start + lax.broadcasted_iota(jnp.int32, (ROWS, width), 0)
        top = jnp.where(pos < length, ct_s[rows].astype(F32), 0.0)
        add_sum(4, top * xh)
        add_sum(5, top)
        gy = top * gain2
        dr = (gy - mean(gy) - xh * mean(gy * xh)) * inv
        add_sum(3, dr)
        dres[rows] = dr
        dl2[own_slice(rows)] = dr.astype(BF16)

    for k in range(CHUNKS):
        rs_rows(1, k, norm2)
        ag_send(dl2, 2, k)

    def spread(share, out, o):
        pltpu.make_async_copy(share, out.at[t], out_r.at[o, 0]).start()
        for j in range(1, nt):
            remote(
                share, out.at[t], out_s.at[o, j], out_r.at[o, j], (f, c, lax.rem(t + j, nt))
            ).start()

    def spread_wait(share, out, o):
        pltpu.make_async_copy(share, out.at[t], out_r.at[o, 0]).wait()
        for j in range(1, nt):
            ts = lax.rem(t + nt - j, nt)
            remote(share, out.at[ts], out_s.at[o, j], out_r.at[o, j], (f, c, ts)).wait_recv()
            remote(
                share, out.at[t], out_s.at[o, j], out_r.at[o, j], (f, c, lax.rem(t + j, nt))
            ).wait_send()

    spread(res_s, res_h, 0)

    def back(b):
        rows = aligned(b, seq)
        db = dl2[rows]

        def tile(n, _):
            cols = aligned(n, TILE)
            dp = (dot(db, wd[:, cols]) * dg[rows, cols].astype(F32)).astype(BF16)
            dpl[rows, cols] = dp
            dpf = dp.astype(F32)
            sums[6, :, cols] = sums[6, :, cols] + jnp.sum(dpf.reshape(seq // 8, 8, TILE), 0)
            return 0

        lax.fori_loop(0, ff // TILE, tile, 0)

    def up_back(b):
        pb = dpl[aligned(b, seq)]
        return lambda n: dot_last(pb, wu[aligned(n, TILE)])

    def weight_grad(dst, left, right):
        def step(m, _):
            rows = aligned(m, TILE)
            dst[rows] = dot_first(left[:, rows], right[...]).astype(BF16)
            return 0

        lax.fori_loop(0, width // TILE, step, 0)

    grads = (
        (gwd, xg_d, z3, zf_d, zp_d),
        (gwu, xg_u, z2, zf_u, zp_u),
        (gwo, xg_o, z1, zf_o, zp_o),
        (gqkv, xg_q, z0, zf_q, zp_q),
    )
    pair = t + 1 - 2 * lax.rem(t, 2)
    inner = (t == 1) | (t == nt - 2)
    far_in = jnp.where(t < 2, 2, 1)
    far_out = jnp.where(t < 2, nt - 1, 0)

    def gx_copy(g, df, i, dev_f):
        buf, got = grads[g][:2]
        cc = lax.rem(c + i, nc)
        return remote(
            buf.at[aligned(dev_f * nc + cc, rows_w)],
            got.at[df - 1, aligned(cc, rows_w)],
            gx_s.at[g, df, i],
            gx_r.at[g, df, i],
            (dev_f, c, t),
        )

    order = tuple(range(1, nc)) + (0,)

    def g_start(g):
        for i in order:
            for df in range(1, nf):
                gx_copy(g, df, i, lax.rem(f + df, nf)).start()

    def gy_copy(g, i, slot, cc):
        buf, _, got = grads[g][:3]
        return remote(
            buf.at[own_rows(cc)], got.at[slot], gy_s.at[g, i], gy_r.at[g, i], (f, cc, t)
        )

    def g_cross(g, i):
        buf, got, held = grads[g][:3]
        cc = lax.rem(c + i, nc)
        for df in range(1, nf):
            gx_copy(g, df, i, lax.rem(f + nf - df, nf)).wait_recv()

        def add(n, _):
            rows = pl.ds(pl.multiple_of((f * nc + cc) * rows_w + n * ROWS, ROWS), ROWS)
            total = buf[rows].astype(F32)
            for df in range(1, nf):
                theirs = pl.ds(pl.multiple_of(cc * rows_w + n * ROWS, ROWS), ROWS)
                total = total + got[df - 1, theirs].astype(F32)
            if i:
                buf[rows] = total.astype(BF16)
            else:
                held[c, pl.ds(pl.multiple_of(n * ROWS, ROWS), ROWS)] = total.astype(BF16)
            return 0

        lax.fori_loop(0, rows_w // ROWS, add, 0)
        if i:
            gy_copy(g, i, c, cc).start()

    def gz_copy(g, n, src, dst, to):
        return remote(src, dst, gz_s.at[g, n], gz_r.at[g, n], (f, c, to))

    def g_line(g):
        _, _, held, final, part = grads[g]
        for i in range(1, nc):
            cs = lax.rem(c + nc - i, nc)
            gy_copy(g, i, cs, cs).wait_recv()

        @pl.when(jnp.logical_not(inner))
        def _():
            gz_copy(g, 2, held.at[far_out], part.at[1], pair).start()
            gz_copy(g, 1, held.at[far_in], part.at[0], pair).start()

        gz_copy(g, 0, held.at[pair], final.at[0], pair).start()

    def g_relay(g):
        _, _, held, final, part = grads[g]

        @pl.when(inner)
        def _():
            for n, (to, slot) in enumerate(((far_out, 1), (far_in, 0))):
                gz_copy(g, 1 + slot, held.at[to], part.at[slot], pair).wait_recv()

                def add(m, _):
                    rows = pl.ds(pl.multiple_of(m * ROWS, ROWS), ROWS)
                    held[to, rows] = (
                        held[to, rows].astype(F32) + part[slot, rows].astype(F32)
                    ).astype(BF16)
                    return 0

                lax.fori_loop(0, rows_w // ROWS, add, 0)
                remote(
                    held.at[to], final.at[1], gz_s.at[g, 1 + slot], gz_r.at[g, 3], (f, c, to)
                ).start()

    def g_out(g, store):
        _, _, held, final, _ = grads[g]
        gz_copy(g, 0, held.at[t], final.at[0], pair).wait_recv()
        gz_copy(g, 3, held.at[t], final.at[1], far_in).wait_recv()

        def add(m, _):
            rows = pl.ds(pl.multiple_of(m * ROWS, ROWS), ROWS)
            store(
                rows,
                held[t, rows].astype(F32)
                + final[0, rows].astype(F32)
                + final[1, rows].astype(F32),
            )
            return 0

        lax.fori_loop(0, rows_w // ROWS, add, 0)

    def g_finish(g):
        _, _, held, final, part = grads[g]
        for i in order:
            for df in range(1, nf):
                gx_copy(g, df, i, lax.rem(f + df, nf)).wait_send()
        for i in range(1, nc):
            gy_copy(g, i, c, lax.rem(c + i, nc)).wait_send()
        for n in range(3):
            gz_copy(g, n, held.at[0], final.at[0], pair).wait_send()

    back(c)
    for k in range(CHUNKS):
        ag_wait(dl2, 2, k, 0)
    back(c_sib)
    rs_sib(2, 1, up_back(c_sib))
    rs_own(2, up_back(c))
    for k in range(CHUNKS):
        ag_pass(dl2, 2, k)
    back(c_y)
    for k in range(CHUNKS):
        ag_wait(dl2, 2, k, 2)
    back(c_ysib)
    rs_sib(2, 0, up_back(c_ysib))
    rs_y(2, up_back(c_y))
    weight_grad(gwd, dl2, act)
    g_start(0)
    weight_grad(gwu, nl, dpl)
    g_start(1)
    rs_copy(2, 1).wait_recv()

    def norm1_back(rows, i):
        dn = dres[rows] + rs_row(rows)
        xh = xh1[rows]
        add_sum(1, dn * xh)
        add_sum(2, dn)
        gy = dn * gain1
        dr = (gy - mean(gy) - xh * mean(gy * xh)) * rstd1[rows, 0:1]
        add_sum(0, dr)
        dres[rows] = dr
        dl1[own_slice(rows)] = dr.astype(BF16)

    for k in range(CHUNKS):
        rs_rows(2, k, norm1_back)
        ag_send(dl1, 3, k)

    dk_acc[...] = jnp.zeros_like(dk_acc)
    dv_acc[...] = jnp.zeros_like(dv_acc)

    def attend_back(b):
        rows = aligned(b, seq)
        datt[rows] = dot(dl1[rows], wo[...]).astype(BF16)
        qb = qs[rows]
        db = datt[rows]

        def head(h, _):
            qm = head_part(qb, h)
            dm = head_part(db, h)
            p = jnp.exp(masked_scores(qm) - lse[h, :, rows])
            dv_acc[...] += dot(p.astype(BF16), dm)
            pd = p * dot_last(vv[...], dm)
            delta = jnp.sum(pd, 0, keepdims=True)
            ds = (pd - p * delta).astype(BF16)
            dk_acc[...] += dot(ds, qm)
            hrows = aligned(h, DH)
            ot[hrows] = dot(kt[hrows], ds)
            return 0

        lax.fori_loop(0, heads, head, 0)
        dq = (ot[...].T * scale).astype(BF16)
        dqkv[rows, 0:hid] = dq
        dqf = dq.astype(F32)
        sums[7, :, 0:hid] = sums[7, :, 0:hid] + jnp.sum(dqf.reshape(seq // 8, 8, hid), 0)

    attend_back(c)
    g_cross(0, 1)
    g_cross(0, 2)
    for k in range(CHUNKS):
        ag_wait(dl1, 3, k, 0)
    for k in range(CHUNKS):
        ag_pass(dl1, 3, k)
    attend_back(c_sib)
    g_cross(0, 3)
    g_cross(0, 0)
    attend_back(c_y)
    for k in range(CHUNKS):
        ag_wait(dl1, 3, k, 2)
    weight_grad(gwo, dl1, att)
    g_start(2)
    g_line(0)
    for i in order:
        g_cross(1, i)
    attend_back(c_ysib)
    g_relay(0)
    g_line(1)

    def finish_kv(b, _):
        rows = aligned(b, seq)
        dqkv[rows, hid : 2 * hid] = dk_acc[rows].astype(BF16)
        dvb = dv_acc[rows].astype(BF16)
        dqkv[rows, 2 * hid : 3 * hid] = dvb
        sums[7, :, hid : 2 * hid] = sums[7, :, hid : 2 * hid] + jnp.sum(
            dvb.astype(F32).reshape(seq // 8, 8, hid), 0
        )
        return 0

    lax.fori_loop(0, nc, finish_kv, 0)

    def in_back(b):
        qb = dqkv[aligned(b, seq)]
        return lambda n: dot_last(qb, wqkv[aligned(n, TILE)])

    rs_sib(3, 0, in_back(c_ysib))
    rs_y(3, in_back(c_y))
    rs_sib(3, 1, in_back(c_sib))
    rs_own(3, in_back(c))
    weight_grad(gqkv, x_tok, dqkv)
    g_start(3)
    sm[...] = jnp.sum(sums[...], 1)

    def sm_copy(stage, j, src, dst, dev):
        return remote(src, dst, sm_s.at[stage, j], sm_r.at[stage, j], dev)

    for j in range(1, nt):
        sm_copy(0, j, sm, smz.at[j], (f, c, lax.rem(t + j, nt))).start()
    for i in order:
        g_cross(2, i)
    g_relay(1)
    rs_copy(3, 1).wait_recv()

    def grad_in(rows, i):
        gi_s[rows] = (dres[rows] + rs_row(rows)).astype(BF16)

    def line_copy(k, src, ts, n, to):
        rows = pl.ds(k * chunk, chunk)
        return remote(
            src.at[rows], gi_h.at[ts, rows], line_s.at[k, n], line_r.at[k, n], (f, c, to)
        )

    for k in range(CHUNKS):
        rs_rows(3, k, grad_in)
        rows = pl.ds(k * chunk, chunk)
        pltpu.make_async_copy(gi_s.at[rows], gi_h.at[t, rows], line_r.at[k, 0]).start()
        hops(lambda ts, n, to: line_copy(k, gi_s, ts, n, to).start(), 0)
    g_line(2)

    def line_hop(k, h):
        arrivals(lambda ts, n, source: line_copy(k, gi_h.at[ts], ts, n, source).wait_recv(), h)
        if h < nt - 1:
            hops(lambda ts, n, to: line_copy(k, gi_h.at[ts], ts, n, to).start(), h)

    for i in order[:2]:
        g_cross(3, i)
    for k in range(CHUNKS):
        line_hop(k, 1)
    for i in order[2:]:
        g_cross(3, i)
    g_line(3)
    g_relay(2)
    total = sm[...]
    for j in range(1, nt):
        sm_copy(0, j, sm, smz.at[j], (f, c, lax.rem(t + nt - j, nt))).wait_recv()
        total = total + smz[j]
    smz[0] = total
    for df in range(1, nf):
        sm_copy(1, df, smz.at[0], smx.at[df], (lax.rem(f + df, nf), c, t)).start()
    for k in range(CHUNKS):
        line_hop(k, 2)
    for df in range(1, nf):
        sm_copy(1, df, smz.at[0], smx.at[df], (lax.rem(f + nf - df, nf), c, t)).wait_recv()
        total = total + smx[df]
    smx[0] = total
    for dc in range(1, nc):
        sm_copy(2, dc, smx.at[0], smc.at[c], (f, lax.rem(c + dc, nc), t)).start()
    smc[c] = total
    g_relay(3)

    def store_at(out, base):
        def store(rows, value):
            out[rows, base : base + value.shape[1]] = value

        return store

    g_out(0, store_at(gffn_o, ff))
    g_out(1, store_at(gffn_o, 0))
    g_out(2, store_at(gatt_o, 3 * hid))
    for dc in range(1, nc):
        cs = lax.rem(c + nc - dc, nc)
        sm_copy(2, dc, smx.at[0], smc.at[cs], (f, cs, t)).wait_recv()
    whole = smc[0]
    for s in range(1, nc):
        whole = whole + smc[s]
    small_o[0:6] = whole[0:6]
    small_o[6:8] = smc[t, 6:8]
    g_out(3, store_at(gatt_o, 0))
    spread_wait(res_s, res_h, 0)
    for k in range(CHUNKS):
        line_hop(k, 3)
        rows = pl.ds(k * chunk, chunk)
        pltpu.make_async_copy(gi_s.at[rows], gi_h.at[t, rows], line_r.at[k, 0]).wait()
        for h in range(nt - 1):
            hops(lambda ts, n, to: line_copy(k, gi_h.at[ts], ts, n, to).wait_send(), h)

    for g in range(4):
        g_finish(g)
    for a, buf in enumerate((x_tok, nl, dl2, dl1)):
        ag_finish(buf, a)
    rs_copy(3, 0).wait_send()
    rs_copy(3, 1).wait_send()
    for k in range(CHUNKS):
        ry_copy(3, k).wait_send()
    for j in range(1, nt):
        sm_copy(0, j, sm, smz.at[j], (f, c, lax.rem(t + j, nt))).wait_send()
    for df in range(1, nf):
        sm_copy(1, df, smz.at[0], smx.at[df], (lax.rem(f + df, nf), c, t)).wait_send()
    for dc in range(1, nc):
        sm_copy(2, dc, smx.at[0], smc.at[c], (f, lax.rem(c + dc, nc), t)).wait_send()

    @pl.when(t == c)
    def _():
        for j in range(1, nt):
            remote(
                bias_h, bias, bias_s.at[j], bias_r.at[0], (f, c, lax.rem(t + j, nt))
            ).wait_send()


def shards(
    dims,
    inputs,
    lengths,
    w_query,
    w_key,
    w_value,
    b_query,
    b_value,
    w_out,
    b_out,
    gain_attn,
    shift_attn,
    w_up,
    b_up,
    w_down,
    b_down,
    gain_ffn,
    shift_ffn,
    cotangent,
):
    nf, nc, nt = dims
    seq_dev, seq, width = inputs.shape
    rows_w, hid = w_query.shape
    ff = w_up.shape[1]
    assert nc == 4 and nt == nc and seq_dev == nt and ff == width
    tok = seq * nc
    heads = hid // DH
    part = nc * rows_w
    bias = jnp.broadcast_to(jnp.concatenate([b_query, b_value, b_up])[None], (8, 2 * hid + ff))
    zero = jnp.zeros_like(b_out)
    vec = jnp.stack([b_out, gain_attn, shift_attn, b_down, gain_ffn, shift_ffn, zero, zero])
    hbm = pl.BlockSpec(memory_space=pl.ANY)
    vmem = pl.BlockSpec(memory_space=pltpu.VMEM)
    smem = pl.BlockSpec(memory_space=pltpu.SMEM)

    def vb(*shape):
        return pltpu.VMEM(shape, BF16)

    def vf(*shape):
        return pltpu.VMEM(shape, F32)

    def sem(*shape):
        return pltpu.SemaphoreType.DMA(shape)

    result, grad_in, g_ffn, g_att, small = pl.pallas_call(
        functools.partial(layer, dims),
        out_shape=(
            jax.ShapeDtypeStruct((nt, seq, width), BF16),
            jax.ShapeDtypeStruct((nt, seq, width), BF16),
            jax.ShapeDtypeStruct((rows_w, 2 * ff), F32),
            jax.ShapeDtypeStruct((rows_w, 4 * hid), F32),
            jax.ShapeDtypeStruct((8, width), F32),
        ),
        in_specs=[smem] + [hbm] * 9 + [vmem],
        out_specs=(hbm, hbm, vmem, vmem, vmem),
        scratch_shapes=[
            vb(width, 3 * hid),
            vb(width, hid),
            vb(width, ff),
            vb(width, ff),
            vb(nt, rows_w, 3 * hid),
            vb(nt, rows_w, hid),
            vb(nt, rows_w, ff),
            vb(nt, rows_w, ff),
            vb(tok, width),
            vb(tok, width),
            vb(tok, width),
            vb(tok, width),
            vb(tok, hid),
            vb(tok, hid),
            vb(tok, hid),
            vb(hid, tok),
            vb(hid, tok),
            vb(tok, hid),
            vb(tok, hid),
            vf(hid, seq),
            vf(heads, 1, tok),
            vb(tok, ff),
            vb(tok, ff),
            vb(tok, ff),
            vb(tok, 3 * hid),
            vf(tok, hid),
            vf(tok, hid),
            vb(2, seq, width),
            vb(2, seq, width),
            vb(seq, width),
            vb(seq, width),
            vf(seq, width),
            vf(seq, width),
            vf(seq, width),
            vf(seq, 128),
            vf(seq, width),
            vb(seq, width),
            vb(seq, width),
            vb(seq, width),
            vf(8, 2 * hid + ff),
            vb(width, ff),
            vb(width, ff),
            vb(width, 3 * hid),
            vb(width, hid),
            vb(nf - 1, part, ff),
            vb(nf - 1, part, ff),
            vb(nf - 1, part, 3 * hid),
            vb(nf - 1, part, hid),
            vb(2, rows_w, ff),
            vb(2, rows_w, ff),
            vb(2, rows_w, 3 * hid),
            vb(2, rows_w, hid),
            vb(2, rows_w, ff),
            vb(2, rows_w, ff),
            vb(2, rows_w, 3 * hid),
            vb(2, rows_w, hid),
            vf(8, 8, width),
            vf(8, width),
            vf(nt, 8, width),
            vf(nf, 8, width),
            vf(nc, 8, width),
            sem(3),
            sem(nt),
            sem(1),
            sem(4, 2 * nt),
            sem(4, 2 * nt),
            sem(4, nt),
            sem(4, nc),
            sem(4, nf),
            sem(4, nf),
            sem(4, 3, CHUNKS),
            sem(4, 3, CHUNKS),
            sem(4, 2),
            sem(4, 2),
            sem(4, CHUNKS),
            sem(4, CHUNKS),
            sem(1, nt),
            sem(1, nt),
            sem(4, nf, nc),
            sem(4, nf, nc),
            sem(4, nc),
            sem(4, nc),
            sem(4, 3),
            sem(4, 4),
            sem(CHUNKS, 2 * nt),
            sem(CHUNKS, 2 * nt),
            sem(3, max(nf, nc)),
            sem(3, max(nf, nc)),
        ],
        compiler_params=pltpu.CompilerParams(
            collective_id=0, has_side_effects=True, vmem_limit_bytes=63 << 20
        ),
    )(lengths, inputs, cotangent, w_query, w_key, w_value, w_out, w_up, w_down, bias, vec)
    return (
        result,
        grad_in.astype(F32),
        g_att[:, :hid],
        g_att[:, hid : 2 * hid],
        g_att[:, 2 * hid : 3 * hid],
        small[7, :hid],
        small[7, hid : 2 * hid],
        g_att[:, 3 * hid :],
        small[0],
        small[1],
        small[2],
        g_ffn[:, :ff],
        small[6, :ff],
        g_ffn[:, ff:],
        small[3],
        small[4],
        small[5],
    )


def solution(mesh):
    weight = P(("fsdp", "ctx"), "tp")
    acts = P("fsdp", "ctx", None)
    dims = tuple(mesh.shape[a] for a in ("fsdp", "ctx", "tp"))
    return jax.shard_map(
        functools.partial(shards, dims),
        mesh=mesh,
        in_specs=(
            acts,
            P("fsdp"),
            weight,
            weight,
            weight,
            P("tp"),
            P("tp"),
            weight,
            P(),
            P(),
            P(),
            weight,
            P("tp"),
            weight,
            P(),
            P(),
            P(),
            acts,
        ),
        out_specs=(
            acts,
            acts,
            weight,
            weight,
            weight,
            P("tp"),
            P("tp"),
            weight,
            P(),
            P(),
            P(),
            weight,
            P("tp"),
            weight,
            P(),
            P(),
            P(),
        ),
        check_vma=False,
    )
```

```python
import functools
import math

import jax
import jax.numpy as jnp
from jax import lax
from jax.experimental import pallas as pl
from jax.experimental.pallas import tpu as pltpu
from jax.sharding import PartitionSpec as P

DH = 64
MESH = pl.DeviceIdType.MESH
F32 = jnp.float32
BF16 = jnp.bfloat16
TILE = 256
ROWS = 16
CHUNKS = 2


def dot(left, right):
    return jnp.dot(left, right, preferred_element_type=F32)


def dot_last(left, right):
    return lax.dot_general(left, right, (((1,), (1,)), ((), ())), preferred_element_type=F32)


def dot_first(left, right):
    return lax.dot_general(left, right, (((0,), (0,)), ((), ())), preferred_element_type=F32)


def aligned(index, size):
    return pl.ds(pl.multiple_of(index * size, size), size)


def layer(
    dims,
    lens,
    x_h,
    ct_h,
    wq_h,
    wk_h,
    wv_h,
    wo_h,
    wu_h,
    wd_h,
    bq_h,
    bv_h,
    bu_h,
    b_out_r,
    gain1_r,
    shift1_r,
    b_down_r,
    gain2_r,
    shift2_r,
    res_h,
    gi_h,
    gq_o,
    gk_o,
    gv_o,
    go_o,
    gu_o,
    gd_o,
    small_o,
    wqkv,
    wo,
    wu,
    wd,
    z0,
    z1,
    z2,
    z3,
    x_tok,
    nl,
    dl2,
    dl1,
    qs,
    kk,
    vv,
    kt,
    vt,
    att,
    datt,
    ot,
    lse,
    act,
    dg,
    dpl,
    dqkv,
    dk_acc,
    dv_acc,
    ps,
    pr,
    ysend,
    yrecv,
    acc_y,
    acc_o,
    xh1,
    rstd1,
    dres,
    res_s,
    gi_s,
    ct_s,
    bias,
    gwd,
    gwu,
    gqkv,
    gwo,
    xg_d,
    xg_u,
    xg_q,
    xg_o,
    zf_d,
    zf_u,
    zf_q,
    zf_o,
    zp_d,
    zp_u,
    zp_q,
    zp_o,
    sums,
    sm,
    smz,
    smx,
    smc,
    loc_sem,
    bias_s,
    bias_r,
    wz_s,
    wz_r,
    wy_s,
    wy_r,
    wx_s,
    wx_r,
    ag_s,
    ag_r,
    rs_s,
    rs_r,
    ry_s,
    ry_r,
    out_s,
    out_r,
    gx_s,
    gx_r,
    gy_s,
    gy_r,
    gz_s,
    gz_r,
    line_s,
    line_r,
    sm_s,
    sm_r,
):
    nf, nc, nt = dims
    f = lax.axis_index("fsdp")
    c = lax.axis_index("ctx")
    t = lax.axis_index("tp")
    yi, ki = c // 2, lax.rem(c, 2)
    c_sib = yi * 2 + (1 - ki)
    c_y = (1 - yi) * 2 + ki
    c_ysib = (1 - yi) * 2 + (1 - ki)
    seq, width = ct_s.shape
    tok = x_tok.shape[0]
    rows_w = z0.shape[1]
    hid = wo.shape[1]
    ff = wu.shape[1]
    heads = hid // DH
    scale = 1.0 / math.sqrt(DH)
    chunk = seq // CHUNKS
    sib = (f, c_sib, t)
    ypeer = (f, c_y, t)
    length = lens[t]

    def remote(src, dst, ssem, rsem, dev):
        return pltpu.make_async_remote_copy(
            src_ref=src, dst_ref=dst, send_sem=ssem, recv_sem=rsem, device_id=dev, device_id_type=MESH
        )

    bar = pltpu.get_barrier_semaphore()
    for dc in range(nc):
        for dt in range(nt):
            if dc or dt:
                pl.semaphore_signal(
                    bar,
                    inc=1,
                    device_id=(f, lax.rem(c + dc, nc), lax.rem(t + dt, nt)),
                    device_id_type=MESH,
                )
    for df in range(1, nf):
        pl.semaphore_signal(bar, inc=1, device_id=(lax.rem(f + df, nf), c, t), device_id_type=MESH)
    pl.semaphore_wait(bar, nc * nt - 1 + nf - 1)

    groups = (
        ((wq_h, wk_h, wv_h), z0, wqkv),
        ((wo_h,), z1, wo),
        ((wu_h,), z2, wu),
        ((wd_h,), z3, wd),
    )

    def own_rows(cc):
        return aligned(f * nc + cc, rows_w)

    def hops(send, h):
        @pl.when((t >= h) & (t < nt - 1))
        def _():
            send(t - h, h + 1, t + 1)

        @pl.when((t + h < nt) & (t > 0))
        def _():
            send(t + h, nt + h, t - 1)

    def arrivals(take, h):
        @pl.when(t >= h)
        def _():
            take(t - h, h, t - 1)

        @pl.when(t + h < nt)
        def _():
            take(t + h, nt - 1 + h, t + 1)

    def w_line_copy(g, src, ts, n, to):
        return remote(
            src, groups[g][1].at[ts], wz_s.at[g, n], wz_r.at[g, n], (f, c, to)
        )

    def w_start(g):
        srcs, stage, _ = groups[g]
        for k, src in enumerate(srcs):
            dst = stage.at[t, :, pl.ds(k * src.shape[1], src.shape[1])]
            pltpu.make_async_copy(src, dst, wz_r.at[g, 0]).start()
            if g:
                hops(lambda ts, n, to: w_line_copy(g, src, ts, n, to).start(), 0)
            for j in range(1, 1 if g else nt):
                remote(src, dst, wz_s.at[g, j], wz_r.at[g, j], (f, c, lax.rem(t + j, nt))).start()

    def w_cross_block(g, ts):
        _, stage, final = groups[g]

        @pl.when(ts == c)
        def _():
            pltpu.make_async_copy(stage.at[ts], final.at[own_rows(c)], wy_r.at[g, c]).start()

        @pl.when(ts != c)
        def _():
            remote(
                stage.at[ts], final.at[own_rows(c)], wy_s.at[g, ts], wy_r.at[g, c], (f, ts, t)
            ).start()

    def w_cross(g, j):
        stage = groups[g][1]
        ts = lax.rem(t + nt - j, nt)
        if j == 0:
            pltpu.make_async_copy(stage.at[ts], stage.at[ts], wz_r.at[g, 0]).wait()
        else:
            remote(stage.at[ts], stage.at[ts], wz_s.at[g, j], wz_r.at[g, j], (f, c, ts)).wait_recv()
        w_cross_block(g, ts)

    def w_line(g, h):
        stage = groups[g][1]

        def take(ts, n, source):
            w_line_copy(g, stage.at[ts], ts, n, source).wait_recv()

        arrivals(take, h)
        if h < nt - 1:
            hops(lambda ts, n, to: w_line_copy(g, stage.at[ts], ts, n, to).start(), h)
        arrivals(lambda ts, n, source: w_cross_block(g, ts), h)

    def w_spread(g, i):
        _, _, final = groups[g]
        cc = lax.rem(c + i, nc)
        part = final.at[own_rows(cc)]
        if i == 0:
            pltpu.make_async_copy(part, part, wy_r.at[g, cc]).wait()
        else:
            remote(part, part, wy_s.at[g, 0], wy_r.at[g, cc], (f, cc, t)).wait_recv()
        for df in range(1, nf):
            remote(
                part, part, wx_s.at[g, df], wx_r.at[g, df], (lax.rem(f + df, nf), c, t)
            ).start()

    def w_wait(g):
        _, _, final = groups[g]
        for df in range(1, nf):
            fs = lax.rem(f + nf - df, nf)
            part = final.at[aligned(fs, nc * rows_w)]
            remote(part, part, wx_s.at[g, df], wx_r.at[g, df], (fs, c, t)).wait_recv()

    def w_finish(g):
        _, stage, final = groups[g]
        if g:
            for h in range(nt - 1):
                hops(lambda ts, n, to: w_line_copy(g, stage.at[ts], ts, n, to).wait_send(), h)
        for j in range(1, 1 if g else nt):
            remote(
                stage.at[0], stage.at[0], wz_s.at[g, j], wz_r.at[g, j], (f, c, lax.rem(t + j, nt))
            ).wait_send()
        for j in range(nt):
            ts = lax.rem(t + nt - j, nt)

            @pl.when(ts != c)
            def _():
                remote(
                    stage.at[ts], final.at[own_rows(c)], wy_s.at[g, ts], wy_r.at[g, c], (f, ts, t)
                ).wait_send()

        for df in range(1, nf):
            part = final.at[aligned(f, nc * rows_w)]
            remote(
                part, part, wx_s.at[g, df], wx_r.at[g, df], (lax.rem(f + df, nf), c, t)
            ).wait_send()

    def part_of(buf, cc, k):
        return buf.at[pl.ds(pl.multiple_of(cc * seq + k * chunk, chunk), chunk)]

    def ag_copy(buf, a, k, cc, way, dev):
        part = part_of(buf, cc, k)
        return remote(part, part, ag_s.at[a, way, k], ag_r.at[a, way, k], dev)

    def ag_send(buf, a, k):
        ag_copy(buf, a, k, c, 1, ypeer).start()
        ag_copy(buf, a, k, c, 0, sib).start()

    def ag_pass(buf, a, k):
        ag_copy(buf, a, k, c_y, 1, ypeer).wait_recv()
        ag_copy(buf, a, k, c_y, 2, sib).start()

    def ag_wait(buf, a, k, way):
        ag_copy(buf, a, k, c_sib if way == 0 else c_ysib, way, sib).wait_recv()

    def ag_finish(buf, a):
        for k in range(CHUNKS):
            ag_copy(buf, a, k, c, 0, sib).wait_send()
            ag_copy(buf, a, k, c, 1, ypeer).wait_send()
            ag_copy(buf, a, k, c_y, 2, sib).wait_send()

    tiles = width // TILE

    def rs_copy(o, slot):
        return remote(ps.at[slot], pr.at[slot], rs_s.at[o, slot], rs_r.at[o, slot], sib)

    def ry_copy(o, k):
        rows = pl.ds(k * chunk, chunk)
        return remote(ysend.at[rows], yrecv.at[rows], ry_s.at[o, k], ry_r.at[o, k], ypeer)

    def rs_sib(o, slot, produce):
        if o:
            rs_copy(o - 1, slot).wait_send()

        def tile(n, _):
            ps[slot, :, aligned(n, TILE)] = produce(n).astype(BF16)
            return 0

        lax.fori_loop(0, tiles, tile, 0)
        rs_copy(o, slot).start()

    def rs_y(o, produce):
        def tile(n, _):
            acc_y[:, aligned(n, TILE)] = produce(n)
            return 0

        lax.fori_loop(0, tiles, tile, 0)
        rs_copy(o, 0).wait_recv()
        for k in range(CHUNKS):
            if o:
                ry_copy(o - 1, k).wait_send()

            def add(i, _, k=k):
                rows = pl.ds(pl.multiple_of(k * chunk + i * ROWS, ROWS), ROWS)
                ysend[rows] = (acc_y[rows] + pr[0, rows].astype(F32)).astype(BF16)
                return 0

            lax.fori_loop(0, chunk // ROWS, add, 0)
            ry_copy(o, k).start()

    def rs_own(o, produce):
        def tile(n, _):
            acc_o[:, aligned(n, TILE)] = produce(n)
            return 0

        lax.fori_loop(0, tiles, tile, 0)

    def rs_row(rows):
        return acc_o[rows] + pr[1, rows].astype(F32) + yrecv[rows].astype(F32)

    def rs_rows(o, k, body):
        ry_copy(o, k).wait_recv()

        def step(i, _):
            body(pl.ds(pl.multiple_of(k * chunk + i * ROWS, ROWS), ROWS), i)
            return 0

        lax.fori_loop(0, chunk // ROWS, step, 0)

    def add_sum(k, value):
        half = value[0:8]
        for r in range(8, ROWS, 8):
            half = half + value[r : r + 8]
        sums[k] = sums[k] + half

    def mean(value):
        return jnp.sum(value, -1, keepdims=True) * (1.0 / width)

    w_start(0)
    pltpu.make_async_copy(x_h.at[t], x_tok.at[aligned(c, seq)], loc_sem.at[0]).start()
    pltpu.make_async_copy(ct_h.at[t], ct_s, loc_sem.at[1]).start()

    biases = (
        (bq_h, bias.at[:, pl.ds(0, hid)]),
        (bv_h, bias.at[:, pl.ds(hid, hid)]),
        (bu_h, bias.at[:, pl.ds(2 * hid, ff)]),
    )

    @pl.when(t == c)
    def _():
        for src, dst in biases:
            pltpu.make_async_copy(src, dst, loc_sem.at[2]).start()
            for j in range(1, nt):
                remote(src, dst, bias_s.at[j], bias_r.at[0], (f, c, lax.rem(t + j, nt))).start()

    pltpu.make_async_copy(x_h.at[t], x_tok.at[aligned(c, seq)], loc_sem.at[0]).wait()
    for k in range(CHUNKS):
        ag_send(x_tok, 0, k)
    w_start(1)
    w_start(2)
    w_cross(0, 0)
    w_cross(1, 0)
    sums[...] = jnp.zeros_like(sums)
    w_cross(0, 1)
    ag_pass(x_tok, 0, 0)
    w_cross(0, 2)
    for k in range(1, CHUNKS):
        ag_pass(x_tok, 0, k)
    w_cross(0, 3)
    w_cross(2, 0)
    w_line(1, 1)
    for i in range(nc):
        w_spread(0, i)
    w_start(3)
    w_line(1, 2)
    w_line(2, 1)
    w_cross(3, 0)
    w_line(1, 3)
    for i in range(nc):
        w_spread(1, i)

    @pl.when(t == c)
    def _():
        pltpu.make_async_copy(bias, bias, loc_sem.at[2]).wait()

    @pl.when(t != c)
    def _():
        remote(bias, bias, bias_s.at[0], bias_r.at[0], (f, c, c)).wait_recv()

    for k in range(CHUNKS):
        ag_wait(x_tok, 0, k, 0)
        ag_wait(x_tok, 0, k, 2)
    w_wait(0)
    w_line(3, 1)
    w_line(2, 2)

    def project(b, _):
        rows = aligned(b, seq)
        xb = x_tok[rows]
        qv = dot(xb, wqkv[:, 0:hid]) + bias[0:1, 0:hid]
        qs[rows] = (qv * scale).astype(BF16)
        kb = dot(xb, wqkv[:, hid : 2 * hid])
        kk[rows] = kb.astype(BF16)
        kt[:, rows] = kb.T.astype(BF16)
        vb = dot(xb, wqkv[:, 2 * hid : 3 * hid]) + bias[0:1, hid : 2 * hid]
        vv[rows] = vb.astype(BF16)
        vt[:, rows] = vb.T.astype(BF16)
        return 0

    lax.fori_loop(0, nc, project, 0)

    lane = lax.broadcasted_iota(jnp.int32, (seq, hid), 1)

    def head_part(value, h):
        inside = (lane >= h * DH) & (lane < (h + 1) * DH)
        return jnp.where(inside, value, jnp.zeros_like(value))

    def masked_scores(qm):
        s = dot_last(kk[...], qm)
        key = lax.broadcasted_iota(jnp.int32, s.shape, 0)
        return jnp.where(key < length, s, -1e30)

    def attend(b):
        rows = aligned(b, seq)
        qb = qs[rows]

        def head(h, _):
            s = masked_scores(head_part(qb, h))
            top = jnp.max(s, 0, keepdims=True)
            e = jnp.exp(s - top)
            total = jnp.sum(e, 0, keepdims=True)
            hrows = aligned(h, DH)
            ot[hrows] = dot(vt[hrows], e.astype(BF16)) / total
            lse[h, :, rows] = top + jnp.log(total)
            return 0

        lax.fori_loop(0, heads, head, 0)
        att[rows] = ot[...].T.astype(BF16)

    def out_proj(b):
        ab = att[aligned(b, seq)]
        return lambda n: dot_last(ab, wo[aligned(n, TILE)])

    attend(c_ysib)
    w_line(3, 2)
    w_line(2, 3)
    attend(c_y)
    for i in range(nc):
        w_spread(2, i)
    w_wait(1)
    rs_sib(0, 0, out_proj(c_ysib))
    w_line(3, 3)
    rs_y(0, out_proj(c_y))
    for i in range(nc):
        w_spread(3, i)
    attend(c_sib)
    rs_sib(0, 1, out_proj(c_sib))
    attend(c)
    rs_own(0, out_proj(c))
    rs_copy(0, 1).wait_recv()

    b_out, gain1, shift1 = b_out_r[...], gain1_r[...], shift1_r[...]
    b_down, gain2, shift2 = b_down_r[...], gain2_r[...], shift2_r[...]
    own = c * seq

    def own_slice(rows):
        return pl.ds(pl.multiple_of(own + rows.start, ROWS), ROWS)

    def norm1(rows, i):
        h = x_tok[own_slice(rows)].astype(F32) + rs_row(rows) + b_out
        cen = h - mean(h)
        inv = lax.rsqrt(mean(cen * cen) + 1e-5)
        xh = cen * inv
        xh1[rows] = xh
        rstd1[rows] = jnp.broadcast_to(inv, (ROWS, 128))
        nl[own_slice(rows)] = (xh * gain1 + shift1).astype(BF16)

    for k in range(CHUNKS):
        rs_rows(0, k, norm1)
        ag_send(nl, 1, k)
    w_wait(2)

    def up(b):
        rows = aligned(b, seq)
        nb = nl[rows]

        def tile(n, _):
            cols = aligned(n, TILE)
            v = dot(nb, wu[:, cols]) + bias[0:1, pl.ds(pl.multiple_of(2 * hid + n * TILE, 128), TILE)]
            cdf = 0.5 * (1.0 + lax.erf(v * math.sqrt(0.5)))
            act[rows, cols] = (v * cdf).astype(BF16)
            pdf = jnp.exp(-0.5 * v * v) * (1.0 / math.sqrt(2.0 * math.pi))
            dg[rows, cols] = (cdf + v * pdf).astype(BF16)
            return 0

        lax.fori_loop(0, ff // TILE, tile, 0)

    def down(b):
        ab = act[aligned(b, seq)]
        return lambda n: dot_last(ab, wd[aligned(n, TILE)])

    up(c)
    for k in range(CHUNKS):
        ag_wait(nl, 1, k, 0)
    up(c_sib)
    for k in range(CHUNKS):
        ag_pass(nl, 1, k)
    w_wait(3)
    rs_sib(1, 1, down(c_sib))
    rs_own(1, down(c))
    up(c_y)
    for k in range(CHUNKS):
        ag_wait(nl, 1, k, 2)
    up(c_ysib)
    rs_sib(1, 0, down(c_ysib))
    rs_y(1, down(c_y))
    rs_copy(1, 1).wait_recv()
    for g in range(4):
        w_finish(g)
    pltpu.make_async_copy(ct_h.at[t], ct_s, loc_sem.at[1]).wait()

    def norm2(rows, i):
        h = xh1[rows] * gain1 + shift1 + rs_row(rows) + b_down
        cen = h - mean(h)
        inv = lax.rsqrt(mean(cen * cen) + 1e-5)
        xh = cen * inv
        res_s[rows] = (xh * gain2 + shift2).astype(BF16)
        pos = own + rows.start + lax.broadcasted_iota(jnp.int32, (ROWS, width), 0)
        top = jnp.where(pos < length, ct_s[rows].astype(F32), 0.0)
        add_sum(4, top * xh)
        add_sum(5, top)
        gy = top * gain2
        dr = (gy - mean(gy) - xh * mean(gy * xh)) * inv
        add_sum(3, dr)
        dres[rows] = dr
        dl2[own_slice(rows)] = dr.astype(BF16)

    for k in range(CHUNKS):
        rs_rows(1, k, norm2)
        ag_send(dl2, 2, k)

    def spread(share, out, o):
        pltpu.make_async_copy(share, out.at[t], out_r.at[o, 0]).start()
        for j in range(1, nt):
            remote(
                share, out.at[t], out_s.at[o, j], out_r.at[o, j], (f, c, lax.rem(t + j, nt))
            ).start()

    def spread_wait(share, out, o):
        pltpu.make_async_copy(share, out.at[t], out_r.at[o, 0]).wait()
        for j in range(1, nt):
            ts = lax.rem(t + nt - j, nt)
            remote(share, out.at[ts], out_s.at[o, j], out_r.at[o, j], (f, c, ts)).wait_recv()
            remote(
                share, out.at[t], out_s.at[o, j], out_r.at[o, j], (f, c, lax.rem(t + j, nt))
            ).wait_send()

    spread(res_s, res_h, 0)

    def back(b):
        rows = aligned(b, seq)
        db = dl2[rows]

        def tile(n, _):
            cols = aligned(n, TILE)
            dp = (dot(db, wd[:, cols]) * dg[rows, cols].astype(F32)).astype(BF16)
            dpl[rows, cols] = dp
            dpf = dp.astype(F32)
            sums[6, :, cols] = sums[6, :, cols] + jnp.sum(dpf.reshape(seq // 8, 8, TILE), 0)
            return 0

        lax.fori_loop(0, ff // TILE, tile, 0)

    def up_back(b):
        pb = dpl[aligned(b, seq)]
        return lambda n: dot_last(pb, wu[aligned(n, TILE)])

    grads = (
        (gwd, xg_d, z3, zf_d, zp_d),
        (gwu, xg_u, z2, zf_u, zp_u),
        (gwo, xg_o, z1, zf_o, zp_o),
        (gqkv, xg_q, z0, zf_q, zp_q),
    )
    pair = t + 1 - 2 * lax.rem(t, 2)
    inner = (t == 1) | (t == nt - 2)
    far_in = jnp.where(t < 2, 2, 1)
    far_out = jnp.where(t < 2, nt - 1, 0)

    def gx_copy(g, df, i, dev_f):
        buf, got = grads[g][:2]
        cc = lax.rem(c + i, nc)
        return remote(
            buf.at[aligned(dev_f * nc + cc, rows_w)],
            got.at[df - 1, aligned(cc, rows_w)],
            gx_s.at[g, df, i],
            gx_r.at[g, df, i],
            (dev_f, c, t),
        )

    order = tuple(range(1, nc)) + (0,)

    part_rows = nc * rows_w
    def weight_grad(g, left, right):
        dst = grads[g][0]

        def rows_from(first, count):
            def step(m, _):
                rows = pl.ds(pl.multiple_of(first + m * TILE, TILE), TILE)
                dst[rows] = dot_first(left[:, rows], right[...]).astype(BF16)
                return 0

            lax.fori_loop(0, count // TILE, step, 0)

        split = part_rows % TILE == 0
        if not split:
            rows_from(0, width)
        for df in tuple(range(1, nf)) + (0,):
            to = lax.rem(f + df, nf)
            if split:
                rows_from(to * part_rows, part_rows)
            if df:
                for i in order:
                    gx_copy(g, df, i, to).start()

    def gy_copy(g, i, slot, cc):
        buf, _, got = grads[g][:3]
        return remote(
            buf.at[own_rows(cc)], got.at[slot], gy_s.at[g, i], gy_r.at[g, i], (f, cc, t)
        )

    def g_cross(g, i):
        buf, got, held = grads[g][:3]
        cc = lax.rem(c + i, nc)
        for df in range(1, nf):
            gx_copy(g, df, i, lax.rem(f + nf - df, nf)).wait_recv()

        def add(n, _):
            rows = pl.ds(pl.multiple_of((f * nc + cc) * rows_w + n * ROWS, ROWS), ROWS)
            total = buf[rows].astype(F32)
            for df in range(1, nf):
                theirs = pl.ds(pl.multiple_of(cc * rows_w + n * ROWS, ROWS), ROWS)
                total = total + got[df - 1, theirs].astype(F32)
            if i:
                buf[rows] = total.astype(BF16)
            else:
                held[c, pl.ds(pl.multiple_of(n * ROWS, ROWS), ROWS)] = total.astype(BF16)
            return 0

        lax.fori_loop(0, rows_w // ROWS, add, 0)
        if i:
            gy_copy(g, i, c, cc).start()

    def gz_copy(g, n, src, dst, to):
        return remote(src, dst, gz_s.at[g, n], gz_r.at[g, n], (f, c, to))

    def g_line(g):
        _, _, held, final, part = grads[g]
        for i in range(1, nc):
            cs = lax.rem(c + nc - i, nc)
            gy_copy(g, i, cs, cs).wait_recv()

        @pl.when(jnp.logical_not(inner))
        def _():
            gz_copy(g, 2, held.at[far_out], part.at[1], pair).start()
            gz_copy(g, 1, held.at[far_in], part.at[0], pair).start()

        gz_copy(g, 0, held.at[pair], final.at[0], pair).start()

    def g_relay(g):
        _, _, held, final, part = grads[g]

        @pl.when(inner)
        def _():
            for n, (to, slot) in enumerate(((far_out, 1), (far_in, 0))):
                gz_copy(g, 1 + slot, held.at[to], part.at[slot], pair).wait_recv()

                def add(m, _):
                    rows = pl.ds(pl.multiple_of(m * ROWS, ROWS), ROWS)
                    held[to, rows] = (
                        held[to, rows].astype(F32) + part[slot, rows].astype(F32)
                    ).astype(BF16)
                    return 0

                lax.fori_loop(0, rows_w // ROWS, add, 0)
                remote(
                    held.at[to], final.at[1], gz_s.at[g, 1 + slot], gz_r.at[g, 3], (f, c, to)
                ).start()

    def g_out(g, store):
        _, _, held, final, _ = grads[g]
        gz_copy(g, 0, held.at[t], final.at[0], pair).wait_recv()
        gz_copy(g, 3, held.at[t], final.at[1], far_in).wait_recv()

        def add(m, _):
            rows = pl.ds(pl.multiple_of(m * ROWS, ROWS), ROWS)
            store(
                rows,
                held[t, rows].astype(F32)
                + final[0, rows].astype(F32)
                + final[1, rows].astype(F32),
            )
            return 0

        lax.fori_loop(0, rows_w // ROWS, add, 0)

    def g_finish(g):
        _, _, held, final, part = grads[g]
        for i in order:
            for df in range(1, nf):
                gx_copy(g, df, i, lax.rem(f + df, nf)).wait_send()
        for i in range(1, nc):
            gy_copy(g, i, c, lax.rem(c + i, nc)).wait_send()
        for n in range(3):
            gz_copy(g, n, held.at[0], final.at[0], pair).wait_send()

    back(c)
    for k in range(CHUNKS):
        ag_wait(dl2, 2, k, 0)
    back(c_sib)
    rs_sib(2, 1, up_back(c_sib))
    rs_own(2, up_back(c))
    for k in range(CHUNKS):
        ag_pass(dl2, 2, k)
    back(c_y)
    for k in range(CHUNKS):
        ag_wait(dl2, 2, k, 2)
    back(c_ysib)
    rs_sib(2, 0, up_back(c_ysib))
    rs_y(2, up_back(c_y))
    weight_grad(0, dl2, act)
    weight_grad(1, nl, dpl)
    rs_copy(2, 1).wait_recv()

    def norm1_back(rows, i):
        dn = dres[rows] + rs_row(rows)
        xh = xh1[rows]
        add_sum(1, dn * xh)
        add_sum(2, dn)
        gy = dn * gain1
        dr = (gy - mean(gy) - xh * mean(gy * xh)) * rstd1[rows, 0:1]
        add_sum(0, dr)
        dres[rows] = dr
        dl1[own_slice(rows)] = dr.astype(BF16)

    for k in range(CHUNKS):
        rs_rows(2, k, norm1_back)
        ag_send(dl1, 3, k)

    dk_acc[...] = jnp.zeros_like(dk_acc)
    dv_acc[...] = jnp.zeros_like(dv_acc)

    def attend_back(b):
        rows = aligned(b, seq)
        datt[rows] = dot(dl1[rows], wo[...]).astype(BF16)
        qb = qs[rows]
        db = datt[rows]

        def head(h, _):
            qm = head_part(qb, h)
            dm = head_part(db, h)
            p = jnp.exp(masked_scores(qm) - lse[h, :, rows])
            dv_acc[...] += dot(p.astype(BF16), dm)
            pd = p * dot_last(vv[...], dm)
            delta = jnp.sum(pd, 0, keepdims=True)
            ds = (pd - p * delta).astype(BF16)
            dk_acc[...] += dot(ds, qm)
            hrows = aligned(h, DH)
            ot[hrows] = dot(kt[hrows], ds)
            return 0

        lax.fori_loop(0, heads, head, 0)
        dq = (ot[...].T * scale).astype(BF16)
        dqkv[rows, 0:hid] = dq
        dqf = dq.astype(F32)
        sums[7, :, 0:hid] = sums[7, :, 0:hid] + jnp.sum(dqf.reshape(seq // 8, 8, hid), 0)

    attend_back(c)
    g_cross(0, 1)
    g_cross(0, 2)
    for k in range(CHUNKS):
        ag_wait(dl1, 3, k, 0)
    attend_back(c_sib)
    for k in range(CHUNKS):
        ag_pass(dl1, 3, k)
    g_cross(0, 3)
    g_cross(0, 0)
    attend_back(c_y)
    g_line(0)
    for k in range(CHUNKS):
        ag_wait(dl1, 3, k, 2)
    weight_grad(2, dl1, att)
    g_cross(1, 1)
    g_cross(1, 2)
    attend_back(c_ysib)
    g_relay(0)

    def finish_kv(b, _):
        rows = aligned(b, seq)
        dqkv[rows, hid : 2 * hid] = dk_acc[rows].astype(BF16)
        dvb = dv_acc[rows].astype(BF16)
        dqkv[rows, 2 * hid : 3 * hid] = dvb
        sums[7, :, hid : 2 * hid] = sums[7, :, hid : 2 * hid] + jnp.sum(
            dvb.astype(F32).reshape(seq // 8, 8, hid), 0
        )
        return 0

    lax.fori_loop(0, nc, finish_kv, 0)

    def in_back(b):
        qb = dqkv[aligned(b, seq)]
        return lambda n: dot_last(qb, wqkv[aligned(n, TILE)])

    rs_sib(3, 0, in_back(c_ysib))
    rs_y(3, in_back(c_y))
    rs_sib(3, 1, in_back(c_sib))
    rs_own(3, in_back(c))
    weight_grad(3, x_tok, dqkv)
    g_cross(1, 3)
    g_cross(1, 0)
    g_line(1)
    sm[...] = jnp.sum(sums[...], 1)

    def sm_copy(stage, j, src, dst, dev):
        return remote(src, dst, sm_s.at[stage, j], sm_r.at[stage, j], dev)

    for j in range(1, nt):
        sm_copy(0, j, sm, smz.at[j], (f, c, lax.rem(t + j, nt))).start()
    for i in order:
        g_cross(2, i)
    g_relay(1)
    rs_copy(3, 1).wait_recv()

    def grad_in(rows, i):
        gi_s[rows] = (dres[rows] + rs_row(rows)).astype(BF16)

    def line_copy(k, src, ts, n, to):
        rows = pl.ds(k * chunk, chunk)
        return remote(
            src.at[rows], gi_h.at[ts, rows], line_s.at[k, n], line_r.at[k, n], (f, c, to)
        )

    for k in range(CHUNKS):
        rs_rows(3, k, grad_in)
        rows = pl.ds(k * chunk, chunk)
        pltpu.make_async_copy(gi_s.at[rows], gi_h.at[t, rows], line_r.at[k, 0]).start()
        hops(lambda ts, n, to: line_copy(k, gi_s, ts, n, to).start(), 0)
    g_line(2)

    def line_hop(k, h):
        arrivals(lambda ts, n, source: line_copy(k, gi_h.at[ts], ts, n, source).wait_recv(), h)
        if h < nt - 1:
            hops(lambda ts, n, to: line_copy(k, gi_h.at[ts], ts, n, to).start(), h)

    for i in order[:2]:
        g_cross(3, i)
    for k in range(CHUNKS):
        line_hop(k, 1)
    for i in order[2:]:
        g_cross(3, i)
    g_line(3)
    g_relay(2)
    total = sm[...]
    for j in range(1, nt):
        sm_copy(0, j, sm, smz.at[j], (f, c, lax.rem(t + nt - j, nt))).wait_recv()
        total = total + smz[j]
    smz[0] = total
    for df in range(1, nf):
        sm_copy(1, df, smz.at[0], smx.at[df], (lax.rem(f + df, nf), c, t)).start()
    for k in range(CHUNKS):
        line_hop(k, 2)
    for df in range(1, nf):
        sm_copy(1, df, smz.at[0], smx.at[df], (lax.rem(f + nf - df, nf), c, t)).wait_recv()
        total = total + smx[df]
    smx[0] = total
    for dc in range(1, nc):
        sm_copy(2, dc, smx.at[0], smc.at[c], (f, lax.rem(c + dc, nc), t)).start()
    smc[c] = total
    g_relay(3)

    def store_in(*outs):
        def store(rows, value):
            for k, out in enumerate(outs):
                out[rows] = value[:, k * out.shape[1] : (k + 1) * out.shape[1]]

        return store

    g_out(0, store_in(gd_o))
    g_out(1, store_in(gu_o))
    g_out(2, store_in(go_o))
    for dc in range(1, nc):
        cs = lax.rem(c + nc - dc, nc)
        sm_copy(2, dc, smx.at[0], smc.at[cs], (f, cs, t)).wait_recv()
    whole = smc[0]
    for s in range(1, nc):
        whole = whole + smc[s]
    small_o[0:6] = whole[0:6]
    small_o[6:8] = smc[t, 6:8]
    g_out(3, store_in(gq_o, gk_o, gv_o))
    spread_wait(res_s, res_h, 0)
    for k in range(CHUNKS):
        line_hop(k, 3)
        rows = pl.ds(k * chunk, chunk)
        pltpu.make_async_copy(gi_s.at[rows], gi_h.at[t, rows], line_r.at[k, 0]).wait()
        for h in range(nt - 1):
            hops(lambda ts, n, to: line_copy(k, gi_h.at[ts], ts, n, to).wait_send(), h)

    for g in range(4):
        g_finish(g)
    for a, buf in enumerate((x_tok, nl, dl2, dl1)):
        ag_finish(buf, a)
    rs_copy(3, 0).wait_send()
    rs_copy(3, 1).wait_send()
    for k in range(CHUNKS):
        ry_copy(3, k).wait_send()
    for j in range(1, nt):
        sm_copy(0, j, sm, smz.at[j], (f, c, lax.rem(t + j, nt))).wait_send()
    for df in range(1, nf):
        sm_copy(1, df, smz.at[0], smx.at[df], (lax.rem(f + df, nf), c, t)).wait_send()
    for dc in range(1, nc):
        sm_copy(2, dc, smx.at[0], smc.at[c], (f, lax.rem(c + dc, nc), t)).wait_send()

    @pl.when(t == c)
    def _():
        for j in range(1, nt):
            remote(
                bias, bias, bias_s.at[j], bias_r.at[0], (f, c, lax.rem(t + j, nt))
            ).wait_send()


def hand_over(small_rows, *refs):
    whole, small = refs[:8], refs[8]
    outs, small_o = refs[9:17], refs[17:26]

    @pl.when(pl.program_id(0) == 0)
    def _():
        for out, (row, start, size) in zip(small_o, small_rows):
            out[...] = small[row : row + 1, start : start + size]

    for out, value in zip(outs, whole):
        out[...] = value[...].astype(out.dtype)


def shards(
    dims,
    inputs,
    lengths,
    w_query,
    w_key,
    w_value,
    b_query,
    b_value,
    w_out,
    b_out,
    gain_attn,
    shift_attn,
    w_up,
    b_up,
    w_down,
    b_down,
    gain_ffn,
    shift_ffn,
    cotangent,
):
    nf, nc, nt = dims
    seq_dev, seq, width = inputs.shape
    rows_w, hid = w_query.shape
    ff = w_up.shape[1]
    assert nc == 4 and nt == nc and seq_dev == nt and ff == width
    tok = seq * nc
    heads = hid // DH
    part = nc * rows_w
    rows = [
        v.reshape(1, -1)
        for v in (
            b_query,
            b_value,
            b_up,
            b_out,
            gain_attn,
            shift_attn,
            b_down,
            gain_ffn,
            shift_ffn,
        )
    ]
    hbm = pl.BlockSpec(memory_space=pl.ANY)
    vmem = pl.BlockSpec(memory_space=pltpu.VMEM)
    smem = pl.BlockSpec(memory_space=pltpu.SMEM)

    def vb(*shape):
        return pltpu.VMEM(shape, BF16)

    def vf(*shape):
        return pltpu.VMEM(shape, F32)

    def sem(*shape):
        return pltpu.SemaphoreType.DMA(shape)

    result, grad_in, g_q, g_k, g_v, g_o, g_u, g_d, small = pl.pallas_call(
        functools.partial(layer, dims),
        out_shape=(
            jax.ShapeDtypeStruct((nt, seq, width), BF16),
            jax.ShapeDtypeStruct((nt, seq, width), BF16),
            *[jax.ShapeDtypeStruct((rows_w, hid), F32)] * 4,
            *[jax.ShapeDtypeStruct((rows_w, ff), F32)] * 2,
            jax.ShapeDtypeStruct((8, width), F32),
        ),
        in_specs=[smem] + [hbm] * 11 + [vmem] * 6,
        out_specs=(hbm, hbm) + (vmem,) * 7,
        scratch_shapes=[
            vb(width, 3 * hid),
            vb(width, hid),
            vb(width, ff),
            vb(width, ff),
            vb(nt, rows_w, 3 * hid),
            vb(nt, rows_w, hid),
            vb(nt, rows_w, ff),
            vb(nt, rows_w, ff),
            vb(tok, width),
            vb(tok, width),
            vb(tok, width),
            vb(tok, width),
            vb(tok, hid),
            vb(tok, hid),
            vb(tok, hid),
            vb(hid, tok),
            vb(hid, tok),
            vb(tok, hid),
            vb(tok, hid),
            vf(hid, seq),
            vf(heads, 1, tok),
            vb(tok, ff),
            vb(tok, ff),
            vb(tok, ff),
            vb(tok, 3 * hid),
            vf(tok, hid),
            vf(tok, hid),
            vb(2, seq, width),
            vb(2, seq, width),
            vb(seq, width),
            vb(seq, width),
            vf(seq, width),
            vf(seq, width),
            vf(seq, width),
            vf(seq, 128),
            vf(seq, width),
            vb(seq, width),
            vb(seq, width),
            vb(seq, width),
            vf(1, 2 * hid + ff),
            vb(width, ff),
            vb(width, ff),
            vb(width, 3 * hid),
            vb(width, hid),
            vb(nf - 1, part, ff),
            vb(nf - 1, part, ff),
            vb(nf - 1, part, 3 * hid),
            vb(nf - 1, part, hid),
            vb(2, rows_w, ff),
            vb(2, rows_w, ff),
            vb(2, rows_w, 3 * hid),
            vb(2, rows_w, hid),
            vb(2, rows_w, ff),
            vb(2, rows_w, ff),
            vb(2, rows_w, 3 * hid),
            vb(2, rows_w, hid),
            vf(8, 8, width),
            vf(8, width),
            vf(nt, 8, width),
            vf(nf, 8, width),
            vf(nc, 8, width),
            sem(3),
            sem(nt),
            sem(1),
            sem(4, 2 * nt),
            sem(4, 2 * nt),
            sem(4, nt),
            sem(4, nc),
            sem(4, nf),
            sem(4, nf),
            sem(4, 3, CHUNKS),
            sem(4, 3, CHUNKS),
            sem(4, 2),
            sem(4, 2),
            sem(4, CHUNKS),
            sem(4, CHUNKS),
            sem(1, nt),
            sem(1, nt),
            sem(4, nf, nc),
            sem(4, nf, nc),
            sem(4, nc),
            sem(4, nc),
            sem(4, 3),
            sem(4, 4),
            sem(CHUNKS, 2 * nt),
            sem(CHUNKS, 2 * nt),
            sem(3, max(nf, nc)),
            sem(3, max(nf, nc)),
        ],
        compiler_params=pltpu.CompilerParams(
            collective_id=0, has_side_effects=True, vmem_limit_bytes=63 << 20
        ),
    )(lengths, inputs, cotangent, w_query, w_key, w_value, w_out, w_up, w_down, *rows)
    small_rows = ((7, 0, hid), (7, hid, hid), (0, 0, width), (1, 0, width), (2, 0, width))
    small_rows += ((6, 0, ff), (3, 0, width), (4, 0, width), (5, 0, width))
    whole = (result, g_q, g_k, g_v, g_o, g_u, g_d, grad_in)
    step = rows_w // nt if rows_w % (8 * nt) == 0 else rows_w

    def block(a):
        if a.ndim == 3:
            return pl.BlockSpec((1, seq, width), lambda i: (i, 0, 0))
        return pl.BlockSpec((step, a.shape[1]), lambda i: (i if step < rows_w else 0, 0))

    outs = pl.pallas_call(
        functools.partial(hand_over, small_rows),
        grid=(nt,),
        out_shape=tuple(jax.ShapeDtypeStruct(a.shape, a.dtype) for a in whole[:7])
        + (jax.ShapeDtypeStruct(grad_in.shape, F32),)
        + tuple(jax.ShapeDtypeStruct((1, n), F32) for _, _, n in small_rows),
        in_specs=[block(a) for a in whole] + [vmem],
        out_specs=tuple(block(a) for a in whole) + (vmem,) * 9,
    )(*whole, small)
    result, g_q, g_k, g_v, g_o, g_u, g_d, grad_in = outs[:8]
    s_bq, s_bv, s_bo, s_ga, s_sa, s_bu, s_bd, s_gf, s_sf = (a.reshape(-1) for a in outs[8:])
    return (
        result,
        grad_in,
        g_q,
        g_k,
        g_v,
        s_bq,
        s_bv,
        g_o,
        s_bo,
        s_ga,
        s_sa,
        g_u,
        s_bu,
        g_d,
        s_bd,
        s_gf,
        s_sf,
    )


def solution(mesh):
    weight = P(("fsdp", "ctx"), "tp")
    acts = P("fsdp", "ctx", None)
    dims = tuple(mesh.shape[a] for a in ("fsdp", "ctx", "tp"))
    return jax.shard_map(
        functools.partial(shards, dims),
        mesh=mesh,
        in_specs=(
            acts,
            P("fsdp"),
            weight,
            weight,
            weight,
            P("tp"),
            P("tp"),
            weight,
            P(),
            P(),
            P(),
            weight,
            P("tp"),
            weight,
            P(),
            P(),
            P(),
            acts,
        ),
        out_specs=(
            acts,
            acts,
            weight,
            weight,
            weight,
            P("tp"),
            P("tp"),
            weight,
            P(),
            P(),
            P(),
            weight,
            P("tp"),
            weight,
            P(),
            P(),
            P(),
        ),
        check_vma=False,
    )
```

```python
import functools
import math

import jax
import jax.numpy as jnp
from jax import lax
from jax.experimental import pallas as pl
from jax.experimental.pallas import tpu as pltpu
from jax.sharding import PartitionSpec as P

DH = 64
MESH = pl.DeviceIdType.MESH
F32 = jnp.float32
BF16 = jnp.bfloat16
TILE = 256
ROWS = 16
CHUNKS = 2


def dot(left, right):
    return jnp.dot(left, right, preferred_element_type=F32)


def dot_last(left, right):
    return lax.dot_general(left, right, (((1,), (1,)), ((), ())), preferred_element_type=F32)


def dot_first(left, right):
    return lax.dot_general(left, right, (((0,), (0,)), ((), ())), preferred_element_type=F32)


def aligned(index, size):
    return pl.ds(pl.multiple_of(index * size, size), size)


def layer(
    dims,
    lens,
    x_h,
    ct_h,
    wq_h,
    wk_h,
    wv_h,
    wo_h,
    wu_h,
    wd_h,
    bq_h,
    bv_h,
    bu_h,
    b_out_r,
    gain1_r,
    shift1_r,
    b_down_r,
    gain2_r,
    shift2_r,
    res_h,
    gi_h,
    gq_o,
    gk_o,
    gv_o,
    go_o,
    gu_o,
    gd_o,
    small_o,
    wqkv,
    wo,
    wu,
    wd,
    z0,
    z1,
    z2,
    z3,
    x_tok,
    nl,
    dl2,
    dl1,
    qs,
    kk,
    vv,
    kt,
    vt,
    att,
    datt,
    ot,
    lse,
    act,
    dg,
    dpl,
    dqkv,
    dk_acc,
    dv_acc,
    ps,
    pr,
    ysend,
    yrecv,
    acc_y,
    acc_o,
    xh1,
    rstd1,
    dres,
    res_s,
    gi_s,
    ct_s,
    bias,
    gwd,
    gwu,
    gqkv,
    gwo,
    xg_d,
    xg_u,
    xg_q,
    xg_o,
    zf_d,
    zf_u,
    zf_q,
    zf_o,
    zp_d,
    zp_u,
    zp_q,
    zp_o,
    sums,
    sm,
    smz,
    smx,
    smc,
    loc_sem,
    bias_s,
    bias_r,
    wz_s,
    wz_r,
    wy_s,
    wy_r,
    wx_s,
    wx_r,
    ag_s,
    ag_r,
    rs_s,
    rs_r,
    ry_s,
    ry_r,
    out_s,
    out_r,
    gx_s,
    gx_r,
    gy_s,
    gy_r,
    gz_s,
    gz_r,
    line_s,
    line_r,
    sm_s,
    sm_r,
):
    nf, nc, nt = dims
    f = lax.axis_index("fsdp")
    c = lax.axis_index("ctx")
    t = lax.axis_index("tp")
    yi, ki = c // 2, lax.rem(c, 2)
    c_sib = yi * 2 + (1 - ki)
    c_y = (1 - yi) * 2 + ki
    c_ysib = (1 - yi) * 2 + (1 - ki)
    seq, width = ct_s.shape
    tok = x_tok.shape[0]
    rows_w = z0.shape[1]
    hid = wo.shape[1]
    ff = wu.shape[1]
    heads = hid // DH
    scale = 1.0 / math.sqrt(DH)
    chunk = seq // CHUNKS
    sib = (f, c_sib, t)
    ypeer = (f, c_y, t)
    length = lens[t]

    def remote(src, dst, ssem, rsem, dev):
        return pltpu.make_async_remote_copy(
            src_ref=src, dst_ref=dst, send_sem=ssem, recv_sem=rsem, device_id=dev, device_id_type=MESH
        )

    bar = pltpu.get_barrier_semaphore()
    for dc in range(nc):
        for dt in range(nt):
            if dc or dt:
                pl.semaphore_signal(
                    bar,
                    inc=1,
                    device_id=(f, lax.rem(c + dc, nc), lax.rem(t + dt, nt)),
                    device_id_type=MESH,
                )
    for df in range(1, nf):
        pl.semaphore_signal(bar, inc=1, device_id=(lax.rem(f + df, nf), c, t), device_id_type=MESH)
    pl.semaphore_wait(bar, nc * nt - 1 + nf - 1)

    groups = (
        ((wq_h, wk_h, wv_h), z0, wqkv),
        ((wo_h,), z1, wo),
        ((wu_h,), z2, wu),
        ((wd_h,), z3, wd),
    )

    def own_rows(cc):
        return aligned(f * nc + cc, rows_w)

    def hops(send, h):
        @pl.when((t >= h) & (t < nt - 1))
        def _():
            send(t - h, h + 1, t + 1)

        @pl.when((t + h < nt) & (t > 0))
        def _():
            send(t + h, nt + h, t - 1)

    def arrivals(take, h):
        @pl.when(t >= h)
        def _():
            take(t - h, h, t - 1)

        @pl.when(t + h < nt)
        def _():
            take(t + h, nt - 1 + h, t + 1)

    def w_cross_at(g, h):
        pl.when(t >= h)(lambda: w_cross(g, h))
        pl.when(t + h < nt)(lambda: w_cross(g, nt - h))

    def w_line_copy(g, src, ts, n, to):
        return remote(
            src, groups[g][1].at[ts], wz_s.at[g, n], wz_r.at[g, n], (f, c, to)
        )

    def w_start(g):
        srcs, stage, _ = groups[g]
        for k, src in enumerate(srcs):
            dst = stage.at[t, :, pl.ds(k * src.shape[1], src.shape[1])]
            pltpu.make_async_copy(src, dst, wz_r.at[g, 0]).start()
            if g:
                hops(lambda ts, n, to: w_line_copy(g, src, ts, n, to).start(), 0)
            for j in range(1, 1 if g else nt):
                remote(src, dst, wz_s.at[g, j], wz_r.at[g, j], (f, c, lax.rem(t + j, nt))).start()

    def w_cross_block(g, ts):
        _, stage, final = groups[g]

        @pl.when(ts == c)
        def _():
            pltpu.make_async_copy(stage.at[ts], final.at[own_rows(c)], wy_r.at[g, c]).start()

        @pl.when(ts != c)
        def _():
            remote(
                stage.at[ts], final.at[own_rows(c)], wy_s.at[g, ts], wy_r.at[g, c], (f, ts, t)
            ).start()

    def w_cross(g, j):
        stage = groups[g][1]
        ts = lax.rem(t + nt - j, nt)
        if j == 0:
            pltpu.make_async_copy(stage.at[ts], stage.at[ts], wz_r.at[g, 0]).wait()
        else:
            remote(stage.at[ts], stage.at[ts], wz_s.at[g, j], wz_r.at[g, j], (f, c, ts)).wait_recv()
        w_cross_block(g, ts)

    def w_line(g, h):
        stage = groups[g][1]

        def take(ts, n, source):
            w_line_copy(g, stage.at[ts], ts, n, source).wait_recv()

        arrivals(take, h)
        if h < nt - 1:
            hops(lambda ts, n, to: w_line_copy(g, stage.at[ts], ts, n, to).start(), h)
        arrivals(lambda ts, n, source: w_cross_block(g, ts), h)

    def w_spread(g, i):
        _, _, final = groups[g]
        cc = lax.rem(c + i, nc)
        part = final.at[own_rows(cc)]
        if i == 0:
            pltpu.make_async_copy(part, part, wy_r.at[g, cc]).wait()
        else:
            remote(part, part, wy_s.at[g, 0], wy_r.at[g, cc], (f, cc, t)).wait_recv()
        for df in range(1, nf):
            remote(
                part, part, wx_s.at[g, df], wx_r.at[g, df], (lax.rem(f + df, nf), c, t)
            ).start()

    def w_spread_at(g, h):
        @pl.when((t - c == h) | (c - t == h))
        def _():
            for i in range(nc):
                w_spread(g, i)

    def w_wait(g):
        _, _, final = groups[g]
        for df in range(1, nf):
            fs = lax.rem(f + nf - df, nf)
            part = final.at[aligned(fs, nc * rows_w)]
            remote(part, part, wx_s.at[g, df], wx_r.at[g, df], (fs, c, t)).wait_recv()

    def w_finish(g):
        _, stage, final = groups[g]
        if g:
            for h in range(nt - 1):
                hops(lambda ts, n, to: w_line_copy(g, stage.at[ts], ts, n, to).wait_send(), h)
        for j in range(1, 1 if g else nt):
            remote(
                stage.at[0], stage.at[0], wz_s.at[g, j], wz_r.at[g, j], (f, c, lax.rem(t + j, nt))
            ).wait_send()
        for j in range(nt):
            ts = lax.rem(t + nt - j, nt)

            @pl.when(ts != c)
            def _():
                remote(
                    stage.at[ts], final.at[own_rows(c)], wy_s.at[g, ts], wy_r.at[g, c], (f, ts, t)
                ).wait_send()

        for df in range(1, nf):
            part = final.at[aligned(f, nc * rows_w)]
            remote(
                part, part, wx_s.at[g, df], wx_r.at[g, df], (lax.rem(f + df, nf), c, t)
            ).wait_send()

    def part_of(buf, cc, k):
        return buf.at[pl.ds(pl.multiple_of(cc * seq + k * chunk, chunk), chunk)]

    def ag_copy(buf, a, k, cc, way, dev):
        part = part_of(buf, cc, k)
        return remote(part, part, ag_s.at[a, way, k], ag_r.at[a, way, k], dev)

    def ag_send(buf, a, k):
        ag_copy(buf, a, k, c, 1, ypeer).start()
        ag_copy(buf, a, k, c, 0, sib).start()

    def ag_pass(buf, a, k):
        ag_copy(buf, a, k, c_y, 1, ypeer).wait_recv()
        ag_copy(buf, a, k, c_y, 2, sib).start()

    def ag_wait(buf, a, k, way):
        ag_copy(buf, a, k, c_sib if way == 0 else c_ysib, way, sib).wait_recv()

    def ag_finish(buf, a):
        for k in range(CHUNKS):
            ag_copy(buf, a, k, c, 0, sib).wait_send()
            ag_copy(buf, a, k, c, 1, ypeer).wait_send()
            ag_copy(buf, a, k, c_y, 2, sib).wait_send()

    tiles = width // TILE

    def rs_copy(o, slot):
        return remote(ps.at[slot], pr.at[slot], rs_s.at[o, slot], rs_r.at[o, slot], sib)

    def ry_copy(o, k):
        rows = pl.ds(k * chunk, chunk)
        return remote(ysend.at[rows], yrecv.at[rows], ry_s.at[o, k], ry_r.at[o, k], ypeer)

    def rs_sib(o, slot, produce):
        if o:
            rs_copy(o - 1, slot).wait_send()

        def tile(n, _):
            ps[slot, :, aligned(n, TILE)] = produce(n).astype(BF16)
            return 0

        lax.fori_loop(0, tiles, tile, 0)
        rs_copy(o, slot).start()

    def rs_y(o, produce):
        def tile(n, _):
            acc_y[:, aligned(n, TILE)] = produce(n)
            return 0

        lax.fori_loop(0, tiles, tile, 0)
        rs_copy(o, 0).wait_recv()
        for k in range(CHUNKS):
            if o:
                ry_copy(o - 1, k).wait_send()

            def add(i, _, k=k):
                rows = pl.ds(pl.multiple_of(k * chunk + i * ROWS, ROWS), ROWS)
                ysend[rows] = (acc_y[rows] + pr[0, rows].astype(F32)).astype(BF16)
                return 0

            lax.fori_loop(0, chunk // ROWS, add, 0)
            ry_copy(o, k).start()

    def rs_own(o, produce):
        def tile(n, _):
            acc_o[:, aligned(n, TILE)] = produce(n)
            return 0

        lax.fori_loop(0, tiles, tile, 0)

    def rs_row(rows):
        return acc_o[rows] + pr[1, rows].astype(F32) + yrecv[rows].astype(F32)

    def rs_rows(o, k, body):
        ry_copy(o, k).wait_recv()

        def step(i, _):
            body(pl.ds(pl.multiple_of(k * chunk + i * ROWS, ROWS), ROWS), i)
            return 0

        lax.fori_loop(0, chunk // ROWS, step, 0)

    def add_sum(k, value):
        half = value[0:8]
        for r in range(8, ROWS, 8):
            half = half + value[r : r + 8]
        sums[k] = sums[k] + half

    def mean(value):
        return jnp.sum(value, -1, keepdims=True) * (1.0 / width)

    w_start(0)
    pltpu.make_async_copy(x_h.at[t], x_tok.at[aligned(c, seq)], loc_sem.at[0]).start()
    pltpu.make_async_copy(ct_h.at[t], ct_s, loc_sem.at[1]).start()

    biases = (
        (bq_h, bias.at[:, pl.ds(0, hid)]),
        (bv_h, bias.at[:, pl.ds(hid, hid)]),
        (bu_h, bias.at[:, pl.ds(2 * hid, ff)]),
    )

    @pl.when(t == c)
    def _():
        for src, dst in biases:
            pltpu.make_async_copy(src, dst, loc_sem.at[2]).start()
            for j in range(1, nt):
                remote(src, dst, bias_s.at[j], bias_r.at[0], (f, c, lax.rem(t + j, nt))).start()

    pltpu.make_async_copy(x_h.at[t], x_tok.at[aligned(c, seq)], loc_sem.at[0]).wait()
    for k in range(CHUNKS):
        ag_send(x_tok, 0, k)
    w_start(1)
    w_start(2)
    w_cross(0, 0)
    w_cross(1, 0)
    sums[...] = jnp.zeros_like(sums)
    w_cross_at(0, 1)
    ag_pass(x_tok, 0, 0)
    w_spread_at(0, 0)
    w_cross_at(0, 2)
    for k in range(1, CHUNKS):
        ag_pass(x_tok, 0, k)
    w_spread_at(0, 1)
    w_cross_at(0, 3)
    w_spread_at(1, 0)
    w_cross(2, 0)
    w_line(1, 1)
    w_spread_at(0, 2)
    w_start(3)
    w_line(1, 2)
    w_spread_at(1, 1)
    w_line(2, 1)
    w_spread_at(0, 3)
    w_spread_at(2, 0)
    w_cross(3, 0)
    w_line(1, 3)
    w_spread_at(1, 2)

    @pl.when(t == c)
    def _():
        pltpu.make_async_copy(bias, bias, loc_sem.at[2]).wait()

    @pl.when(t != c)
    def _():
        remote(bias, bias, bias_s.at[0], bias_r.at[0], (f, c, c)).wait_recv()

    for k in range(CHUNKS):
        ag_wait(x_tok, 0, k, 0)
        ag_wait(x_tok, 0, k, 2)
    w_wait(0)
    w_line(3, 1)
    w_spread_at(1, 3)

    def project(b, _):
        rows = aligned(b, seq)
        xb = x_tok[rows]
        qv = dot(xb, wqkv[:, 0:hid]) + bias[0:1, 0:hid]
        qs[rows] = (qv * scale).astype(BF16)
        kb = dot(xb, wqkv[:, hid : 2 * hid])
        kk[rows] = kb.astype(BF16)
        kt[:, rows] = kb.T.astype(BF16)
        vb = dot(xb, wqkv[:, 2 * hid : 3 * hid]) + bias[0:1, hid : 2 * hid]
        vv[rows] = vb.astype(BF16)
        vt[:, rows] = vb.T.astype(BF16)
        return 0

    lax.fori_loop(0, nc, project, 0)

    lane = lax.broadcasted_iota(jnp.int32, (seq, hid), 1)

    def head_part(value, h):
        inside = (lane >= h * DH) & (lane < (h + 1) * DH)
        return jnp.where(inside, value, jnp.zeros_like(value))

    def masked_scores(qm):
        s = dot_last(kk[...], qm)
        key = lax.broadcasted_iota(jnp.int32, s.shape, 0)
        return jnp.where(key < length, s, -1e30)

    def attend(b):
        rows = aligned(b, seq)
        qb = qs[rows]

        def head(h, _):
            s = masked_scores(head_part(qb, h))
            top = jnp.max(s, 0, keepdims=True)
            e = jnp.exp(s - top)
            total = jnp.sum(e, 0, keepdims=True)
            hrows = aligned(h, DH)
            ot[hrows] = dot(vt[hrows], e.astype(BF16)) / total
            lse[h, :, rows] = top + jnp.log(total)
            return 0

        lax.fori_loop(0, heads, head, 0)
        att[rows] = ot[...].T.astype(BF16)

    def out_proj(b):
        ab = att[aligned(b, seq)]
        return lambda n: dot_last(ab, wo[aligned(n, TILE)])

    w_line(2, 2)
    w_spread_at(2, 1)
    w_spread_at(3, 0)
    attend(c_ysib)
    w_line(3, 2)
    w_spread_at(2, 2)
    w_spread_at(3, 1)
    attend(c_y)
    w_line(2, 3)
    w_wait(1)
    rs_sib(0, 0, out_proj(c_ysib))
    rs_y(0, out_proj(c_y))
    w_spread_at(2, 3)
    w_spread_at(3, 2)
    w_line(3, 3)
    attend(c_sib)
    rs_sib(0, 1, out_proj(c_sib))
    w_spread_at(3, 3)
    attend(c)
    rs_own(0, out_proj(c))
    rs_copy(0, 1).wait_recv()

    b_out, gain1, shift1 = b_out_r[...], gain1_r[...], shift1_r[...]
    b_down, gain2, shift2 = b_down_r[...], gain2_r[...], shift2_r[...]
    own = c * seq

    def own_slice(rows):
        return pl.ds(pl.multiple_of(own + rows.start, ROWS), ROWS)

    def norm1(rows, i):
        h = x_tok[own_slice(rows)].astype(F32) + rs_row(rows) + b_out
        cen = h - mean(h)
        inv = lax.rsqrt(mean(cen * cen) + 1e-5)
        xh = cen * inv
        xh1[rows] = xh
        rstd1[rows] = jnp.broadcast_to(inv, (ROWS, 128))
        nl[own_slice(rows)] = (xh * gain1 + shift1).astype(BF16)

    for k in range(CHUNKS):
        rs_rows(0, k, norm1)
        ag_send(nl, 1, k)
    w_wait(2)

    def up(b):
        rows = aligned(b, seq)
        nb = nl[rows]

        def tile(n, _):
            cols = aligned(n, TILE)
            v = dot(nb, wu[:, cols]) + bias[0:1, pl.ds(pl.multiple_of(2 * hid + n * TILE, 128), TILE)]
            cdf = 0.5 * (1.0 + lax.erf(v * math.sqrt(0.5)))
            act[rows, cols] = (v * cdf).astype(BF16)
            pdf = jnp.exp(-0.5 * v * v) * (1.0 / math.sqrt(2.0 * math.pi))
            dg[rows, cols] = (cdf + v * pdf).astype(BF16)
            return 0

        lax.fori_loop(0, ff // TILE, tile, 0)

    def down(b):
        ab = act[aligned(b, seq)]
        return lambda n: dot_last(ab, wd[aligned(n, TILE)])

    up(c)
    for k in range(CHUNKS):
        ag_wait(nl, 1, k, 0)
    up(c_sib)
    for k in range(CHUNKS):
        ag_pass(nl, 1, k)
    up(c_y)
    for k in range(CHUNKS):
        ag_wait(nl, 1, k, 2)
    up(c_ysib)
    w_wait(3)
    rs_sib(1, 0, down(c_ysib))
    rs_y(1, down(c_y))
    rs_sib(1, 1, down(c_sib))
    rs_own(1, down(c))
    rs_copy(1, 1).wait_recv()
    for g in range(4):
        w_finish(g)
    pltpu.make_async_copy(ct_h.at[t], ct_s, loc_sem.at[1]).wait()

    def norm2(rows, i):
        h = xh1[rows] * gain1 + shift1 + rs_row(rows) + b_down
        cen = h - mean(h)
        inv = lax.rsqrt(mean(cen * cen) + 1e-5)
        xh = cen * inv
        res_s[rows] = (xh * gain2 + shift2).astype(BF16)
        pos = own + rows.start + lax.broadcasted_iota(jnp.int32, (ROWS, width), 0)
        top = jnp.where(pos < length, ct_s[rows].astype(F32), 0.0)
        add_sum(4, top * xh)
        add_sum(5, top)
        gy = top * gain2
        dr = (gy - mean(gy) - xh * mean(gy * xh)) * inv
        add_sum(3, dr)
        dres[rows] = dr
        dl2[own_slice(rows)] = dr.astype(BF16)

    for k in range(CHUNKS):
        rs_rows(1, k, norm2)
        ag_send(dl2, 2, k)

    def spread(share, out, o):
        pltpu.make_async_copy(share, out.at[t], out_r.at[o, 0]).start()
        for j in range(1, nt):
            remote(
                share, out.at[t], out_s.at[o, j], out_r.at[o, j], (f, c, lax.rem(t + j, nt))
            ).start()

    def spread_wait(share, out, o):
        pltpu.make_async_copy(share, out.at[t], out_r.at[o, 0]).wait()
        for j in range(1, nt):
            ts = lax.rem(t + nt - j, nt)
            remote(share, out.at[ts], out_s.at[o, j], out_r.at[o, j], (f, c, ts)).wait_recv()
            remote(
                share, out.at[t], out_s.at[o, j], out_r.at[o, j], (f, c, lax.rem(t + j, nt))
            ).wait_send()

    spread(res_s, res_h, 0)

    def back(b):
        rows = aligned(b, seq)
        db = dl2[rows]

        def tile(n, _):
            cols = aligned(n, TILE)
            dp = (dot(db, wd[:, cols]) * dg[rows, cols].astype(F32)).astype(BF16)
            dpl[rows, cols] = dp
            dpf = dp.astype(F32)
            sums[6, :, cols] = sums[6, :, cols] + jnp.sum(dpf.reshape(seq // 8, 8, TILE), 0)
            return 0

        lax.fori_loop(0, ff // TILE, tile, 0)

    def up_back(b):
        pb = dpl[aligned(b, seq)]
        return lambda n: dot_last(pb, wu[aligned(n, TILE)])

    grads = (
        (gwd, xg_d, z3, zf_d, zp_d),
        (gwu, xg_u, z2, zf_u, zp_u),
        (gwo, xg_o, z1, zf_o, zp_o),
        (gqkv, xg_q, z0, zf_q, zp_q),
    )
    pair = t + 1 - 2 * lax.rem(t, 2)
    inner = (t == 1) | (t == nt - 2)
    far_in = jnp.where(t < 2, 2, 1)
    far_out = jnp.where(t < 2, nt - 1, 0)

    def gx_copy(g, df, i, dev_f):
        buf, got = grads[g][:2]
        cc = lax.rem(c + i, nc)
        return remote(
            buf.at[aligned(dev_f * nc + cc, rows_w)],
            got.at[df - 1, aligned(cc, rows_w)],
            gx_s.at[g, df, i],
            gx_r.at[g, df, i],
            (dev_f, c, t),
        )

    order = tuple(range(1, nc)) + (0,)

    part_rows = nc * rows_w
    def weight_grad(g, left, right):
        dst = grads[g][0]

        def rows_from(first, count):
            def step(m, _):
                rows = pl.ds(pl.multiple_of(first + m * TILE, TILE), TILE)
                dst[rows] = dot_first(left[:, rows], right[...]).astype(BF16)
                return 0

            lax.fori_loop(0, count // TILE, step, 0)

        split = part_rows % TILE == 0
        if not split:
            rows_from(0, width)
        for df in tuple(range(1, nf)) + (0,):
            to = lax.rem(f + df, nf)
            if split:
                rows_from(to * part_rows, part_rows)
            if df:
                for i in order:
                    gx_copy(g, df, i, to).start()

    def gy_copy(g, i, slot, cc):
        buf, _, got = grads[g][:3]
        return remote(
            buf.at[own_rows(cc)], got.at[slot], gy_s.at[g, i], gy_r.at[g, i], (f, cc, t)
        )

    def g_cross(g, i):
        buf, got, held = grads[g][:3]
        cc = lax.rem(c + i, nc)
        for df in range(1, nf):
            gx_copy(g, df, i, lax.rem(f + nf - df, nf)).wait_recv()

        def add(n, _):
            rows = pl.ds(pl.multiple_of((f * nc + cc) * rows_w + n * ROWS, ROWS), ROWS)
            total = buf[rows].astype(F32)
            for df in range(1, nf):
                theirs = pl.ds(pl.multiple_of(cc * rows_w + n * ROWS, ROWS), ROWS)
                total = total + got[df - 1, theirs].astype(F32)
            if i:
                buf[rows] = total.astype(BF16)
            else:
                held[c, pl.ds(pl.multiple_of(n * ROWS, ROWS), ROWS)] = total.astype(BF16)
            return 0

        lax.fori_loop(0, rows_w // ROWS, add, 0)
        if i:
            gy_copy(g, i, c, cc).start()

    def gz_copy(g, n, src, dst, to):
        return remote(src, dst, gz_s.at[g, n], gz_r.at[g, n], (f, c, to))

    def g_line(g):
        _, _, held, final, part = grads[g]
        for i in range(1, nc):
            cs = lax.rem(c + nc - i, nc)
            gy_copy(g, i, cs, cs).wait_recv()

        @pl.when(jnp.logical_not(inner))
        def _():
            gz_copy(g, 2, held.at[far_out], part.at[1], pair).start()
            gz_copy(g, 1, held.at[far_in], part.at[0], pair).start()

        gz_copy(g, 0, held.at[pair], final.at[0], pair).start()

    def g_relay(g):
        _, _, held, final, part = grads[g]

        @pl.when(inner)
        def _():
            for n, (to, slot) in enumerate(((far_out, 1), (far_in, 0))):
                gz_copy(g, 1 + slot, held.at[to], part.at[slot], pair).wait_recv()

                def add(m, _):
                    rows = pl.ds(pl.multiple_of(m * ROWS, ROWS), ROWS)
                    held[to, rows] = (
                        held[to, rows].astype(F32) + part[slot, rows].astype(F32)
                    ).astype(BF16)
                    return 0

                lax.fori_loop(0, rows_w // ROWS, add, 0)
                remote(
                    held.at[to], final.at[1], gz_s.at[g, 1 + slot], gz_r.at[g, 3], (f, c, to)
                ).start()

    def g_out(g, store):
        _, _, held, final, _ = grads[g]
        gz_copy(g, 0, held.at[t], final.at[0], pair).wait_recv()
        gz_copy(g, 3, held.at[t], final.at[1], far_in).wait_recv()

        def add(m, _):
            rows = pl.ds(pl.multiple_of(m * ROWS, ROWS), ROWS)
            store(
                rows,
                held[t, rows].astype(F32)
                + final[0, rows].astype(F32)
                + final[1, rows].astype(F32),
            )
            return 0

        lax.fori_loop(0, rows_w // ROWS, add, 0)

    def g_finish(g):
        _, _, held, final, part = grads[g]
        for i in order:
            for df in range(1, nf):
                gx_copy(g, df, i, lax.rem(f + df, nf)).wait_send()
        for i in range(1, nc):
            gy_copy(g, i, c, lax.rem(c + i, nc)).wait_send()
        for n in range(3):
            gz_copy(g, n, held.at[0], final.at[0], pair).wait_send()

    back(c)
    for k in range(CHUNKS):
        ag_wait(dl2, 2, k, 0)
    back(c_sib)
    rs_sib(2, 1, up_back(c_sib))
    rs_own(2, up_back(c))
    for k in range(CHUNKS):
        ag_pass(dl2, 2, k)
    back(c_y)
    for k in range(CHUNKS):
        ag_wait(dl2, 2, k, 2)
    back(c_ysib)
    rs_sib(2, 0, up_back(c_ysib))
    rs_y(2, up_back(c_y))
    weight_grad(0, dl2, act)
    weight_grad(1, nl, dpl)
    rs_copy(2, 1).wait_recv()

    def norm1_back(rows, i):
        dn = dres[rows] + rs_row(rows)
        xh = xh1[rows]
        add_sum(1, dn * xh)
        add_sum(2, dn)
        gy = dn * gain1
        dr = (gy - mean(gy) - xh * mean(gy * xh)) * rstd1[rows, 0:1]
        add_sum(0, dr)
        dres[rows] = dr
        dl1[own_slice(rows)] = dr.astype(BF16)

    for k in range(CHUNKS):
        rs_rows(2, k, norm1_back)
        ag_send(dl1, 3, k)

    dk_acc[...] = jnp.zeros_like(dk_acc)
    dv_acc[...] = jnp.zeros_like(dv_acc)

    def attend_back(b):
        rows = aligned(b, seq)
        datt[rows] = dot(dl1[rows], wo[...]).astype(BF16)
        qb = qs[rows]
        db = datt[rows]

        def head(h, _):
            qm = head_part(qb, h)
            dm = head_part(db, h)
            p = jnp.exp(masked_scores(qm) - lse[h, :, rows])
            dv_acc[...] += dot(p.astype(BF16), dm)
            pd = p * dot_last(vv[...], dm)
            delta = jnp.sum(pd, 0, keepdims=True)
            ds = (pd - p * delta).astype(BF16)
            dk_acc[...] += dot(ds, qm)
            hrows = aligned(h, DH)
            ot[hrows] = dot(kt[hrows], ds)
            return 0

        lax.fori_loop(0, heads, head, 0)
        dq = (ot[...].T * scale).astype(BF16)
        dqkv[rows, 0:hid] = dq
        dqf = dq.astype(F32)
        sums[7, :, 0:hid] = sums[7, :, 0:hid] + jnp.sum(dqf.reshape(seq // 8, 8, hid), 0)

    attend_back(c)
    g_cross(0, 1)
    g_cross(0, 2)
    for k in range(CHUNKS):
        ag_wait(dl1, 3, k, 0)
    attend_back(c_sib)
    for k in range(CHUNKS):
        ag_pass(dl1, 3, k)
    g_cross(0, 3)
    g_cross(0, 0)
    attend_back(c_y)
    g_line(0)
    for k in range(CHUNKS):
        ag_wait(dl1, 3, k, 2)
    weight_grad(2, dl1, att)
    g_cross(1, 1)
    g_cross(1, 2)
    attend_back(c_ysib)
    g_relay(0)
    g_cross(1, 3)
    g_cross(1, 0)

    def finish_kv(b, _):
        rows = aligned(b, seq)
        dqkv[rows, hid : 2 * hid] = dk_acc[rows].astype(BF16)
        dvb = dv_acc[rows].astype(BF16)
        dqkv[rows, 2 * hid : 3 * hid] = dvb
        sums[7, :, hid : 2 * hid] = sums[7, :, hid : 2 * hid] + jnp.sum(
            dvb.astype(F32).reshape(seq // 8, 8, hid), 0
        )
        return 0

    lax.fori_loop(0, nc, finish_kv, 0)

    def in_back(b):
        qb = dqkv[aligned(b, seq)]
        return lambda n: dot_last(qb, wqkv[aligned(n, TILE)])

    rs_sib(3, 0, in_back(c_ysib))
    rs_y(3, in_back(c_y))
    g_line(1)
    rs_sib(3, 1, in_back(c_sib))
    rs_own(3, in_back(c))
    weight_grad(3, x_tok, dqkv)
    g_relay(1)
    sm[...] = jnp.sum(sums[...], 1)

    def sm_copy(stage, j, src, dst, dev):
        return remote(src, dst, sm_s.at[stage, j], sm_r.at[stage, j], dev)

    for j in range(1, nt):
        sm_copy(0, j, sm, smz.at[j], (f, c, lax.rem(t + j, nt))).start()
    for i in order:
        g_cross(2, i)
    rs_copy(3, 1).wait_recv()

    def grad_in(rows, i):
        gi_s[rows] = (dres[rows] + rs_row(rows)).astype(BF16)

    def line_copy(k, src, ts, n, to):
        rows = pl.ds(k * chunk, chunk)
        return remote(
            src.at[rows], gi_h.at[ts, rows], line_s.at[k, n], line_r.at[k, n], (f, c, to)
        )

    for k in range(CHUNKS):
        rs_rows(3, k, grad_in)
        rows = pl.ds(k * chunk, chunk)
        pltpu.make_async_copy(gi_s.at[rows], gi_h.at[t, rows], line_r.at[k, 0]).start()
        hops(lambda ts, n, to: line_copy(k, gi_s, ts, n, to).start(), 0)
    g_line(2)

    def line_hop(k, h):
        arrivals(lambda ts, n, source: line_copy(k, gi_h.at[ts], ts, n, source).wait_recv(), h)
        if h < nt - 1:
            hops(lambda ts, n, to: line_copy(k, gi_h.at[ts], ts, n, to).start(), h)

    for i in order[:2]:
        g_cross(3, i)
    for k in range(CHUNKS):
        line_hop(k, 1)
    for i in order[2:]:
        g_cross(3, i)
    g_line(3)
    g_relay(2)
    total = sm[...]
    for j in range(1, nt):
        sm_copy(0, j, sm, smz.at[j], (f, c, lax.rem(t + nt - j, nt))).wait_recv()
        total = total + smz[j]
    smz[0] = total
    for df in range(1, nf):
        sm_copy(1, df, smz.at[0], smx.at[df], (lax.rem(f + df, nf), c, t)).start()
    for k in range(CHUNKS):
        line_hop(k, 2)
    for df in range(1, nf):
        sm_copy(1, df, smz.at[0], smx.at[df], (lax.rem(f + nf - df, nf), c, t)).wait_recv()
        total = total + smx[df]
    smx[0] = total
    for dc in range(1, nc):
        sm_copy(2, dc, smx.at[0], smc.at[c], (f, lax.rem(c + dc, nc), t)).start()
    smc[c] = total
    g_relay(3)

    def store_in(*outs):
        def store(rows, value):
            for k, out in enumerate(outs):
                out[rows] = value[:, k * out.shape[1] : (k + 1) * out.shape[1]]

        return store

    g_out(0, store_in(gd_o))
    g_out(1, store_in(gu_o))
    g_out(2, store_in(go_o))
    for dc in range(1, nc):
        cs = lax.rem(c + nc - dc, nc)
        sm_copy(2, dc, smx.at[0], smc.at[cs], (f, cs, t)).wait_recv()
    whole = smc[0]
    for s in range(1, nc):
        whole = whole + smc[s]
    small_o[0:6] = whole[0:6]
    small_o[6:8] = smc[t, 6:8]
    g_out(3, store_in(gq_o, gk_o, gv_o))
    spread_wait(res_s, res_h, 0)
    for k in range(CHUNKS):
        line_hop(k, 3)
        rows = pl.ds(k * chunk, chunk)
        pltpu.make_async_copy(gi_s.at[rows], gi_h.at[t, rows], line_r.at[k, 0]).wait()
        for h in range(nt - 1):
            hops(lambda ts, n, to: line_copy(k, gi_h.at[ts], ts, n, to).wait_send(), h)

    for g in range(4):
        g_finish(g)
    for a, buf in enumerate((x_tok, nl, dl2, dl1)):
        ag_finish(buf, a)
    rs_copy(3, 0).wait_send()
    rs_copy(3, 1).wait_send()
    for k in range(CHUNKS):
        ry_copy(3, k).wait_send()
    for j in range(1, nt):
        sm_copy(0, j, sm, smz.at[j], (f, c, lax.rem(t + j, nt))).wait_send()
    for df in range(1, nf):
        sm_copy(1, df, smz.at[0], smx.at[df], (lax.rem(f + df, nf), c, t)).wait_send()
    for dc in range(1, nc):
        sm_copy(2, dc, smx.at[0], smc.at[c], (f, lax.rem(c + dc, nc), t)).wait_send()

    @pl.when(t == c)
    def _():
        for j in range(1, nt):
            remote(
                bias, bias, bias_s.at[j], bias_r.at[0], (f, c, lax.rem(t + j, nt))
            ).wait_send()


def hand_over(small_rows, *refs):
    whole, small = refs[:8], refs[8]
    outs, small_o = refs[9:17], refs[17:26]

    @pl.when(pl.program_id(0) == 0)
    def _():
        for out, (row, start, size) in zip(small_o, small_rows):
            out[...] = small[row : row + 1, start : start + size]

    for out, value in zip(outs, whole):
        out[...] = value[...].astype(out.dtype)


def shards(
    dims,
    inputs,
    lengths,
    w_query,
    w_key,
    w_value,
    b_query,
    b_value,
    w_out,
    b_out,
    gain_attn,
    shift_attn,
    w_up,
    b_up,
    w_down,
    b_down,
    gain_ffn,
    shift_ffn,
    cotangent,
):
    nf, nc, nt = dims
    seq_dev, seq, width = inputs.shape
    rows_w, hid = w_query.shape
    ff = w_up.shape[1]
    assert nc == 4 and nt == nc and seq_dev == nt and ff == width
    tok = seq * nc
    heads = hid // DH
    part = nc * rows_w
    rows = [
        v.reshape(1, -1)
        for v in (
            b_query,
            b_value,
            b_up,
            b_out,
            gain_attn,
            shift_attn,
            b_down,
            gain_ffn,
            shift_ffn,
        )
    ]
    hbm = pl.BlockSpec(memory_space=pl.ANY)
    vmem = pl.BlockSpec(memory_space=pltpu.VMEM)
    smem = pl.BlockSpec(memory_space=pltpu.SMEM)

    def vb(*shape):
        return pltpu.VMEM(shape, BF16)

    def vf(*shape):
        return pltpu.VMEM(shape, F32)

    def sem(*shape):
        return pltpu.SemaphoreType.DMA(shape)

    result, grad_in, g_q, g_k, g_v, g_o, g_u, g_d, small = pl.pallas_call(
        functools.partial(layer, dims),
        out_shape=(
            jax.ShapeDtypeStruct((nt, seq, width), BF16),
            jax.ShapeDtypeStruct((nt, seq, width), BF16),
            *[jax.ShapeDtypeStruct((rows_w, hid), F32)] * 4,
            *[jax.ShapeDtypeStruct((rows_w, ff), F32)] * 2,
            jax.ShapeDtypeStruct((8, width), F32),
        ),
        in_specs=[smem] + [hbm] * 11 + [vmem] * 6,
        out_specs=(hbm, hbm) + (vmem,) * 7,
        scratch_shapes=[
            vb(width, 3 * hid),
            vb(width, hid),
            vb(width, ff),
            vb(width, ff),
            vb(nt, rows_w, 3 * hid),
            vb(nt, rows_w, hid),
            vb(nt, rows_w, ff),
            vb(nt, rows_w, ff),
            vb(tok, width),
            vb(tok, width),
            vb(tok, width),
            vb(tok, width),
            vb(tok, hid),
            vb(tok, hid),
            vb(tok, hid),
            vb(hid, tok),
            vb(hid, tok),
            vb(tok, hid),
            vb(tok, hid),
            vf(hid, seq),
            vf(heads, 1, tok),
            vb(tok, ff),
            vb(tok, ff),
            vb(tok, ff),
            vb(tok, 3 * hid),
            vf(tok, hid),
            vf(tok, hid),
            vb(2, seq, width),
            vb(2, seq, width),
            vb(seq, width),
            vb(seq, width),
            vf(seq, width),
            vf(seq, width),
            vf(seq, width),
            vf(seq, 128),
            vf(seq, width),
            vb(seq, width),
            vb(seq, width),
            vb(seq, width),
            vf(1, 2 * hid + ff),
            vb(width, ff),
            vb(width, ff),
            vb(width, 3 * hid),
            vb(width, hid),
            vb(nf - 1, part, ff),
            vb(nf - 1, part, ff),
            vb(nf - 1, part, 3 * hid),
            vb(nf - 1, part, hid),
            vb(2, rows_w, ff),
            vb(2, rows_w, ff),
            vb(2, rows_w, 3 * hid),
            vb(2, rows_w, hid),
            vb(2, rows_w, ff),
            vb(2, rows_w, ff),
            vb(2, rows_w, 3 * hid),
            vb(2, rows_w, hid),
            vf(8, 8, width),
            vf(8, width),
            vf(nt, 8, width),
            vf(nf, 8, width),
            vf(nc, 8, width),
            sem(3),
            sem(nt),
            sem(1),
            sem(4, 2 * nt),
            sem(4, 2 * nt),
            sem(4, nt),
            sem(4, nc),
            sem(4, nf),
            sem(4, nf),
            sem(4, 3, CHUNKS),
            sem(4, 3, CHUNKS),
            sem(4, 2),
            sem(4, 2),
            sem(4, CHUNKS),
            sem(4, CHUNKS),
            sem(1, nt),
            sem(1, nt),
            sem(4, nf, nc),
            sem(4, nf, nc),
            sem(4, nc),
            sem(4, nc),
            sem(4, 3),
            sem(4, 4),
            sem(CHUNKS, 2 * nt),
            sem(CHUNKS, 2 * nt),
            sem(3, max(nf, nc)),
            sem(3, max(nf, nc)),
        ],
        compiler_params=pltpu.CompilerParams(
            collective_id=0, has_side_effects=True, vmem_limit_bytes=63 << 20
        ),
    )(lengths, inputs, cotangent, w_query, w_key, w_value, w_out, w_up, w_down, *rows)
    small_rows = ((7, 0, hid), (7, hid, hid), (0, 0, width), (1, 0, width), (2, 0, width))
    small_rows += ((6, 0, ff), (3, 0, width), (4, 0, width), (5, 0, width))
    whole = (result, g_q, g_k, g_v, g_o, g_u, g_d, grad_in)
    step = rows_w // nt if rows_w % (8 * nt) == 0 else rows_w

    def block(a):
        if a.ndim == 3:
            return pl.BlockSpec((1, seq, width), lambda i: (i, 0, 0))
        return pl.BlockSpec((step, a.shape[1]), lambda i: (i if step < rows_w else 0, 0))

    outs = pl.pallas_call(
        functools.partial(hand_over, small_rows),
        grid=(nt,),
        out_shape=tuple(jax.ShapeDtypeStruct(a.shape, a.dtype) for a in whole[:7])
        + (jax.ShapeDtypeStruct(grad_in.shape, F32),)
        + tuple(jax.ShapeDtypeStruct((1, n), F32) for _, _, n in small_rows),
        in_specs=[block(a) for a in whole] + [vmem],
        out_specs=tuple(block(a) for a in whole) + (vmem,) * 9,
    )(*whole, small)
    result, g_q, g_k, g_v, g_o, g_u, g_d, grad_in = outs[:8]
    s_bq, s_bv, s_bo, s_ga, s_sa, s_bu, s_bd, s_gf, s_sf = (a.reshape(-1) for a in outs[8:])
    return (
        result,
        grad_in,
        g_q,
        g_k,
        g_v,
        s_bq,
        s_bv,
        g_o,
        s_bo,
        s_ga,
        s_sa,
        g_u,
        s_bu,
        g_d,
        s_bd,
        s_gf,
        s_sf,
    )


def solution(mesh):
    weight = P(("fsdp", "ctx"), "tp")
    acts = P("fsdp", "ctx", None)
    dims = tuple(mesh.shape[a] for a in ("fsdp", "ctx", "tp"))
    return jax.shard_map(
        functools.partial(shards, dims),
        mesh=mesh,
        in_specs=(
            acts,
            P("fsdp"),
            weight,
            weight,
            weight,
            P("tp"),
            P("tp"),
            weight,
            P(),
            P(),
            P(),
            weight,
            P("tp"),
            weight,
            P(),
            P(),
            P(),
            acts,
        ),
        out_specs=(
            acts,
            acts,
            weight,
            weight,
            weight,
            P("tp"),
            P("tp"),
            weight,
            P(),
            P(),
            P(),
            weight,
            P("tp"),
            weight,
            P(),
            P(),
            P(),
        ),
        check_vma=False,
    )
```

```python
import functools
import math

import jax
import jax.numpy as jnp
from jax import lax
from jax.experimental import pallas as pl
from jax.experimental.pallas import tpu as pltpu
from jax.sharding import PartitionSpec as P

DH = 64
MESH = pl.DeviceIdType.MESH
F32 = jnp.float32
BF16 = jnp.bfloat16
TILE = 256
ROWS = 16
CHUNKS = 2


def dot(left, right):
    return jnp.dot(left, right, preferred_element_type=F32)


def dot_last(left, right):
    return lax.dot_general(left, right, (((1,), (1,)), ((), ())), preferred_element_type=F32)


def dot_first(left, right):
    return lax.dot_general(left, right, (((0,), (0,)), ((), ())), preferred_element_type=F32)


def aligned(index, size):
    return pl.ds(pl.multiple_of(index * size, size), size)


def layer(
    dims,
    lens,
    x_h,
    ct_h,
    wq_h,
    wk_h,
    wv_h,
    wo_h,
    wu_h,
    wd_h,
    bq_h,
    bv_h,
    bu_h,
    b_out_r,
    gain1_r,
    shift1_r,
    b_down_r,
    gain2_r,
    shift2_r,
    res_h,
    gi_h,
    gq_o,
    gk_o,
    gv_o,
    go_o,
    gu_o,
    gd_o,
    small_o,
    wqkv,
    wo,
    wu,
    wd,
    z0,
    z1,
    z2,
    z3,
    x_tok,
    nl,
    dl2,
    dl1,
    qs,
    kk,
    vv,
    kt,
    vt,
    att,
    datt,
    ot,
    lse,
    act,
    dg,
    dpl,
    dqkv,
    dk_acc,
    dv_acc,
    ps,
    pr,
    ysend,
    yrecv,
    acc_y,
    acc_o,
    xh1,
    rstd1,
    dres,
    res_s,
    gi_s,
    ct_s,
    bias,
    gwd,
    gwu,
    gqkv,
    gwo,
    xg_d,
    xg_u,
    xg_q,
    xg_o,
    zf_d,
    zf_u,
    zf_q,
    zf_o,
    zp_d,
    zp_u,
    zp_q,
    zp_o,
    sums,
    sm,
    smz,
    smx,
    smc,
    loc_sem,
    bias_s,
    bias_r,
    wz_s,
    wz_r,
    wy_s,
    wy_r,
    wx_s,
    wx_r,
    ag_s,
    ag_r,
    rs_s,
    rs_r,
    ry_s,
    ry_r,
    out_s,
    out_r,
    gx_s,
    gx_r,
    gy_s,
    gy_r,
    gz_s,
    gz_r,
    line_s,
    line_r,
    sm_s,
    sm_r,
):
    nf, nc, nt = dims
    f = lax.axis_index("fsdp")
    c = lax.axis_index("ctx")
    t = lax.axis_index("tp")
    yi, ki = c // 2, lax.rem(c, 2)
    c_sib = yi * 2 + (1 - ki)
    c_y = (1 - yi) * 2 + ki
    c_ysib = (1 - yi) * 2 + (1 - ki)
    seq, width = ct_s.shape
    tok = x_tok.shape[0]
    rows_w = z0.shape[1]
    hid = wo.shape[1]
    ff = wu.shape[1]
    heads = hid // DH
    scale = 1.0 / math.sqrt(DH)
    chunk = seq // CHUNKS
    sib = (f, c_sib, t)
    ypeer = (f, c_y, t)
    length = lens[t]

    def remote(src, dst, ssem, rsem, dev):
        return pltpu.make_async_remote_copy(
            src_ref=src, dst_ref=dst, send_sem=ssem, recv_sem=rsem, device_id=dev, device_id_type=MESH
        )

    bar = pltpu.get_barrier_semaphore()
    for dc in range(nc):
        for dt in range(nt):
            if dc or dt:
                pl.semaphore_signal(
                    bar,
                    inc=1,
                    device_id=(f, lax.rem(c + dc, nc), lax.rem(t + dt, nt)),
                    device_id_type=MESH,
                )
    for df in range(1, nf):
        pl.semaphore_signal(bar, inc=1, device_id=(lax.rem(f + df, nf), c, t), device_id_type=MESH)
    pl.semaphore_wait(bar, nc * nt - 1 + nf - 1)

    groups = (
        ((wq_h, wk_h, wv_h), z0, wqkv),
        ((wo_h,), z1, wo),
        ((wu_h,), z2, wu),
        ((wd_h,), z3, wd),
    )

    def own_rows(cc):
        return aligned(f * nc + cc, rows_w)

    def hops(send, h):
        @pl.when((t >= h) & (t < nt - 1))
        def _():
            send(t - h, h + 1, t + 1)

        @pl.when((t + h < nt) & (t > 0))
        def _():
            send(t + h, nt + h, t - 1)

    def arrivals(take, h):
        @pl.when(t >= h)
        def _():
            take(t - h, h, t - 1)

        @pl.when(t + h < nt)
        def _():
            take(t + h, nt - 1 + h, t + 1)

    def w_cross_at(g, h):
        pl.when(t >= h)(lambda: w_cross(g, h))
        pl.when(t + h < nt)(lambda: w_cross(g, nt - h))

    def w_line_copy(g, src, ts, n, to):
        return remote(
            src, groups[g][1].at[ts], wz_s.at[g, n], wz_r.at[g, n], (f, c, to)
        )

    def w_start(g):
        srcs, stage, _ = groups[g]
        for k, src in enumerate(srcs):
            dst = stage.at[t, :, pl.ds(k * src.shape[1], src.shape[1])]
            pltpu.make_async_copy(src, dst, wz_r.at[g, 0]).start()
            if g:
                hops(lambda ts, n, to: w_line_copy(g, src, ts, n, to).start(), 0)
            for j in range(1, 1 if g else nt):
                remote(src, dst, wz_s.at[g, j], wz_r.at[g, j], (f, c, lax.rem(t + j, nt))).start()

    def w_cross_block(g, ts):
        _, stage, final = groups[g]

        @pl.when(ts == c)
        def _():
            pltpu.make_async_copy(stage.at[ts], final.at[own_rows(c)], wy_r.at[g, c]).start()

        @pl.when(ts != c)
        def _():
            remote(
                stage.at[ts], final.at[own_rows(c)], wy_s.at[g, ts], wy_r.at[g, c], (f, ts, t)
            ).start()

    def w_cross(g, j):
        stage = groups[g][1]
        ts = lax.rem(t + nt - j, nt)
        if j == 0:
            pltpu.make_async_copy(stage.at[ts], stage.at[ts], wz_r.at[g, 0]).wait()
        else:
            remote(stage.at[ts], stage.at[ts], wz_s.at[g, j], wz_r.at[g, j], (f, c, ts)).wait_recv()
        w_cross_block(g, ts)

    def w_line(g, h):
        stage = groups[g][1]

        def take(ts, n, source):
            w_line_copy(g, stage.at[ts], ts, n, source).wait_recv()

        arrivals(take, h)
        if h < nt - 1:
            hops(lambda ts, n, to: w_line_copy(g, stage.at[ts], ts, n, to).start(), h)
        arrivals(lambda ts, n, source: w_cross_block(g, ts), h)

    def w_spread(g, i):
        _, _, final = groups[g]
        cc = lax.rem(c + i, nc)
        part = final.at[own_rows(cc)]
        if i == 0:
            pltpu.make_async_copy(part, part, wy_r.at[g, cc]).wait()
        else:
            remote(part, part, wy_s.at[g, 0], wy_r.at[g, cc], (f, cc, t)).wait_recv()
        for df in range(1, nf):
            remote(
                part, part, wx_s.at[g, df], wx_r.at[g, df], (lax.rem(f + df, nf), c, t)
            ).start()

    def w_spread_at(g, h):
        @pl.when((t - c == h) | (c - t == h))
        def _():
            for i in range(nc):
                w_spread(g, i)

    def w_wait(g):
        _, _, final = groups[g]
        for df in range(1, nf):
            fs = lax.rem(f + nf - df, nf)
            part = final.at[aligned(fs, nc * rows_w)]
            remote(part, part, wx_s.at[g, df], wx_r.at[g, df], (fs, c, t)).wait_recv()

    def w_finish(g):
        _, stage, final = groups[g]
        if g:
            for h in range(nt - 1):
                hops(lambda ts, n, to: w_line_copy(g, stage.at[ts], ts, n, to).wait_send(), h)
        for j in range(1, 1 if g else nt):
            remote(
                stage.at[0], stage.at[0], wz_s.at[g, j], wz_r.at[g, j], (f, c, lax.rem(t + j, nt))
            ).wait_send()
        for j in range(nt):
            ts = lax.rem(t + nt - j, nt)

            @pl.when(ts != c)
            def _():
                remote(
                    stage.at[ts], final.at[own_rows(c)], wy_s.at[g, ts], wy_r.at[g, c], (f, ts, t)
                ).wait_send()

        for df in range(1, nf):
            part = final.at[aligned(f, nc * rows_w)]
            remote(
                part, part, wx_s.at[g, df], wx_r.at[g, df], (lax.rem(f + df, nf), c, t)
            ).wait_send()

    def part_of(buf, cc, k):
        return buf.at[pl.ds(pl.multiple_of(cc * seq + k * chunk, chunk), chunk)]

    def ag_copy(buf, a, k, cc, way, dev):
        part = part_of(buf, cc, k)
        return remote(part, part, ag_s.at[a, way, k], ag_r.at[a, way, k], dev)

    def ag_send(buf, a, k):
        ag_copy(buf, a, k, c, 1, ypeer).start()
        ag_copy(buf, a, k, c, 0, sib).start()

    def ag_pass(buf, a, k):
        ag_copy(buf, a, k, c_y, 1, ypeer).wait_recv()
        ag_copy(buf, a, k, c_y, 2, sib).start()

    def ag_wait(buf, a, k, way):
        ag_copy(buf, a, k, c_sib if way == 0 else c_ysib, way, sib).wait_recv()

    def ag_finish(buf, a):
        for k in range(CHUNKS):
            ag_copy(buf, a, k, c, 0, sib).wait_send()
            ag_copy(buf, a, k, c, 1, ypeer).wait_send()
            ag_copy(buf, a, k, c_y, 2, sib).wait_send()

    tiles = width // TILE

    def rs_copy(o, slot):
        return remote(ps.at[slot], pr.at[slot], rs_s.at[o, slot], rs_r.at[o, slot], sib)

    def ry_copy(o, k):
        rows = pl.ds(k * chunk, chunk)
        return remote(ysend.at[rows], yrecv.at[rows], ry_s.at[o, k], ry_r.at[o, k], ypeer)

    def rs_sib(o, slot, produce):
        if o:
            rs_copy(o - 1, slot).wait_send()

        def tile(n, _):
            ps[slot, :, aligned(n, TILE)] = produce(n).astype(BF16)
            return 0

        lax.fori_loop(0, tiles, tile, 0)
        rs_copy(o, slot).start()

    def rs_y(o, produce):
        def tile(n, _):
            acc_y[:, aligned(n, TILE)] = produce(n)
            return 0

        lax.fori_loop(0, tiles, tile, 0)
        rs_copy(o, 0).wait_recv()
        for k in range(CHUNKS):
            if o:
                ry_copy(o - 1, k).wait_send()

            def add(i, _, k=k):
                rows = pl.ds(pl.multiple_of(k * chunk + i * ROWS, ROWS), ROWS)
                ysend[rows] = (acc_y[rows] + pr[0, rows].astype(F32)).astype(BF16)
                return 0

            lax.fori_loop(0, chunk // ROWS, add, 0)
            ry_copy(o, k).start()

    def rs_own(o, produce):
        def tile(n, _):
            acc_o[:, aligned(n, TILE)] = produce(n)
            return 0

        lax.fori_loop(0, tiles, tile, 0)

    def rs_row(rows):
        return acc_o[rows] + pr[1, rows].astype(F32) + yrecv[rows].astype(F32)

    def rs_rows(o, k, body):
        ry_copy(o, k).wait_recv()

        def step(i, _):
            body(pl.ds(pl.multiple_of(k * chunk + i * ROWS, ROWS), ROWS), i)
            return 0

        lax.fori_loop(0, chunk // ROWS, step, 0)

    def add_sum(k, value):
        half = value[0:8]
        for r in range(8, ROWS, 8):
            half = half + value[r : r + 8]
        sums[k] = sums[k] + half

    def mean(value):
        return jnp.sum(value, -1, keepdims=True) * (1.0 / width)

    w_start(0)
    pltpu.make_async_copy(x_h.at[t], x_tok.at[aligned(c, seq)], loc_sem.at[0]).start()
    pltpu.make_async_copy(ct_h.at[t], ct_s, loc_sem.at[1]).start()

    biases = (
        (bq_h, bias.at[:, pl.ds(0, hid)]),
        (bv_h, bias.at[:, pl.ds(hid, hid)]),
        (bu_h, bias.at[:, pl.ds(2 * hid, ff)]),
    )

    @pl.when(t == c)
    def _():
        for src, dst in biases:
            pltpu.make_async_copy(src, dst, loc_sem.at[2]).start()
            for j in range(1, nt):
                remote(src, dst, bias_s.at[j], bias_r.at[0], (f, c, lax.rem(t + j, nt))).start()

    pltpu.make_async_copy(x_h.at[t], x_tok.at[aligned(c, seq)], loc_sem.at[0]).wait()
    for k in range(CHUNKS):
        ag_send(x_tok, 0, k)
    w_start(1)
    w_start(2)
    w_cross(0, 0)
    w_cross(1, 0)
    sums[...] = jnp.zeros_like(sums)
    w_cross_at(0, 1)
    ag_pass(x_tok, 0, 0)
    w_spread_at(0, 0)
    w_cross_at(0, 2)
    for k in range(1, CHUNKS):
        ag_pass(x_tok, 0, k)
    w_spread_at(0, 1)
    w_cross_at(0, 3)
    w_spread_at(1, 0)
    w_cross(2, 0)
    w_line(1, 1)
    w_spread_at(0, 2)
    w_start(3)
    w_line(1, 2)
    w_spread_at(1, 1)
    w_line(2, 1)
    w_spread_at(0, 3)
    w_spread_at(2, 0)
    w_cross(3, 0)
    w_line(1, 3)
    w_spread_at(1, 2)

    @pl.when(t == c)
    def _():
        pltpu.make_async_copy(bias, bias, loc_sem.at[2]).wait()

    @pl.when(t != c)
    def _():
        remote(bias, bias, bias_s.at[0], bias_r.at[0], (f, c, c)).wait_recv()

    for k in range(CHUNKS):
        ag_wait(x_tok, 0, k, 0)
        ag_wait(x_tok, 0, k, 2)
    w_wait(0)
    w_line(3, 1)
    w_spread_at(1, 3)

    def project(b, _):
        rows = aligned(b, seq)
        xb = x_tok[rows]
        qv = dot(xb, wqkv[:, 0:hid]) + bias[0:1, 0:hid]
        qs[rows] = (qv * scale).astype(BF16)
        kb = dot(xb, wqkv[:, hid : 2 * hid])
        kk[rows] = kb.astype(BF16)
        kt[:, rows] = kb.T.astype(BF16)
        vb = dot(xb, wqkv[:, 2 * hid : 3 * hid]) + bias[0:1, hid : 2 * hid]
        vv[rows] = vb.astype(BF16)
        vt[:, rows] = vb.T.astype(BF16)
        return 0

    lax.fori_loop(0, nc, project, 0)

    lane = lax.broadcasted_iota(jnp.int32, (seq, hid), 1)

    def head_part(value, h):
        inside = (lane >= h * DH) & (lane < (h + 1) * DH)
        return jnp.where(inside, value, jnp.zeros_like(value))

    def masked_scores(qm):
        s = dot_last(kk[...], qm)
        key = lax.broadcasted_iota(jnp.int32, s.shape, 0)
        return jnp.where(key < length, s, -1e30)

    def attend(b):
        rows = aligned(b, seq)
        qb = qs[rows]

        def head(h, _):
            s = masked_scores(head_part(qb, h))
            top = jnp.max(s, 0, keepdims=True)
            e = jnp.exp(s - top)
            total = jnp.sum(e, 0, keepdims=True)
            hrows = aligned(h, DH)
            ot[hrows] = dot(vt[hrows], e.astype(BF16)) / total
            lse[h, :, rows] = top + jnp.log(total)
            return 0

        lax.fori_loop(0, heads, head, 0)
        att[rows] = ot[...].T.astype(BF16)

    def out_proj(b):
        ab = att[aligned(b, seq)]
        return lambda n: dot_last(ab, wo[aligned(n, TILE)])

    w_line(2, 2)
    w_spread_at(2, 1)
    w_spread_at(3, 0)
    attend(c_ysib)
    w_line(3, 2)
    w_spread_at(2, 2)
    w_spread_at(3, 1)
    attend(c_y)
    w_line(2, 3)
    w_wait(1)
    rs_sib(0, 0, out_proj(c_ysib))
    rs_y(0, out_proj(c_y))
    w_spread_at(2, 3)
    w_spread_at(3, 2)
    w_line(3, 3)
    attend(c_sib)
    rs_sib(0, 1, out_proj(c_sib))
    w_spread_at(3, 3)
    attend(c)
    rs_own(0, out_proj(c))
    rs_copy(0, 1).wait_recv()

    b_out, gain1, shift1 = b_out_r[...], gain1_r[...], shift1_r[...]
    b_down, gain2, shift2 = b_down_r[...], gain2_r[...], shift2_r[...]
    own = c * seq

    def own_slice(rows):
        return pl.ds(pl.multiple_of(own + rows.start, ROWS), ROWS)

    def norm1(rows, i):
        h = x_tok[own_slice(rows)].astype(F32) + rs_row(rows) + b_out
        cen = h - mean(h)
        inv = lax.rsqrt(mean(cen * cen) + 1e-5)
        xh = cen * inv
        xh1[rows] = xh
        rstd1[rows] = jnp.broadcast_to(inv, (ROWS, 128))
        nl[own_slice(rows)] = (xh * gain1 + shift1).astype(BF16)

    for k in range(CHUNKS):
        rs_rows(0, k, norm1)
        ag_send(nl, 1, k)
    w_wait(2)

    def up(b):
        rows = aligned(b, seq)
        nb = nl[rows]

        def tile(n, _):
            cols = aligned(n, TILE)
            v = dot(nb, wu[:, cols]) + bias[0:1, pl.ds(pl.multiple_of(2 * hid + n * TILE, 128), TILE)]
            cdf = 0.5 * (1.0 + lax.erf(v * math.sqrt(0.5)))
            act[rows, cols] = (v * cdf).astype(BF16)
            pdf = jnp.exp(-0.5 * v * v) * (1.0 / math.sqrt(2.0 * math.pi))
            dg[rows, cols] = (cdf + v * pdf).astype(BF16)
            return 0

        lax.fori_loop(0, ff // TILE, tile, 0)

    def down(b):
        ab = act[aligned(b, seq)]
        return lambda n: dot_last(ab, wd[aligned(n, TILE)])

    up(c)
    for k in range(CHUNKS):
        ag_wait(nl, 1, k, 0)
    up(c_sib)
    for k in range(CHUNKS):
        ag_pass(nl, 1, k)
    up(c_y)
    for k in range(CHUNKS):
        ag_wait(nl, 1, k, 2)
    up(c_ysib)
    w_wait(3)
    rs_sib(1, 0, down(c_ysib))
    rs_y(1, down(c_y))
    rs_sib(1, 1, down(c_sib))
    rs_own(1, down(c))
    rs_copy(1, 1).wait_recv()
    for g in range(4):
        w_finish(g)
    pltpu.make_async_copy(ct_h.at[t], ct_s, loc_sem.at[1]).wait()

    def norm2(rows, i):
        h = xh1[rows] * gain1 + shift1 + rs_row(rows) + b_down
        cen = h - mean(h)
        inv = lax.rsqrt(mean(cen * cen) + 1e-5)
        xh = cen * inv
        res_s[rows] = (xh * gain2 + shift2).astype(BF16)
        pos = own + rows.start + lax.broadcasted_iota(jnp.int32, (ROWS, width), 0)
        top = jnp.where(pos < length, ct_s[rows].astype(F32), 0.0)
        add_sum(4, top * xh)
        add_sum(5, top)
        gy = top * gain2
        dr = (gy - mean(gy) - xh * mean(gy * xh)) * inv
        add_sum(3, dr)
        dres[rows] = dr
        dl2[own_slice(rows)] = dr.astype(BF16)

    for k in range(CHUNKS):
        rs_rows(1, k, norm2)
        ag_send(dl2, 2, k)

    def spread(share, out, o):
        pltpu.make_async_copy(share, out.at[t], out_r.at[o, 0]).start()
        for j in range(1, nt):
            remote(
                share, out.at[t], out_s.at[o, j], out_r.at[o, j], (f, c, lax.rem(t + j, nt))
            ).start()

    def spread_wait(share, out, o):
        pltpu.make_async_copy(share, out.at[t], out_r.at[o, 0]).wait()
        for j in range(1, nt):
            ts = lax.rem(t + nt - j, nt)
            remote(share, out.at[ts], out_s.at[o, j], out_r.at[o, j], (f, c, ts)).wait_recv()
            remote(
                share, out.at[t], out_s.at[o, j], out_r.at[o, j], (f, c, lax.rem(t + j, nt))
            ).wait_send()

    spread(res_s, res_h, 0)

    def back(b):
        rows = aligned(b, seq)
        db = dl2[rows]

        def tile(n, _):
            cols = aligned(n, TILE)
            dp = (dot(db, wd[:, cols]) * dg[rows, cols].astype(F32)).astype(BF16)
            dpl[rows, cols] = dp
            dpf = dp.astype(F32)
            sums[6, :, cols] = sums[6, :, cols] + jnp.sum(dpf.reshape(seq // 8, 8, TILE), 0)
            return 0

        lax.fori_loop(0, ff // TILE, tile, 0)

    def up_back(b):
        pb = dpl[aligned(b, seq)]
        return lambda n: dot_last(pb, wu[aligned(n, TILE)])

    grads = (
        (gwd, xg_d, z3, zf_d, zp_d),
        (gwu, xg_u, z2, zf_u, zp_u),
        (gwo, xg_o, z1, zf_o, zp_o),
        (gqkv, xg_q, z0, zf_q, zp_q),
    )
    pair = t + 1 - 2 * lax.rem(t, 2)
    inner = (t == 1) | (t == nt - 2)
    far_in = jnp.where(t < 2, 2, 1)
    far_out = jnp.where(t < 2, nt - 1, 0)

    def gx_copy(g, df, i, dev_f):
        buf, got = grads[g][:2]
        cc = lax.rem(c + i, nc)
        return remote(
            buf.at[aligned(dev_f * nc + cc, rows_w)],
            got.at[df - 1, aligned(cc, rows_w)],
            gx_s.at[g, df, i],
            gx_r.at[g, df, i],
            (dev_f, c, t),
        )

    order = tuple(range(1, nc)) + (0,)

    part_rows = nc * rows_w
    def weight_grad(g, left, right):
        dst = grads[g][0]

        def rows_from(first, count):
            def step(m, _):
                rows = pl.ds(pl.multiple_of(first + m * TILE, TILE), TILE)
                dst[rows] = dot_first(left[:, rows], right[...]).astype(BF16)
                return 0

            lax.fori_loop(0, count // TILE, step, 0)

        split = part_rows % TILE == 0
        if not split:
            rows_from(0, width)
        for df in tuple(range(1, nf)) + (0,):
            to = lax.rem(f + df, nf)
            if split:
                rows_from(to * part_rows, part_rows)
            if df:
                for i in order:
                    gx_copy(g, df, i, to).start()

    def gy_copy(g, i, slot, cc):
        buf, _, got = grads[g][:3]
        return remote(
            buf.at[own_rows(cc)], got.at[slot], gy_s.at[g, i], gy_r.at[g, i], (f, cc, t)
        )

    def g_cross(g, i):
        buf, got, held = grads[g][:3]
        cc = lax.rem(c + i, nc)
        for df in range(1, nf):
            gx_copy(g, df, i, lax.rem(f + nf - df, nf)).wait_recv()

        def add(n, _):
            rows = pl.ds(pl.multiple_of((f * nc + cc) * rows_w + n * ROWS, ROWS), ROWS)
            total = buf[rows].astype(F32)
            for df in range(1, nf):
                theirs = pl.ds(pl.multiple_of(cc * rows_w + n * ROWS, ROWS), ROWS)
                total = total + got[df - 1, theirs].astype(F32)
            if i:
                buf[rows] = total.astype(BF16)
            else:
                held[c, pl.ds(pl.multiple_of(n * ROWS, ROWS), ROWS)] = total.astype(BF16)
            return 0

        lax.fori_loop(0, rows_w // ROWS, add, 0)
        if i:
            gy_copy(g, i, c, cc).start()

    def gz_copy(g, n, src, dst, to):
        return remote(src, dst, gz_s.at[g, n], gz_r.at[g, n], (f, c, to))

    def g_line(g):
        _, _, held, final, part = grads[g]
        for i in range(1, nc):
            cs = lax.rem(c + nc - i, nc)
            gy_copy(g, i, cs, cs).wait_recv()

        @pl.when(jnp.logical_not(inner))
        def _():
            gz_copy(g, 2, held.at[far_out], part.at[1], pair).start()
            gz_copy(g, 1, held.at[far_in], part.at[0], pair).start()

        gz_copy(g, 0, held.at[pair], final.at[0], pair).start()

    def g_relay(g):
        _, _, held, final, part = grads[g]

        @pl.when(inner)
        def _():
            for n, (to, slot) in enumerate(((far_out, 1), (far_in, 0))):
                gz_copy(g, 1 + slot, held.at[to], part.at[slot], pair).wait_recv()

                def add(m, _):
                    rows = pl.ds(pl.multiple_of(m * ROWS, ROWS), ROWS)
                    held[to, rows] = (
                        held[to, rows].astype(F32) + part[slot, rows].astype(F32)
                    ).astype(BF16)
                    return 0

                lax.fori_loop(0, rows_w // ROWS, add, 0)
                remote(
                    held.at[to], final.at[1], gz_s.at[g, 1 + slot], gz_r.at[g, 3], (f, c, to)
                ).start()

    def g_out(g, store):
        _, _, held, final, _ = grads[g]
        gz_copy(g, 0, held.at[t], final.at[0], pair).wait_recv()
        gz_copy(g, 3, held.at[t], final.at[1], far_in).wait_recv()

        def add(m, _):
            rows = pl.ds(pl.multiple_of(m * ROWS, ROWS), ROWS)
            store(
                rows,
                held[t, rows].astype(F32)
                + final[0, rows].astype(F32)
                + final[1, rows].astype(F32),
            )
            return 0

        lax.fori_loop(0, rows_w // ROWS, add, 0)

    def g_finish(g):
        _, _, held, final, part = grads[g]
        for i in order:
            for df in range(1, nf):
                gx_copy(g, df, i, lax.rem(f + df, nf)).wait_send()
        for i in range(1, nc):
            gy_copy(g, i, c, lax.rem(c + i, nc)).wait_send()
        for n in range(3):
            gz_copy(g, n, held.at[0], final.at[0], pair).wait_send()

    back(c)
    for k in range(CHUNKS):
        ag_wait(dl2, 2, k, 0)
    back(c_sib)
    rs_sib(2, 1, up_back(c_sib))
    rs_own(2, up_back(c))
    for k in range(CHUNKS):
        ag_pass(dl2, 2, k)
    back(c_y)
    for k in range(CHUNKS):
        ag_wait(dl2, 2, k, 2)
    back(c_ysib)
    rs_sib(2, 0, up_back(c_ysib))
    rs_y(2, up_back(c_y))
    weight_grad(0, dl2, act)
    weight_grad(1, nl, dpl)
    rs_copy(2, 1).wait_recv()

    def norm1_back(rows, i):
        dn = dres[rows] + rs_row(rows)
        xh = xh1[rows]
        add_sum(1, dn * xh)
        add_sum(2, dn)
        gy = dn * gain1
        dr = (gy - mean(gy) - xh * mean(gy * xh)) * rstd1[rows, 0:1]
        add_sum(0, dr)
        dres[rows] = dr
        dl1[own_slice(rows)] = dr.astype(BF16)

    for k in range(CHUNKS):
        rs_rows(2, k, norm1_back)
        ag_send(dl1, 3, k)

    dk_acc[...] = jnp.zeros_like(dk_acc)
    dv_acc[...] = jnp.zeros_like(dv_acc)

    def attend_back(b):
        rows = aligned(b, seq)
        datt[rows] = dot(dl1[rows], wo[...]).astype(BF16)
        qb = qs[rows]
        db = datt[rows]

        def head(h, _):
            qm = head_part(qb, h)
            dm = head_part(db, h)
            p = jnp.exp(masked_scores(qm) - lse[h, :, rows])
            dv_acc[...] += dot(p.astype(BF16), dm)
            pd = p * dot_last(vv[...], dm)
            delta = jnp.sum(pd, 0, keepdims=True)
            ds = (pd - p * delta).astype(BF16)
            dk_acc[...] += dot(ds, qm)
            hrows = aligned(h, DH)
            ot[hrows] = dot(kt[hrows], ds)
            return 0

        lax.fori_loop(0, heads, head, 0)
        dq = (ot[...].T * scale).astype(BF16)
        dqkv[rows, 0:hid] = dq
        dqf = dq.astype(F32)
        sums[7, :, 0:hid] = sums[7, :, 0:hid] + jnp.sum(dqf.reshape(seq // 8, 8, hid), 0)

    attend_back(c)
    g_cross(0, 1)
    g_cross(0, 2)
    g_cross(0, 3)
    for k in range(CHUNKS):
        ag_wait(dl1, 3, k, 0)
    attend_back(c_sib)
    for k in range(CHUNKS):
        ag_pass(dl1, 3, k)
    g_cross(0, 0)
    g_line(0)
    attend_back(c_y)
    g_cross(1, 1)
    g_cross(1, 2)
    for k in range(CHUNKS):
        ag_wait(dl1, 3, k, 2)
    weight_grad(2, dl1, att)
    attend_back(c_ysib)
    g_relay(0)
    g_cross(1, 3)
    g_cross(1, 0)

    def finish_kv(b, _):
        rows = aligned(b, seq)
        dqkv[rows, hid : 2 * hid] = dk_acc[rows].astype(BF16)
        dvb = dv_acc[rows].astype(BF16)
        dqkv[rows, 2 * hid : 3 * hid] = dvb
        sums[7, :, hid : 2 * hid] = sums[7, :, hid : 2 * hid] + jnp.sum(
            dvb.astype(F32).reshape(seq // 8, 8, hid), 0
        )
        return 0

    lax.fori_loop(0, nc, finish_kv, 0)

    def in_back(b):
        qb = dqkv[aligned(b, seq)]
        return lambda n: dot_last(qb, wqkv[aligned(n, TILE)])

    rs_sib(3, 0, in_back(c_ysib))
    rs_y(3, in_back(c_y))
    g_line(1)
    rs_sib(3, 1, in_back(c_sib))
    rs_own(3, in_back(c))
    weight_grad(3, x_tok, dqkv)
    sm[...] = jnp.sum(sums[...], 1)

    def sm_copy(stage, j, src, dst, dev):
        return remote(src, dst, sm_s.at[stage, j], sm_r.at[stage, j], dev)

    for j in range(1, nt):
        sm_copy(0, j, sm, smz.at[j], (f, c, lax.rem(t + j, nt))).start()
    for i in order:
        g_cross(2, i)
    rs_copy(3, 1).wait_recv()

    def grad_in(rows, i):
        gi_s[rows] = (dres[rows] + rs_row(rows)).astype(BF16)

    def line_copy(k, src, ts, n, to):
        rows = pl.ds(k * chunk, chunk)
        return remote(
            src.at[rows], gi_h.at[ts, rows], line_s.at[k, n], line_r.at[k, n], (f, c, to)
        )

    for k in range(CHUNKS):
        rs_rows(3, k, grad_in)
        rows = pl.ds(k * chunk, chunk)
        pltpu.make_async_copy(gi_s.at[rows], gi_h.at[t, rows], line_r.at[k, 0]).start()
        hops(lambda ts, n, to: line_copy(k, gi_s, ts, n, to).start(), 0)
    g_relay(1)
    g_line(2)

    def line_hop(k, h):
        arrivals(lambda ts, n, source: line_copy(k, gi_h.at[ts], ts, n, source).wait_recv(), h)
        if h < nt - 1:
            hops(lambda ts, n, to: line_copy(k, gi_h.at[ts], ts, n, to).start(), h)

    for i in order[:2]:
        g_cross(3, i)
    for k in range(CHUNKS):
        line_hop(k, 1)
    for i in order[2:]:
        g_cross(3, i)
    g_line(3)
    g_relay(2)
    total = sm[...]
    for j in range(1, nt):
        sm_copy(0, j, sm, smz.at[j], (f, c, lax.rem(t + nt - j, nt))).wait_recv()
        total = total + smz[j]
    smz[0] = total
    for df in range(1, nf):
        sm_copy(1, df, smz.at[0], smx.at[df], (lax.rem(f + df, nf), c, t)).start()
    for k in range(CHUNKS):
        line_hop(k, 2)
    for df in range(1, nf):
        sm_copy(1, df, smz.at[0], smx.at[df], (lax.rem(f + nf - df, nf), c, t)).wait_recv()
        total = total + smx[df]
    smx[0] = total
    for dc in range(1, nc):
        sm_copy(2, dc, smx.at[0], smc.at[c], (f, lax.rem(c + dc, nc), t)).start()
    smc[c] = total
    g_relay(3)

    def store_in(*outs):
        def store(rows, value):
            for k, out in enumerate(outs):
                out[rows] = value[:, k * out.shape[1] : (k + 1) * out.shape[1]]

        return store

    g_out(0, store_in(gd_o))
    g_out(1, store_in(gu_o))
    g_out(2, store_in(go_o))
    for dc in range(1, nc):
        cs = lax.rem(c + nc - dc, nc)
        sm_copy(2, dc, smx.at[0], smc.at[cs], (f, cs, t)).wait_recv()
    whole = smc[0]
    for s in range(1, nc):
        whole = whole + smc[s]
    small_o[0:6] = whole[0:6]
    small_o[6:8] = smc[t, 6:8]
    g_out(3, store_in(gq_o, gk_o, gv_o))
    spread_wait(res_s, res_h, 0)
    for k in range(CHUNKS):
        line_hop(k, 3)
        rows = pl.ds(k * chunk, chunk)
        pltpu.make_async_copy(gi_s.at[rows], gi_h.at[t, rows], line_r.at[k, 0]).wait()
        for h in range(nt - 1):
            hops(lambda ts, n, to: line_copy(k, gi_h.at[ts], ts, n, to).wait_send(), h)

    for g in range(4):
        g_finish(g)
    for a, buf in enumerate((x_tok, nl, dl2, dl1)):
        ag_finish(buf, a)
    rs_copy(3, 0).wait_send()
    rs_copy(3, 1).wait_send()
    for k in range(CHUNKS):
        ry_copy(3, k).wait_send()
    for j in range(1, nt):
        sm_copy(0, j, sm, smz.at[j], (f, c, lax.rem(t + j, nt))).wait_send()
    for df in range(1, nf):
        sm_copy(1, df, smz.at[0], smx.at[df], (lax.rem(f + df, nf), c, t)).wait_send()
    for dc in range(1, nc):
        sm_copy(2, dc, smx.at[0], smc.at[c], (f, lax.rem(c + dc, nc), t)).wait_send()

    @pl.when(t == c)
    def _():
        for j in range(1, nt):
            remote(
                bias, bias, bias_s.at[j], bias_r.at[0], (f, c, lax.rem(t + j, nt))
            ).wait_send()


def hand_over(small_rows, *refs):
    whole, small = refs[:8], refs[8]
    outs, small_o = refs[9:17], refs[17:26]

    @pl.when(pl.program_id(0) == 0)
    def _():
        for out, (row, start, size) in zip(small_o, small_rows):
            out[...] = small[row : row + 1, start : start + size]

    for out, value in zip(outs, whole):
        out[...] = value[...].astype(out.dtype)


def shards(
    dims,
    inputs,
    lengths,
    w_query,
    w_key,
    w_value,
    b_query,
    b_value,
    w_out,
    b_out,
    gain_attn,
    shift_attn,
    w_up,
    b_up,
    w_down,
    b_down,
    gain_ffn,
    shift_ffn,
    cotangent,
):
    nf, nc, nt = dims
    seq_dev, seq, width = inputs.shape
    rows_w, hid = w_query.shape
    ff = w_up.shape[1]
    assert nc == 4 and nt == nc and seq_dev == nt and ff == width
    tok = seq * nc
    heads = hid // DH
    part = nc * rows_w
    rows = [
        v.reshape(1, -1)
        for v in (
            b_query,
            b_value,
            b_up,
            b_out,
            gain_attn,
            shift_attn,
            b_down,
            gain_ffn,
            shift_ffn,
        )
    ]
    hbm = pl.BlockSpec(memory_space=pl.ANY)
    vmem = pl.BlockSpec(memory_space=pltpu.VMEM)
    smem = pl.BlockSpec(memory_space=pltpu.SMEM)

    def vb(*shape):
        return pltpu.VMEM(shape, BF16)

    def vf(*shape):
        return pltpu.VMEM(shape, F32)

    def sem(*shape):
        return pltpu.SemaphoreType.DMA(shape)

    result, grad_in, g_q, g_k, g_v, g_o, g_u, g_d, small = pl.pallas_call(
        functools.partial(layer, dims),
        out_shape=(
            jax.ShapeDtypeStruct((nt, seq, width), BF16),
            jax.ShapeDtypeStruct((nt, seq, width), BF16),
            *[jax.ShapeDtypeStruct((rows_w, hid), F32)] * 4,
            *[jax.ShapeDtypeStruct((rows_w, ff), F32)] * 2,
            jax.ShapeDtypeStruct((8, width), F32),
        ),
        in_specs=[smem] + [hbm] * 11 + [vmem] * 6,
        out_specs=(hbm, hbm) + (vmem,) * 7,
        scratch_shapes=[
            vb(width, 3 * hid),
            vb(width, hid),
            vb(width, ff),
            vb(width, ff),
            vb(nt, rows_w, 3 * hid),
            vb(nt, rows_w, hid),
            vb(nt, rows_w, ff),
            vb(nt, rows_w, ff),
            vb(tok, width),
            vb(tok, width),
            vb(tok, width),
            vb(tok, width),
            vb(tok, hid),
            vb(tok, hid),
            vb(tok, hid),
            vb(hid, tok),
            vb(hid, tok),
            vb(tok, hid),
            vb(tok, hid),
            vf(hid, seq),
            vf(heads, 1, tok),
            vb(tok, ff),
            vb(tok, ff),
            vb(tok, ff),
            vb(tok, 3 * hid),
            vf(tok, hid),
            vf(tok, hid),
            vb(2, seq, width),
            vb(2, seq, width),
            vb(seq, width),
            vb(seq, width),
            vf(seq, width),
            vf(seq, width),
            vf(seq, width),
            vf(seq, 128),
            vf(seq, width),
            vb(seq, width),
            vb(seq, width),
            vb(seq, width),
            vf(1, 2 * hid + ff),
            vb(width, ff),
            vb(width, ff),
            vb(width, 3 * hid),
            vb(width, hid),
            vb(nf - 1, part, ff),
            vb(nf - 1, part, ff),
            vb(nf - 1, part, 3 * hid),
            vb(nf - 1, part, hid),
            vb(2, rows_w, ff),
            vb(2, rows_w, ff),
            vb(2, rows_w, 3 * hid),
            vb(2, rows_w, hid),
            vb(2, rows_w, ff),
            vb(2, rows_w, ff),
            vb(2, rows_w, 3 * hid),
            vb(2, rows_w, hid),
            vf(8, 8, width),
            vf(8, width),
            vf(nt, 8, width),
            vf(nf, 8, width),
            vf(nc, 8, width),
            sem(3),
            sem(nt),
            sem(1),
            sem(4, 2 * nt),
            sem(4, 2 * nt),
            sem(4, nt),
            sem(4, nc),
            sem(4, nf),
            sem(4, nf),
            sem(4, 3, CHUNKS),
            sem(4, 3, CHUNKS),
            sem(4, 2),
            sem(4, 2),
            sem(4, CHUNKS),
            sem(4, CHUNKS),
            sem(1, nt),
            sem(1, nt),
            sem(4, nf, nc),
            sem(4, nf, nc),
            sem(4, nc),
            sem(4, nc),
            sem(4, 3),
            sem(4, 4),
            sem(CHUNKS, 2 * nt),
            sem(CHUNKS, 2 * nt),
            sem(3, max(nf, nc)),
            sem(3, max(nf, nc)),
        ],
        compiler_params=pltpu.CompilerParams(
            collective_id=0, has_side_effects=True, vmem_limit_bytes=63 << 20
        ),
    )(lengths, inputs, cotangent, w_query, w_key, w_value, w_out, w_up, w_down, *rows)
    small_rows = ((7, 0, hid), (7, hid, hid), (0, 0, width), (1, 0, width), (2, 0, width))
    small_rows += ((6, 0, ff), (3, 0, width), (4, 0, width), (5, 0, width))
    whole = (result, g_q, g_k, g_v, g_o, g_u, g_d, grad_in)
    step = rows_w // nt if rows_w % (8 * nt) == 0 else rows_w

    def block(a):
        if a.ndim == 3:
            return pl.BlockSpec((1, seq, width), lambda i: (i, 0, 0))
        return pl.BlockSpec((step, a.shape[1]), lambda i: (i if step < rows_w else 0, 0))

    outs = pl.pallas_call(
        functools.partial(hand_over, small_rows),
        grid=(nt,),
        out_shape=tuple(jax.ShapeDtypeStruct(a.shape, a.dtype) for a in whole[:7])
        + (jax.ShapeDtypeStruct(grad_in.shape, F32),)
        + tuple(jax.ShapeDtypeStruct((1, n), F32) for _, _, n in small_rows),
        in_specs=[block(a) for a in whole] + [vmem],
        out_specs=tuple(block(a) for a in whole) + (vmem,) * 9,
    )(*whole, small)
    result, g_q, g_k, g_v, g_o, g_u, g_d, grad_in = outs[:8]
    s_bq, s_bv, s_bo, s_ga, s_sa, s_bu, s_bd, s_gf, s_sf = (a.reshape(-1) for a in outs[8:])
    return (
        result,
        grad_in,
        g_q,
        g_k,
        g_v,
        s_bq,
        s_bv,
        g_o,
        s_bo,
        s_ga,
        s_sa,
        g_u,
        s_bu,
        g_d,
        s_bd,
        s_gf,
        s_sf,
    )


def solution(mesh):
    weight = P(("fsdp", "ctx"), "tp")
    acts = P("fsdp", "ctx", None)
    dims = tuple(mesh.shape[a] for a in ("fsdp", "ctx", "tp"))
    return jax.shard_map(
        functools.partial(shards, dims),
        mesh=mesh,
        in_specs=(
            acts,
            P("fsdp"),
            weight,
            weight,
            weight,
            P("tp"),
            P("tp"),
            weight,
            P(),
            P(),
            P(),
            weight,
            P("tp"),
            weight,
            P(),
            P(),
            P(),
            acts,
        ),
        out_specs=(
            acts,
            acts,
            weight,
            weight,
            weight,
            P("tp"),
            P("tp"),
            weight,
            P(),
            P(),
            P(),
            weight,
            P("tp"),
            weight,
            P(),
            P(),
            P(),
        ),
        check_vma=False,
    )
```

```python
import functools
import math

import jax
import jax.numpy as jnp
from jax import lax
from jax.experimental import pallas as pl
from jax.experimental.pallas import tpu as pltpu
from jax.sharding import PartitionSpec as P

DH = 64
MESH = pl.DeviceIdType.MESH
F32 = jnp.float32
BF16 = jnp.bfloat16
TILE = 256
ROWS = 16
CHUNKS = 4


def dot(left, right):
    return jnp.dot(left, right, preferred_element_type=F32)


def dot_last(left, right):
    return lax.dot_general(left, right, (((1,), (1,)), ((), ())), preferred_element_type=F32)


def dot_first(left, right):
    return lax.dot_general(left, right, (((0,), (0,)), ((), ())), preferred_element_type=F32)


def aligned(index, size):
    return pl.ds(pl.multiple_of(index * size, size), size)


def layer(
    dims,
    lens,
    x_h,
    ct_h,
    wq_h,
    wk_h,
    wv_h,
    wo_h,
    wu_h,
    wd_h,
    bq_h,
    bv_h,
    bu_h,
    b_out_r,
    gain1_r,
    shift1_r,
    b_down_r,
    gain2_r,
    shift2_r,
    res_h,
    gi_h,
    gq_o,
    gk_o,
    gv_o,
    go_o,
    gu_o,
    gd_o,
    small_o,
    wqkv,
    wo,
    wu,
    wd,
    z0,
    z1,
    z2,
    z3,
    x_tok,
    nl,
    dl2,
    dl1,
    qs,
    kk,
    vv,
    kt,
    vt,
    att,
    datt,
    ot,
    lse,
    act,
    dg,
    dpl,
    dqkv,
    dk_acc,
    dv_acc,
    ps,
    pr,
    ysend,
    yrecv,
    acc_y,
    acc_o,
    xh1,
    rstd1,
    dres,
    res_s,
    gi_s,
    ct_s,
    bias,
    gwd,
    gwu,
    gqkv,
    gwo,
    xg_d,
    xg_u,
    xg_q,
    xg_o,
    zf_d,
    zf_u,
    zf_q,
    zf_o,
    zp_d,
    zp_u,
    zp_q,
    zp_o,
    sums,
    sm,
    smz,
    smx,
    smc,
    loc_sem,
    bias_s,
    bias_r,
    wz_s,
    wz_r,
    wy_s,
    wy_r,
    wx_s,
    wx_r,
    ag_s,
    ag_r,
    rs_s,
    rs_r,
    ry_s,
    ry_r,
    out_s,
    out_r,
    gx_s,
    gx_r,
    gy_s,
    gy_r,
    gz_s,
    gz_r,
    line_s,
    line_r,
    sm_s,
    sm_r,
):
    nf, nc, nt = dims
    f = lax.axis_index("fsdp")
    c = lax.axis_index("ctx")
    t = lax.axis_index("tp")
    yi, ki = c // 2, lax.rem(c, 2)
    c_sib = yi * 2 + (1 - ki)
    c_y = (1 - yi) * 2 + ki
    c_ysib = (1 - yi) * 2 + (1 - ki)
    seq, width = ct_s.shape
    tok = x_tok.shape[0]
    rows_w = z0.shape[1]
    hid = wo.shape[1]
    ff = wu.shape[1]
    heads = hid // DH
    scale = 1.0 / math.sqrt(DH)
    chunk = seq // CHUNKS
    sib = (f, c_sib, t)
    ypeer = (f, c_y, t)
    length = lens[t]

    def remote(src, dst, ssem, rsem, dev):
        return pltpu.make_async_remote_copy(
            src_ref=src, dst_ref=dst, send_sem=ssem, recv_sem=rsem, device_id=dev, device_id_type=MESH
        )

    bar = pltpu.get_barrier_semaphore()
    for dc in range(nc):
        for dt in range(nt):
            if dc or dt:
                pl.semaphore_signal(
                    bar,
                    inc=1,
                    device_id=(f, lax.rem(c + dc, nc), lax.rem(t + dt, nt)),
                    device_id_type=MESH,
                )
    for df in range(1, nf):
        pl.semaphore_signal(bar, inc=1, device_id=(lax.rem(f + df, nf), c, t), device_id_type=MESH)
    pl.semaphore_wait(bar, nc * nt - 1 + nf - 1)

    groups = (
        ((wq_h, wk_h, wv_h), z0, wqkv),
        ((wo_h,), z1, wo),
        ((wu_h,), z2, wu),
        ((wd_h,), z3, wd),
    )

    def own_rows(cc):
        return aligned(f * nc + cc, rows_w)

    def hops(send, h):
        @pl.when((t >= h) & (t < nt - 1))
        def _():
            send(t - h, h + 1, t + 1)

        @pl.when((t + h < nt) & (t > 0))
        def _():
            send(t + h, nt + h, t - 1)

    def arrivals(take, h):
        @pl.when(t >= h)
        def _():
            take(t - h, h, t - 1)

        @pl.when(t + h < nt)
        def _():
            take(t + h, nt - 1 + h, t + 1)

    def w_cross_at(g, h):
        pl.when(t >= h)(lambda: w_cross(g, h))
        pl.when(t + h < nt)(lambda: w_cross(g, nt - h))

    def w_line_copy(g, src, ts, n, to):
        return remote(
            src, groups[g][1].at[ts], wz_s.at[g, n], wz_r.at[g, n], (f, c, to)
        )

    def w_start(g):
        srcs, stage, _ = groups[g]
        for k, src in enumerate(srcs):
            dst = stage.at[t, :, pl.ds(k * src.shape[1], src.shape[1])]
            pltpu.make_async_copy(src, dst, wz_r.at[g, 0]).start()
            if g:
                hops(lambda ts, n, to: w_line_copy(g, src, ts, n, to).start(), 0)
            for j in range(1, 1 if g else nt):
                remote(src, dst, wz_s.at[g, j], wz_r.at[g, j], (f, c, lax.rem(t + j, nt))).start()

    def w_cross_block(g, ts):
        _, stage, final = groups[g]

        @pl.when(ts == c)
        def _():
            pltpu.make_async_copy(stage.at[ts], final.at[own_rows(c)], wy_r.at[g, c]).start()

        @pl.when(ts != c)
        def _():
            remote(
                stage.at[ts], final.at[own_rows(c)], wy_s.at[g, ts], wy_r.at[g, c], (f, ts, t)
            ).start()

    def w_cross(g, j):
        stage = groups[g][1]
        ts = lax.rem(t + nt - j, nt)
        if j == 0:
            pltpu.make_async_copy(stage.at[ts], stage.at[ts], wz_r.at[g, 0]).wait()
        else:
            remote(stage.at[ts], stage.at[ts], wz_s.at[g, j], wz_r.at[g, j], (f, c, ts)).wait_recv()
        w_cross_block(g, ts)

    def w_line(g, h):
        stage = groups[g][1]

        def take(ts, n, source):
            w_line_copy(g, stage.at[ts], ts, n, source).wait_recv()

        arrivals(take, h)
        if h < nt - 1:
            hops(lambda ts, n, to: w_line_copy(g, stage.at[ts], ts, n, to).start(), h)
        arrivals(lambda ts, n, source: w_cross_block(g, ts), h)

    def w_spread(g, i):
        _, _, final = groups[g]
        cc = lax.rem(c + i, nc)
        part = final.at[own_rows(cc)]
        if i == 0:
            pltpu.make_async_copy(part, part, wy_r.at[g, cc]).wait()
        else:
            remote(part, part, wy_s.at[g, 0], wy_r.at[g, cc], (f, cc, t)).wait_recv()
        for df in range(1, nf):
            remote(
                part, part, wx_s.at[g, df], wx_r.at[g, df], (lax.rem(f + df, nf), c, t)
            ).start()

    def w_spread_at(g, h):
        @pl.when((t - c == h) | (c - t == h))
        def _():
            for i in range(nc):
                w_spread(g, i)

    def w_wait(g):
        _, _, final = groups[g]
        for df in range(1, nf):
            fs = lax.rem(f + nf - df, nf)
            part = final.at[aligned(fs, nc * rows_w)]
            remote(part, part, wx_s.at[g, df], wx_r.at[g, df], (fs, c, t)).wait_recv()

    def w_finish(g):
        _, stage, final = groups[g]
        if g:
            for h in range(nt - 1):
                hops(lambda ts, n, to: w_line_copy(g, stage.at[ts], ts, n, to).wait_send(), h)
        for j in range(1, 1 if g else nt):
            remote(
                stage.at[0], stage.at[0], wz_s.at[g, j], wz_r.at[g, j], (f, c, lax.rem(t + j, nt))
            ).wait_send()
        for j in range(nt):
            ts = lax.rem(t + nt - j, nt)

            @pl.when(ts != c)
            def _():
                remote(
                    stage.at[ts], final.at[own_rows(c)], wy_s.at[g, ts], wy_r.at[g, c], (f, ts, t)
                ).wait_send()

        for df in range(1, nf):
            part = final.at[aligned(f, nc * rows_w)]
            remote(
                part, part, wx_s.at[g, df], wx_r.at[g, df], (lax.rem(f + df, nf), c, t)
            ).wait_send()

    def part_of(buf, cc, k):
        return buf.at[pl.ds(pl.multiple_of(cc * seq + k * chunk, chunk), chunk)]

    def ag_copy(buf, a, k, cc, way, dev):
        part = part_of(buf, cc, k)
        return remote(part, part, ag_s.at[a, way, k], ag_r.at[a, way, k], dev)

    def ag_send(buf, a, k):
        ag_copy(buf, a, k, c, 1, ypeer).start()
        ag_copy(buf, a, k, c, 0, sib).start()

    def ag_pass(buf, a, k):
        ag_copy(buf, a, k, c_y, 1, ypeer).wait_recv()
        ag_copy(buf, a, k, c_y, 2, sib).start()

    def ag_wait(buf, a, k, way):
        ag_copy(buf, a, k, c_sib if way == 0 else c_ysib, way, sib).wait_recv()

    def ag_finish(buf, a):
        for k in range(CHUNKS):
            ag_copy(buf, a, k, c, 0, sib).wait_send()
            ag_copy(buf, a, k, c, 1, ypeer).wait_send()
            ag_copy(buf, a, k, c_y, 2, sib).wait_send()

    tiles = width // TILE

    def rs_copy(o, slot):
        return remote(ps.at[slot], pr.at[slot], rs_s.at[o, slot], rs_r.at[o, slot], sib)

    def ry_copy(o, k):
        rows = pl.ds(k * chunk, chunk)
        return remote(ysend.at[rows], yrecv.at[rows], ry_s.at[o, k], ry_r.at[o, k], ypeer)

    def rs_sib(o, slot, produce):
        if o:
            rs_copy(o - 1, slot).wait_send()

        def tile(n, _):
            ps[slot, :, aligned(n, TILE)] = produce(n).astype(BF16)
            return 0

        lax.fori_loop(0, tiles, tile, 0)
        rs_copy(o, slot).start()

    def rs_y(o, produce):
        def tile(n, _):
            acc_y[:, aligned(n, TILE)] = produce(n)
            return 0

        lax.fori_loop(0, tiles, tile, 0)
        rs_copy(o, 0).wait_recv()
        for k in range(CHUNKS):
            if o:
                ry_copy(o - 1, k).wait_send()

            def add(i, _, k=k):
                rows = pl.ds(pl.multiple_of(k * chunk + i * ROWS, ROWS), ROWS)
                ysend[rows] = (acc_y[rows] + pr[0, rows].astype(F32)).astype(BF16)
                return 0

            lax.fori_loop(0, chunk // ROWS, add, 0)
            ry_copy(o, k).start()

    def rs_own(o, produce):
        def tile(n, _):
            acc_o[:, aligned(n, TILE)] = produce(n)
            return 0

        lax.fori_loop(0, tiles, tile, 0)

    def rs_row(rows):
        return acc_o[rows] + pr[1, rows].astype(F32) + yrecv[rows].astype(F32)

    def rs_rows(o, k, body):
        ry_copy(o, k).wait_recv()

        def step(i, _):
            body(pl.ds(pl.multiple_of(k * chunk + i * ROWS, ROWS), ROWS), i)
            return 0

        lax.fori_loop(0, chunk // ROWS, step, 0)

    def add_sum(k, value):
        half = value[0:8]
        for r in range(8, ROWS, 8):
            half = half + value[r : r + 8]
        sums[k] = sums[k] + half

    def mean(value):
        return jnp.sum(value, -1, keepdims=True) * (1.0 / width)

    w_start(0)
    pltpu.make_async_copy(x_h.at[t], x_tok.at[aligned(c, seq)], loc_sem.at[0]).start()
    pltpu.make_async_copy(ct_h.at[t], ct_s, loc_sem.at[1]).start()

    biases = (
        (bq_h, bias.at[:, pl.ds(0, hid)]),
        (bv_h, bias.at[:, pl.ds(hid, hid)]),
        (bu_h, bias.at[:, pl.ds(2 * hid, ff)]),
    )

    @pl.when(t == c)
    def _():
        for src, dst in biases:
            pltpu.make_async_copy(src, dst, loc_sem.at[2]).start()
            for j in range(1, nt):
                remote(src, dst, bias_s.at[j], bias_r.at[0], (f, c, lax.rem(t + j, nt))).start()

    pltpu.make_async_copy(x_h.at[t], x_tok.at[aligned(c, seq)], loc_sem.at[0]).wait()
    for k in range(CHUNKS):
        ag_send(x_tok, 0, k)
    w_start(1)
    w_start(2)
    w_cross(0, 0)
    w_cross(1, 0)
    sums[...] = jnp.zeros_like(sums)
    w_cross_at(0, 1)
    ag_pass(x_tok, 0, 0)
    w_spread_at(0, 0)
    w_cross_at(0, 2)
    for k in range(1, CHUNKS):
        ag_pass(x_tok, 0, k)
    w_spread_at(0, 1)
    w_cross_at(0, 3)
    w_spread_at(1, 0)
    w_cross(2, 0)
    w_line(1, 1)
    w_spread_at(0, 2)
    w_start(3)
    w_line(1, 2)
    w_spread_at(1, 1)
    w_line(2, 1)
    w_spread_at(0, 3)
    w_spread_at(2, 0)
    w_cross(3, 0)
    w_line(1, 3)
    w_spread_at(1, 2)

    @pl.when(t == c)
    def _():
        pltpu.make_async_copy(bias, bias, loc_sem.at[2]).wait()

    @pl.when(t != c)
    def _():
        remote(bias, bias, bias_s.at[0], bias_r.at[0], (f, c, c)).wait_recv()

    for k in range(CHUNKS):
        ag_wait(x_tok, 0, k, 0)
        ag_wait(x_tok, 0, k, 2)
    w_wait(0)
    w_line(3, 1)
    w_spread_at(1, 3)

    def project(b, _):
        rows = aligned(b, seq)
        xb = x_tok[rows]
        qv = dot(xb, wqkv[:, 0:hid]) + bias[0:1, 0:hid]
        qs[rows] = (qv * scale).astype(BF16)
        kb = dot(xb, wqkv[:, hid : 2 * hid])
        kk[rows] = kb.astype(BF16)
        kt[:, rows] = kb.T.astype(BF16)
        vb = dot(xb, wqkv[:, 2 * hid : 3 * hid]) + bias[0:1, hid : 2 * hid]
        vv[rows] = vb.astype(BF16)
        vt[:, rows] = vb.T.astype(BF16)
        return 0

    lax.fori_loop(0, nc, project, 0)

    lane = lax.broadcasted_iota(jnp.int32, (seq, hid), 1)

    def head_part(value, h):
        inside = (lane >= h * DH) & (lane < (h + 1) * DH)
        return jnp.where(inside, value, jnp.zeros_like(value))

    def masked_scores(qm):
        s = dot_last(kk[...], qm)
        key = lax.broadcasted_iota(jnp.int32, s.shape, 0)
        return jnp.where(key < length, s, -1e30)

    def attend(b):
        rows = aligned(b, seq)
        qb = qs[rows]

        def head(h, _):
            s = masked_scores(head_part(qb, h))
            top = jnp.max(s, 0, keepdims=True)
            e = jnp.exp(s - top)
            total = jnp.sum(e, 0, keepdims=True)
            hrows = aligned(h, DH)
            ot[hrows] = dot(vt[hrows], e.astype(BF16)) / total
            lse[h, :, rows] = top + jnp.log(total)
            return 0

        lax.fori_loop(0, heads, head, 0)
        att[rows] = ot[...].T.astype(BF16)

    def out_proj(b):
        ab = att[aligned(b, seq)]
        return lambda n: dot_last(ab, wo[aligned(n, TILE)])

    w_line(2, 2)
    w_spread_at(2, 1)
    w_spread_at(3, 0)
    attend(c_ysib)
    w_line(3, 2)
    w_spread_at(2, 2)
    w_spread_at(3, 1)
    attend(c_y)
    w_line(2, 3)
    w_wait(1)
    rs_sib(0, 0, out_proj(c_ysib))
    rs_y(0, out_proj(c_y))
    w_spread_at(2, 3)
    w_spread_at(3, 2)
    w_line(3, 3)
    attend(c_sib)
    rs_sib(0, 1, out_proj(c_sib))
    w_spread_at(3, 3)
    attend(c)
    rs_own(0, out_proj(c))
    rs_copy(0, 1).wait_recv()

    b_out, gain1, shift1 = b_out_r[...], gain1_r[...], shift1_r[...]
    b_down, gain2, shift2 = b_down_r[...], gain2_r[...], shift2_r[...]
    own = c * seq

    def own_slice(rows):
        return pl.ds(pl.multiple_of(own + rows.start, ROWS), ROWS)

    def norm1(rows, i):
        h = x_tok[own_slice(rows)].astype(F32) + rs_row(rows) + b_out
        cen = h - mean(h)
        inv = lax.rsqrt(mean(cen * cen) + 1e-5)
        xh = cen * inv
        xh1[rows] = xh
        rstd1[rows] = jnp.broadcast_to(inv, (ROWS, 128))
        nl[own_slice(rows)] = (xh * gain1 + shift1).astype(BF16)

    for k in range(CHUNKS):
        rs_rows(0, k, norm1)
        ag_send(nl, 1, k)
    w_wait(2)

    def up(b):
        rows = aligned(b, seq)
        nb = nl[rows]

        def tile(n, _):
            cols = aligned(n, TILE)
            v = dot(nb, wu[:, cols]) + bias[0:1, pl.ds(pl.multiple_of(2 * hid + n * TILE, 128), TILE)]
            cdf = 0.5 * (1.0 + lax.erf(v * math.sqrt(0.5)))
            act[rows, cols] = (v * cdf).astype(BF16)
            pdf = jnp.exp(-0.5 * v * v) * (1.0 / math.sqrt(2.0 * math.pi))
            dg[rows, cols] = (cdf + v * pdf).astype(BF16)
            return 0

        lax.fori_loop(0, ff // TILE, tile, 0)

    def down(b):
        ab = act[aligned(b, seq)]
        return lambda n: dot_last(ab, wd[aligned(n, TILE)])

    up(c)
    for k in range(CHUNKS):
        ag_wait(nl, 1, k, 0)
    up(c_sib)
    for k in range(CHUNKS):
        ag_pass(nl, 1, k)
    up(c_y)
    for k in range(CHUNKS):
        ag_wait(nl, 1, k, 2)
    up(c_ysib)
    w_wait(3)
    rs_sib(1, 0, down(c_ysib))
    rs_y(1, down(c_y))
    rs_sib(1, 1, down(c_sib))
    rs_own(1, down(c))
    rs_copy(1, 1).wait_recv()
    for g in range(4):
        w_finish(g)
    pltpu.make_async_copy(ct_h.at[t], ct_s, loc_sem.at[1]).wait()

    def norm2(rows, i):
        h = xh1[rows] * gain1 + shift1 + rs_row(rows) + b_down
        cen = h - mean(h)
        inv = lax.rsqrt(mean(cen * cen) + 1e-5)
        xh = cen * inv
        res_s[rows] = (xh * gain2 + shift2).astype(BF16)
        pos = own + rows.start + lax.broadcasted_iota(jnp.int32, (ROWS, width), 0)
        top = jnp.where(pos < length, ct_s[rows].astype(F32), 0.0)
        add_sum(4, top * xh)
        add_sum(5, top)
        gy = top * gain2
        dr = (gy - mean(gy) - xh * mean(gy * xh)) * inv
        add_sum(3, dr)
        dres[rows] = dr
        dl2[own_slice(rows)] = dr.astype(BF16)

    for k in range(CHUNKS):
        rs_rows(1, k, norm2)
        ag_send(dl2, 2, k)

    def spread(share, out, o):
        pltpu.make_async_copy(share, out.at[t], out_r.at[o, 0]).start()
        for j in range(1, nt):
            remote(
                share, out.at[t], out_s.at[o, j], out_r.at[o, j], (f, c, lax.rem(t + j, nt))
            ).start()

    def spread_wait(share, out, o):
        pltpu.make_async_copy(share, out.at[t], out_r.at[o, 0]).wait()
        for j in range(1, nt):
            ts = lax.rem(t + nt - j, nt)
            remote(share, out.at[ts], out_s.at[o, j], out_r.at[o, j], (f, c, ts)).wait_recv()
            remote(
                share, out.at[t], out_s.at[o, j], out_r.at[o, j], (f, c, lax.rem(t + j, nt))
            ).wait_send()

    spread(res_s, res_h, 0)

    def back(b):
        rows = aligned(b, seq)
        db = dl2[rows]

        def tile(n, _):
            cols = aligned(n, TILE)
            dp = (dot(db, wd[:, cols]) * dg[rows, cols].astype(F32)).astype(BF16)
            dpl[rows, cols] = dp
            dpf = dp.astype(F32)
            sums[6, :, cols] = sums[6, :, cols] + jnp.sum(dpf.reshape(seq // 8, 8, TILE), 0)
            return 0

        lax.fori_loop(0, ff // TILE, tile, 0)

    def up_back(b):
        pb = dpl[aligned(b, seq)]
        return lambda n: dot_last(pb, wu[aligned(n, TILE)])

    grads = (
        (gwd, xg_d, z3, zf_d, zp_d),
        (gwu, xg_u, z2, zf_u, zp_u),
        (gwo, xg_o, z1, zf_o, zp_o),
        (gqkv, xg_q, z0, zf_q, zp_q),
    )
    pair = t + 1 - 2 * lax.rem(t, 2)
    inner = (t == 1) | (t == nt - 2)
    far_in = jnp.where(t < 2, 2, 1)
    far_out = jnp.where(t < 2, nt - 1, 0)

    def gx_copy(g, df, i, dev_f):
        buf, got = grads[g][:2]
        cc = lax.rem(c + i, nc)
        return remote(
            buf.at[aligned(dev_f * nc + cc, rows_w)],
            got.at[df - 1, aligned(cc, rows_w)],
            gx_s.at[g, df, i],
            gx_r.at[g, df, i],
            (dev_f, c, t),
        )

    order = tuple(range(1, nc)) + (0,)

    part_rows = nc * rows_w
    def weight_grad(g, left, right):
        dst = grads[g][0]

        def rows_from(first, count):
            def step(m, _):
                rows = pl.ds(pl.multiple_of(first + m * TILE, TILE), TILE)
                dst[rows] = dot_first(left[:, rows], right[...]).astype(BF16)
                return 0

            lax.fori_loop(0, count // TILE, step, 0)

        split = part_rows % TILE == 0
        if not split:
            rows_from(0, width)
        for df in tuple(range(1, nf)) + (0,):
            to = lax.rem(f + df, nf)
            if split:
                rows_from(to * part_rows, part_rows)
            if df:
                for i in order:
                    gx_copy(g, df, i, to).start()

    def gy_copy(g, i, slot, cc):
        buf, _, got = grads[g][:3]
        return remote(
            buf.at[own_rows(cc)], got.at[slot], gy_s.at[g, i], gy_r.at[g, i], (f, cc, t)
        )

    def g_cross(g, i):
        buf, got, held = grads[g][:3]
        cc = lax.rem(c + i, nc)
        for df in range(1, nf):
            gx_copy(g, df, i, lax.rem(f + nf - df, nf)).wait_recv()

        def add(n, _):
            rows = pl.ds(pl.multiple_of((f * nc + cc) * rows_w + n * ROWS, ROWS), ROWS)
            total = buf[rows].astype(F32)
            for df in range(1, nf):
                theirs = pl.ds(pl.multiple_of(cc * rows_w + n * ROWS, ROWS), ROWS)
                total = total + got[df - 1, theirs].astype(F32)
            if i:
                buf[rows] = total.astype(BF16)
            else:
                held[c, pl.ds(pl.multiple_of(n * ROWS, ROWS), ROWS)] = total.astype(BF16)
            return 0

        lax.fori_loop(0, rows_w // ROWS, add, 0)
        if i:
            gy_copy(g, i, c, cc).start()

    def gz_copy(g, n, src, dst, to):
        return remote(src, dst, gz_s.at[g, n], gz_r.at[g, n], (f, c, to))

    def g_line(g):
        _, _, held, final, part = grads[g]
        for i in range(1, nc):
            cs = lax.rem(c + nc - i, nc)
            gy_copy(g, i, cs, cs).wait_recv()

        @pl.when(jnp.logical_not(inner))
        def _():
            gz_copy(g, 2, held.at[far_out], part.at[1], pair).start()
            gz_copy(g, 1, held.at[far_in], part.at[0], pair).start()

        gz_copy(g, 0, held.at[pair], final.at[0], pair).start()

    def g_relay(g):
        _, _, held, final, part = grads[g]

        @pl.when(inner)
        def _():
            for n, (to, slot) in enumerate(((far_out, 1), (far_in, 0))):
                gz_copy(g, 1 + slot, held.at[to], part.at[slot], pair).wait_recv()

                def add(m, _):
                    rows = pl.ds(pl.multiple_of(m * ROWS, ROWS), ROWS)
                    held[to, rows] = (
                        held[to, rows].astype(F32) + part[slot, rows].astype(F32)
                    ).astype(BF16)
                    return 0

                lax.fori_loop(0, rows_w // ROWS, add, 0)
                remote(
                    held.at[to], final.at[1], gz_s.at[g, 1 + slot], gz_r.at[g, 3], (f, c, to)
                ).start()

    def g_out(g, store):
        _, _, held, final, _ = grads[g]
        gz_copy(g, 0, held.at[t], final.at[0], pair).wait_recv()
        gz_copy(g, 3, held.at[t], final.at[1], far_in).wait_recv()

        def add(m, _):
            rows = pl.ds(pl.multiple_of(m * ROWS, ROWS), ROWS)
            store(
                rows,
                held[t, rows].astype(F32)
                + final[0, rows].astype(F32)
                + final[1, rows].astype(F32),
            )
            return 0

        lax.fori_loop(0, rows_w // ROWS, add, 0)

    def g_finish(g):
        _, _, held, final, part = grads[g]
        for i in order:
            for df in range(1, nf):
                gx_copy(g, df, i, lax.rem(f + df, nf)).wait_send()
        for i in range(1, nc):
            gy_copy(g, i, c, lax.rem(c + i, nc)).wait_send()
        for n in range(3):
            gz_copy(g, n, held.at[0], final.at[0], pair).wait_send()

    back(c)
    for k in range(CHUNKS):
        ag_wait(dl2, 2, k, 0)
    back(c_sib)
    rs_sib(2, 1, up_back(c_sib))
    rs_own(2, up_back(c))
    for k in range(CHUNKS):
        ag_pass(dl2, 2, k)
    back(c_y)
    for k in range(CHUNKS):
        ag_wait(dl2, 2, k, 2)
    back(c_ysib)
    rs_sib(2, 0, up_back(c_ysib))
    rs_y(2, up_back(c_y))
    weight_grad(0, dl2, act)
    weight_grad(1, nl, dpl)
    rs_copy(2, 1).wait_recv()

    def norm1_back(rows, i):
        dn = dres[rows] + rs_row(rows)
        xh = xh1[rows]
        add_sum(1, dn * xh)
        add_sum(2, dn)
        gy = dn * gain1
        dr = (gy - mean(gy) - xh * mean(gy * xh)) * rstd1[rows, 0:1]
        add_sum(0, dr)
        dres[rows] = dr
        dl1[own_slice(rows)] = dr.astype(BF16)

    for k in range(CHUNKS):
        rs_rows(2, k, norm1_back)
        ag_send(dl1, 3, k)

    dk_acc[...] = jnp.zeros_like(dk_acc)
    dv_acc[...] = jnp.zeros_like(dv_acc)

    def attend_back(b):
        rows = aligned(b, seq)
        datt[rows] = dot(dl1[rows], wo[...]).astype(BF16)
        qb = qs[rows]
        db = datt[rows]

        def head(h, _):
            qm = head_part(qb, h)
            dm = head_part(db, h)
            p = jnp.exp(masked_scores(qm) - lse[h, :, rows])
            dv_acc[...] += dot(p.astype(BF16), dm)
            pd = p * dot_last(vv[...], dm)
            delta = jnp.sum(pd, 0, keepdims=True)
            ds = (pd - p * delta).astype(BF16)
            dk_acc[...] += dot(ds, qm)
            hrows = aligned(h, DH)
            ot[hrows] = dot(kt[hrows], ds)
            return 0

        lax.fori_loop(0, heads, head, 0)
        dq = (ot[...].T * scale).astype(BF16)
        dqkv[rows, 0:hid] = dq
        dqf = dq.astype(F32)
        sums[7, :, 0:hid] = sums[7, :, 0:hid] + jnp.sum(dqf.reshape(seq // 8, 8, hid), 0)

    attend_back(c)
    g_cross(0, 1)
    g_cross(0, 2)
    g_cross(0, 3)
    for k in range(CHUNKS):
        ag_wait(dl1, 3, k, 0)
    attend_back(c_sib)
    for k in range(CHUNKS):
        ag_pass(dl1, 3, k)
    g_cross(0, 0)
    g_line(0)
    attend_back(c_y)
    g_cross(1, 1)
    g_cross(1, 2)
    for k in range(CHUNKS):
        ag_wait(dl1, 3, k, 2)
    weight_grad(2, dl1, att)
    attend_back(c_ysib)
    g_relay(0)
    g_cross(1, 3)
    g_cross(1, 0)

    def finish_kv(b, _):
        rows = aligned(b, seq)
        dqkv[rows, hid : 2 * hid] = dk_acc[rows].astype(BF16)
        dvb = dv_acc[rows].astype(BF16)
        dqkv[rows, 2 * hid : 3 * hid] = dvb
        sums[7, :, hid : 2 * hid] = sums[7, :, hid : 2 * hid] + jnp.sum(
            dvb.astype(F32).reshape(seq // 8, 8, hid), 0
        )
        return 0

    lax.fori_loop(0, nc, finish_kv, 0)

    def in_back(b):
        qb = dqkv[aligned(b, seq)]
        return lambda n: dot_last(qb, wqkv[aligned(n, TILE)])

    rs_sib(3, 0, in_back(c_ysib))
    rs_y(3, in_back(c_y))
    g_line(1)
    rs_sib(3, 1, in_back(c_sib))
    rs_own(3, in_back(c))
    weight_grad(3, x_tok, dqkv)
    sm[...] = jnp.sum(sums[...], 1)

    def sm_copy(stage, j, src, dst, dev):
        return remote(src, dst, sm_s.at[stage, j], sm_r.at[stage, j], dev)

    for j in range(1, nt):
        sm_copy(0, j, sm, smz.at[j], (f, c, lax.rem(t + j, nt))).start()
    for i in order:
        g_cross(2, i)
    rs_copy(3, 1).wait_recv()

    def grad_in(rows, i):
        gi_s[rows] = (dres[rows] + rs_row(rows)).astype(BF16)

    def line_copy(k, src, ts, n, to):
        rows = pl.ds(k * chunk, chunk)
        return remote(
            src.at[rows], gi_h.at[ts, rows], line_s.at[k, n], line_r.at[k, n], (f, c, to)
        )

    for k in range(CHUNKS):
        rs_rows(3, k, grad_in)
        rows = pl.ds(k * chunk, chunk)
        pltpu.make_async_copy(gi_s.at[rows], gi_h.at[t, rows], line_r.at[k, 0]).start()
        hops(lambda ts, n, to: line_copy(k, gi_s, ts, n, to).start(), 0)
    g_relay(1)
    g_line(2)

    def line_hop(k, h):
        arrivals(lambda ts, n, source: line_copy(k, gi_h.at[ts], ts, n, source).wait_recv(), h)
        if h < nt - 1:
            hops(lambda ts, n, to: line_copy(k, gi_h.at[ts], ts, n, to).start(), h)

    for i in order[:2]:
        g_cross(3, i)
    for k in range(CHUNKS):
        line_hop(k, 1)
    for i in order[2:]:
        g_cross(3, i)
    g_line(3)
    g_relay(2)
    total = sm[...]
    for j in range(1, nt):
        sm_copy(0, j, sm, smz.at[j], (f, c, lax.rem(t + nt - j, nt))).wait_recv()
        total = total + smz[j]
    smz[0] = total
    for df in range(1, nf):
        sm_copy(1, df, smz.at[0], smx.at[df], (lax.rem(f + df, nf), c, t)).start()
    for k in range(CHUNKS):
        line_hop(k, 2)
    for df in range(1, nf):
        sm_copy(1, df, smz.at[0], smx.at[df], (lax.rem(f + nf - df, nf), c, t)).wait_recv()
        total = total + smx[df]
    smx[0] = total
    for dc in range(1, nc):
        sm_copy(2, dc, smx.at[0], smc.at[c], (f, lax.rem(c + dc, nc), t)).start()
    smc[c] = total
    g_relay(3)

    def store_in(*outs):
        def store(rows, value):
            for k, out in enumerate(outs):
                out[rows] = value[:, k * out.shape[1] : (k + 1) * out.shape[1]]

        return store

    g_out(0, store_in(gd_o))
    g_out(1, store_in(gu_o))
    g_out(2, store_in(go_o))
    for dc in range(1, nc):
        cs = lax.rem(c + nc - dc, nc)
        sm_copy(2, dc, smx.at[0], smc.at[cs], (f, cs, t)).wait_recv()
    whole = smc[0]
    for s in range(1, nc):
        whole = whole + smc[s]
    small_o[0:6] = whole[0:6]
    small_o[6:8] = smc[t, 6:8]
    g_out(3, store_in(gq_o, gk_o, gv_o))
    spread_wait(res_s, res_h, 0)
    for k in range(CHUNKS):
        line_hop(k, 3)
        rows = pl.ds(k * chunk, chunk)
        pltpu.make_async_copy(gi_s.at[rows], gi_h.at[t, rows], line_r.at[k, 0]).wait()
        for h in range(nt - 1):
            hops(lambda ts, n, to: line_copy(k, gi_h.at[ts], ts, n, to).wait_send(), h)

    for g in range(4):
        g_finish(g)
    for a, buf in enumerate((x_tok, nl, dl2, dl1)):
        ag_finish(buf, a)
    rs_copy(3, 0).wait_send()
    rs_copy(3, 1).wait_send()
    for k in range(CHUNKS):
        ry_copy(3, k).wait_send()
    for j in range(1, nt):
        sm_copy(0, j, sm, smz.at[j], (f, c, lax.rem(t + j, nt))).wait_send()
    for df in range(1, nf):
        sm_copy(1, df, smz.at[0], smx.at[df], (lax.rem(f + df, nf), c, t)).wait_send()
    for dc in range(1, nc):
        sm_copy(2, dc, smx.at[0], smc.at[c], (f, lax.rem(c + dc, nc), t)).wait_send()

    @pl.when(t == c)
    def _():
        for j in range(1, nt):
            remote(
                bias, bias, bias_s.at[j], bias_r.at[0], (f, c, lax.rem(t + j, nt))
            ).wait_send()


def hand_over(small_rows, *refs):
    whole, small = refs[:8], refs[8]
    outs, small_o = refs[9:17], refs[17:26]

    @pl.when(pl.program_id(0) == 0)
    def _():
        for out, (row, start, size) in zip(small_o, small_rows):
            out[...] = small[row : row + 1, start : start + size]

    for out, value in zip(outs, whole):
        out[...] = value[...].astype(out.dtype)


def shards(
    dims,
    inputs,
    lengths,
    w_query,
    w_key,
    w_value,
    b_query,
    b_value,
    w_out,
    b_out,
    gain_attn,
    shift_attn,
    w_up,
    b_up,
    w_down,
    b_down,
    gain_ffn,
    shift_ffn,
    cotangent,
):
    nf, nc, nt = dims
    seq_dev, seq, width = inputs.shape
    rows_w, hid = w_query.shape
    ff = w_up.shape[1]
    assert nc == 4 and nt == nc and seq_dev == nt and ff == width
    tok = seq * nc
    heads = hid // DH
    part = nc * rows_w
    rows = [
        v.reshape(1, -1)
        for v in (
            b_query,
            b_value,
            b_up,
            b_out,
            gain_attn,
            shift_attn,
            b_down,
            gain_ffn,
            shift_ffn,
        )
    ]
    hbm = pl.BlockSpec(memory_space=pl.ANY)
    vmem = pl.BlockSpec(memory_space=pltpu.VMEM)
    smem = pl.BlockSpec(memory_space=pltpu.SMEM)

    def vb(*shape):
        return pltpu.VMEM(shape, BF16)

    def vf(*shape):
        return pltpu.VMEM(shape, F32)

    def sem(*shape):
        return pltpu.SemaphoreType.DMA(shape)

    result, grad_in, g_q, g_k, g_v, g_o, g_u, g_d, small = pl.pallas_call(
        functools.partial(layer, dims),
        out_shape=(
            jax.ShapeDtypeStruct((nt, seq, width), BF16),
            jax.ShapeDtypeStruct((nt, seq, width), BF16),
            *[jax.ShapeDtypeStruct((rows_w, hid), F32)] * 4,
            *[jax.ShapeDtypeStruct((rows_w, ff), F32)] * 2,
            jax.ShapeDtypeStruct((8, width), F32),
        ),
        in_specs=[smem] + [hbm] * 11 + [vmem] * 6,
        out_specs=(hbm, hbm) + (vmem,) * 7,
        scratch_shapes=[
            vb(width, 3 * hid),
            vb(width, hid),
            vb(width, ff),
            vb(width, ff),
            vb(nt, rows_w, 3 * hid),
            vb(nt, rows_w, hid),
            vb(nt, rows_w, ff),
            vb(nt, rows_w, ff),
            vb(tok, width),
            vb(tok, width),
            vb(tok, width),
            vb(tok, width),
            vb(tok, hid),
            vb(tok, hid),
            vb(tok, hid),
            vb(hid, tok),
            vb(hid, tok),
            vb(tok, hid),
            vb(tok, hid),
            vf(hid, seq),
            vf(heads, 1, tok),
            vb(tok, ff),
            vb(tok, ff),
            vb(tok, ff),
            vb(tok, 3 * hid),
            vf(tok, hid),
            vf(tok, hid),
            vb(2, seq, width),
            vb(2, seq, width),
            vb(seq, width),
            vb(seq, width),
            vf(seq, width),
            vf(seq, width),
            vf(seq, width),
            vf(seq, 128),
            vf(seq, width),
            vb(seq, width),
            vb(seq, width),
            vb(seq, width),
            vf(1, 2 * hid + ff),
            vb(width, ff),
            vb(width, ff),
            vb(width, 3 * hid),
            vb(width, hid),
            vb(nf - 1, part, ff),
            vb(nf - 1, part, ff),
            vb(nf - 1, part, 3 * hid),
            vb(nf - 1, part, hid),
            vb(2, rows_w, ff),
            vb(2, rows_w, ff),
            vb(2, rows_w, 3 * hid),
            vb(2, rows_w, hid),
            vb(2, rows_w, ff),
            vb(2, rows_w, ff),
            vb(2, rows_w, 3 * hid),
            vb(2, rows_w, hid),
            vf(8, 8, width),
            vf(8, width),
            vf(nt, 8, width),
            vf(nf, 8, width),
            vf(nc, 8, width),
            sem(3),
            sem(nt),
            sem(1),
            sem(4, 2 * nt),
            sem(4, 2 * nt),
            sem(4, nt),
            sem(4, nc),
            sem(4, nf),
            sem(4, nf),
            sem(4, 3, CHUNKS),
            sem(4, 3, CHUNKS),
            sem(4, 2),
            sem(4, 2),
            sem(4, CHUNKS),
            sem(4, CHUNKS),
            sem(1, nt),
            sem(1, nt),
            sem(4, nf, nc),
            sem(4, nf, nc),
            sem(4, nc),
            sem(4, nc),
            sem(4, 3),
            sem(4, 4),
            sem(CHUNKS, 2 * nt),
            sem(CHUNKS, 2 * nt),
            sem(3, max(nf, nc)),
            sem(3, max(nf, nc)),
        ],
        compiler_params=pltpu.CompilerParams(
            collective_id=0, has_side_effects=True, vmem_limit_bytes=63 << 20
        ),
    )(lengths, inputs, cotangent, w_query, w_key, w_value, w_out, w_up, w_down, *rows)
    small_rows = ((7, 0, hid), (7, hid, hid), (0, 0, width), (1, 0, width), (2, 0, width))
    small_rows += ((6, 0, ff), (3, 0, width), (4, 0, width), (5, 0, width))
    whole = (result, g_q, g_k, g_v, g_o, g_u, g_d, grad_in)
    step = rows_w // nt if rows_w % (8 * nt) == 0 else rows_w

    def block(a):
        if a.ndim == 3:
            return pl.BlockSpec((1, seq, width), lambda i: (i, 0, 0))
        return pl.BlockSpec((step, a.shape[1]), lambda i: (i if step < rows_w else 0, 0))

    outs = pl.pallas_call(
        functools.partial(hand_over, small_rows),
        grid=(nt,),
        out_shape=tuple(jax.ShapeDtypeStruct(a.shape, a.dtype) for a in whole[:7])
        + (jax.ShapeDtypeStruct(grad_in.shape, F32),)
        + tuple(jax.ShapeDtypeStruct((1, n), F32) for _, _, n in small_rows),
        in_specs=[block(a) for a in whole] + [vmem],
        out_specs=tuple(block(a) for a in whole) + (vmem,) * 9,
    )(*whole, small)
    result, g_q, g_k, g_v, g_o, g_u, g_d, grad_in = outs[:8]
    s_bq, s_bv, s_bo, s_ga, s_sa, s_bu, s_bd, s_gf, s_sf = (a.reshape(-1) for a in outs[8:])
    return (
        result,
        grad_in,
        g_q,
        g_k,
        g_v,
        s_bq,
        s_bv,
        g_o,
        s_bo,
        s_ga,
        s_sa,
        g_u,
        s_bu,
        g_d,
        s_bd,
        s_gf,
        s_sf,
    )


def solution(mesh):
    weight = P(("fsdp", "ctx"), "tp")
    acts = P("fsdp", "ctx", None)
    dims = tuple(mesh.shape[a] for a in ("fsdp", "ctx", "tp"))
    return jax.shard_map(
        functools.partial(shards, dims),
        mesh=mesh,
        in_specs=(
            acts,
            P("fsdp"),
            weight,
            weight,
            weight,
            P("tp"),
            P("tp"),
            weight,
            P(),
            P(),
            P(),
            weight,
            P("tp"),
            weight,
            P(),
            P(),
            P(),
            acts,
        ),
        out_specs=(
            acts,
            acts,
            weight,
            weight,
            weight,
            P("tp"),
            P("tp"),
            weight,
            P(),
            P(),
            P(),
            weight,
            P("tp"),
            weight,
            P(),
            P(),
            P(),
        ),
        check_vma=False,
    )
```
